32 devices in a mesh: dp: 8 (over z, x), mp: 4 (over y, core).
Axes of the slice: x: 2, y: 2, z: 4, core: 2. Of those that a mesh axis runs over, the one named last changes fastest.
Arguments:
- vision: bfloat16 [2048, 3200], P(('dp', 'mp')), may hold values from -6 to 6
- vision_gain: float32 [3200], replicated, may hold values from 0.1 to 1.9
- image_slot: int32 [8], replicated, may hold values from 0 to 15, as said below
- text_embed: bfloat16 [4096, 8192], P('dp', 'mp'), may hold values from -6 to 6
- w_proj: bfloat16 [3200, 8192], P(None, 'mp'), may hold values from -0.109375 to 0.109375
- llm_gain: float32 [8192], P('mp'), may hold values from 0.1 to 1.9
- w_key: bfloat16 [8192, 1024], P('mp'), may hold values from -0.0625 to 0.0625
- w_value: bfloat16 [8192, 1024], P('mp'), may hold values from -0.0625 to 0.0625
- key_grad: bfloat16 [4096, 1024], P('dp', 'mp'), may hold values from -6 to 6
- value_grad: bfloat16 [4096, 1024], P('dp', 'mp'), may hold values from -6 to 6
Outputs:
- key_out: bfloat16 [4096, 1024], P('dp', 'mp')
- value_out: bfloat16 [4096, 1024], P('dp', 'mp')
- text_grad: bfloat16 [4096, 8192], P('dp', 'mp')
- vision_grad: bfloat16 [2048, 3200], P(('dp', 'mp'))
The draws below stay inside these ranges and needn't reach their ends.
Inputs may be any that keep to these rules, and one draw needn't show every extreme that they name: `image_slot`: the 8 entries are different slots. Image i is encoded on index i of dp; slot j covers positions j * 256 to (j + 1) * 256 - 1, so it lies on index j // 2 of dp. One index of dp receives 2 images, every other one at most one.
All inputs are finite; a program needn't handle non-finite values.
Results may differ from the reference program's by a relative error of at most 0.0058.
Values may be sent and summed in bfloat16 or wider, within the bound.
A program may use at most 128 MiB of HBM per device.

```python
import jax
import jax.numpy as jnp
from jax import lax

DV = 3200
D = 8192
KV = 1024
PATCH = 256
SLOT_DEV = 2
IMAGES = 8
TOKENS = 4096


def draw_image_slot(key, part):
    first_key, second_key, third_key, fourth_key = jax.random.split(key, 4)
    count = IMAGES
    sources = jnp.arange(count, dtype=jnp.int32)
    heavy = jax.random.randint(first_key, (), 0, count).astype(jnp.int32)
    before = (heavy - 1) % count
    across = (heavy + 1 - count // 2) % count
    forced = (sources == before) | (sources == across)
    shuffled = jax.random.permutation(second_key, count).astype(jnp.int32)
    score = jnp.where(forced, count + sources, shuffled)
    order = jnp.argsort(score, stable=True).astype(jnp.int32)
    rank = jnp.zeros((count,), jnp.int32).at[order].set(sources)
    other_dest = (heavy + 2 + jax.random.permutation(third_key, count - 2).astype(jnp.int32)) % count
    later = jnp.clip(rank - (SLOT_DEV - 1), 0, count - 3)
    random_within = jax.random.randint(fourth_key, (count,), 0, SLOT_DEV).astype(jnp.int32)
    to_heavy = rank < SLOT_DEV - 1
    dest_of = jnp.where(to_heavy, heavy, other_dest[later])
    within = jnp.where(to_heavy, rank + 1, random_within)
    dest_of = jnp.where(sources == before, heavy, dest_of)
    within = jnp.where(sources == before, 0, within)
    dest_of = jnp.where(sources == across, (heavy + 1) % count, dest_of)
    slots = dest_of * SLOT_DEV + within
    return slots.astype(jnp.int32)


def block_scale(own_key, dims, shards, smallest, high):
    gain = 1.0
    for position, shards_of in shards:
        draws = jax.random.uniform(jax.random.fold_in(jax.random.fold_in(own_key, 6), position), (shards_of,), jnp.float32, smallest / len(shards), high / len(shards))
        gain = gain * jnp.repeat(jnp.exp(draws), dims[position] // shards_of).reshape((-1,) + (1,) * (len(dims) - 1 - position))
    return gain


def noise(stream_key, dims, spread, most, cuts=(), held_as=jnp.bfloat16):
    drawn = jax.random.normal(stream_key, dims, jnp.float32) * spread
    if len(cuts) > 0:
        drawn = block_scale(stream_key, dims, cuts, -0.22, 0.18) * drawn
    return jnp.clip(drawn, min=-most, max=most).astype(held_as)


def setup_inputs(seed: int = 0) -> dict:
    arg_keys = jax.random.split(jax.random.key(seed), 11)
    vision = noise(arg_keys[0], (IMAGES * PATCH, DV), 1.0, 6.0, ((0, 32),))
    vision_gain = jnp.clip(1.0 + 0.18 * jax.random.normal(arg_keys[1], (DV,), jnp.float32), 0.1, 1.9)
    image_slot = draw_image_slot(jax.random.fold_in(arg_keys[10], 71), 0)
    text_embed = noise(arg_keys[3], (TOKENS, D), 1.0, 6.0, ((0, 8), (1, 4)))
    w_proj = noise(arg_keys[4], (DV, D), DV ** -0.5, 0.109375, ((1, 4),))
    llm_gain = jnp.clip(1.0 + 0.18 * jax.random.normal(arg_keys[5], (D,), jnp.float32), 0.1, 1.9)
    w_key = noise(arg_keys[6], (D, KV), D ** -0.5, 0.0625, ((0, 4),))
    w_value = noise(arg_keys[7], (D, KV), D ** -0.5, 0.0625, ((0, 4),))
    key_grad = noise(arg_keys[8], (TOKENS, KV), 1.0, 6.0, ((0, 8), (1, 4)))
    value_grad = noise(arg_keys[9], (TOKENS, KV), 1.0, 6.0, ((0, 8), (1, 4)))
    return dict(vision=vision, vision_gain=vision_gain, image_slot=image_slot, text_embed=text_embed, w_proj=w_proj, llm_gain=llm_gain, w_key=w_key, w_value=w_value, key_grad=key_grad, value_grad=value_grad)


def reference(vision, vision_gain, image_slot, text_embed, w_proj, llm_gain, w_key, w_value, key_grad, value_grad):
    vision_f = vision.astype(jnp.float32)
    vis_scale = lax.rsqrt(lax.optimization_barrier(jnp.mean(vision_f * vision_f, axis=1, keepdims=True)) + 1e-06)
    vis_normed = (vision_f * vis_scale * vision_gain.astype(jnp.float32)).astype(jnp.bfloat16)
    slot_count = TOKENS // PATCH
    onehot = image_slot[:, None] == jnp.arange(slot_count, dtype=jnp.int32)[None, :]
    filled = jnp.any(onehot, axis=0)
    owner = lax.optimization_barrier(jnp.sum(jnp.where(onehot, jnp.arange(IMAGES, dtype=jnp.int32)[:, None], 0), axis=0)).astype(jnp.int32)
    projected = jnp.dot(vis_normed, w_proj, preferred_element_type=jnp.float32).astype(jnp.bfloat16)
    projected = projected.reshape(IMAGES, PATCH, D)
    placed = projected[owner]
    text_blocks = text_embed.reshape(slot_count, PATCH, D)
    embed = jnp.where(filled[:, None, None], placed, text_blocks).reshape(TOKENS, D)
    embed_f = embed.astype(jnp.float32)
    scale = lax.rsqrt(lax.optimization_barrier(jnp.mean(embed_f * embed_f, axis=1, keepdims=True)) + 1e-05)
    gain_f = llm_gain.astype(jnp.float32)
    llm_normed = (embed_f * scale * gain_f).astype(jnp.bfloat16)
    key_out = jnp.dot(llm_normed, w_key, preferred_element_type=jnp.float32).astype(jnp.bfloat16)
    value_out = jnp.dot(llm_normed, w_value, preferred_element_type=jnp.float32).astype(jnp.bfloat16)
    d_normed = jnp.dot(key_grad, w_key.T, preferred_element_type=jnp.float32)
    d_normed = d_normed + jnp.dot(value_grad, w_value.T, preferred_element_type=jnp.float32)
    grad_g = d_normed * gain_f
    inner = lax.optimization_barrier(jnp.sum(grad_g * embed_f, axis=1, keepdims=True))
    d_embed = scale * grad_g - embed_f * scale * scale * scale * (inner / D)
    d_blocks = d_embed.reshape(slot_count, PATCH, D)
    text_grad = jnp.where(filled[:, None, None], 0.0, d_blocks).reshape(TOKENS, D).astype(jnp.bfloat16)
    image_grad = d_blocks[image_slot].reshape(IMAGES * PATCH, D).astype(jnp.bfloat16)
    d_vis = jnp.dot(image_grad, w_proj.T, preferred_element_type=jnp.float32).astype(jnp.bfloat16)
    grad_h = d_vis.astype(jnp.float32) * vision_gain.astype(jnp.float32)
    vis_inner = lax.optimization_barrier(jnp.mean(grad_h * vision_f, axis=1, keepdims=True))
    vision_grad = vis_scale * grad_h - vision_f * vis_scale * vis_scale * vis_scale * vis_inner
    return (key_out, value_out, text_grad, vision_grad.astype(jnp.bfloat16))
```

```python
import functools

import jax
import jax.numpy as jnp
from jax import lax
from jax.experimental import pallas as pl
from jax.experimental.pallas import tpu as pltpu
from jax.sharding import PartitionSpec as P

PATCH = 256
F32 = jnp.float32
BF16 = jnp.bfloat16
NT = (((1,), (1,)), ((), ()))
DMA = pltpu.SemaphoreType.DMA


def nt(a, b):
    return lax.dot_general(a, b, NT, preferred_element_type=F32)


def remote(src, dst, send_sem, recv_sem, device):
    return pltpu.make_async_remote_copy(
        src_ref=src, dst_ref=dst, send_sem=send_sem, recv_sem=recv_sem,
        device_id=device, device_id_type=pl.DeviceIdType.MESH,
    )


def to_rows(sq, inner):
    lane = lax.broadcasted_iota(jnp.int32, (sq.shape[0], 128), 1)
    wide = jnp.where(lane == 0, sq, jnp.where(lane == 1, inner, 0.0))
    return jnp.transpose(wide)[:8]


def to_columns(rows):
    wide = jnp.transpose(jnp.concatenate([rows] * 16, axis=0))
    return wide[:, 0:1], wide[:, 1:2]


def gain_row(ref):
    if ref.shape[0] == 1:
        return ref[...]
    return jnp.concatenate([ref[i:i + 1, :] for i in range(ref.shape[0])], axis=1)


def write_out(*refs):
    count = (len(refs) - 1) // 2
    copies = [pltpu.make_async_copy(refs[n], refs[count + n], refs[-1].at[n]) for n in range(count)]
    for copy in copies:
        copy.start()
    for copy in copies:
        copy.wait()


def kernel(
    dp, mp, slot_ref, vision_h, vgain, text_h, wp_h, gain, wk_h, wv_h, kg_h, vg_h, kg4, vg4,
    k_out, v_out, tg, vg_out,
    vis, vis_all, text, wp, wk, wv, xt, gk, gv, gik, giv, emb, xi, dimg, dg,
    t_send, t_own, t_l1, t_s2, t_l2, i_send, i_own, i_l1, i_s2, i_l2,
    d_send, d_own, d_l1, d_s2, d_l2, kvt, kvi,
    st_t, sr_t, st_i, sr_i, sc_t, co_t, sc_i, co_i,
    r1k, r1v, s2k, s2v, r2k, r2v, kvb, r3, s4, r4,
    load_sem, ag_s, ag_r, rs_s, rs_r, st_s, st_r, dv_s, dv_r,
    a1_s, a1_r, a2_s, a2_r, b1_s, b1_r, b2_s, b2_r, dt,
):
    me_d = lax.axis_index("dp")
    me = lax.axis_index("mp")
    ycount = mp // 2
    core = lax.rem(me, 2)
    y = lax.div(me, 2)
    partner = y * 2 + (1 - core)
    tokens, width = text.shape
    slots = tokens // PATCH
    kvd = gk.shape[1] // mp
    rows = vis.shape[0]
    dv = vis.shape[1]
    d_model = width * mp
    rb = r1k.shape[1]

    def ynext(k):
        return lax.rem(y + k, ycount)

    def yprev(k):
        return lax.rem(y + ycount - k, ycount)

    def dnext(k):
        return lax.rem(me_d + k, dp)

    def dprev(k):
        return lax.rem(me_d + dp - k, dp)

    def col(m):
        return pl.ds(pl.multiple_of(m * kvd, kvd), kvd)

    def owner_of(slot):
        found = jnp.int32(0)
        for i in range(dp):
            found = jnp.where(slot_ref[i] == slot, jnp.int32(i), found)
        return found

    def filled(s):
        found = jnp.int32(0)
        for i in range(dp):
            found = jnp.where(slot_ref[i] == me_d * slots + s, jnp.int32(1), found)
        return found.astype(F32)

    sends = []

    def send(*args):
        copy = remote(*args)
        copy.start()
        sends.append(copy)

    loads = [
        (vision_h, vis), (kg_h, gk.at[:, col(me)]), (vg_h, gv.at[:, col(me)]),
        (text_h, text), (wk_h, wk), (wv_h, wv), (wp_h, wp),
        (kg4.at[:, me_d], r1k.at[pl.ds(me_d * slots, slots)]),
        (vg4.at[:, me_d], r1v.at[pl.ds(me_d * slots, slots)]),
    ]
    loads = [pltpu.make_async_copy(a, b, load_sem.at[n]) for n, (a, b) in enumerate(loads)]
    for copy in loads:
        copy.start()

    barrier = pltpu.get_barrier_semaphore()

    @pl.loop(1, dp)
    def _(k):
        pl.semaphore_signal(barrier, inc=1, device_id=(dnext(k), me), device_id_type=pl.DeviceIdType.MESH)

    for k in range(1, mp):
        pl.semaphore_signal(
            barrier, inc=1, device_id=(me_d, lax.rem(me + k, mp)), device_id_type=pl.DeviceIdType.MESH
        )

    loads[0].wait()
    vf = vis[...].astype(F32)
    vscale = lax.rsqrt(jnp.mean(vf * vf, axis=1, keepdims=True) + 1e-06)
    vis_gain = gain_row(vgain)
    vis_all[me] = (vf * vscale * vis_gain).astype(BF16)
    pl.semaphore_wait(barrier, dp - 1 + mp - 1)

    def gather_start(g, block):
        for k in range(1, ycount):
            send(block(me), block(me), ag_s.at[g, 0, k], ag_r.at[g, 0, k], (me_d, ynext(k) * 2 + core))
        send(block(me), block(me), ag_s.at[g, 0, 0], ag_r.at[g, 0, 0], (me_d, partner))

    def arrived(block, send_sem, recv_sem):
        remote(block, block, send_sem, recv_sem, (me_d, partner)).wait_recv()

    def gather_relay(g, block):
        for k in range(1, ycount):
            got = block(yprev(k) * 2 + core)
            arrived(got, ag_s.at[g, 0, k], ag_r.at[g, 0, k])
            send(got, got, ag_s.at[g, 1, k], ag_r.at[g, 1, k], (me_d, partner))

    def gather_finish(g, block):
        arrived(block(partner), ag_s.at[g, 0, 0], ag_r.at[g, 0, 0])
        for k in range(1, ycount):
            arrived(block(yprev(k) * 2 + 1 - core), ag_s.at[g, 1, k], ag_r.at[g, 1, k])

    vis_block = lambda m: vis_all.at[m]
    gk_block = lambda m: gk.at[:, col(m)]
    gv_block = lambda m: gv.at[:, col(m)]
    gik_block = lambda m: gik.at[:, col(m)]
    giv_block = lambda m: giv.at[:, col(m)]

    gather_start(0, vis_block)

    mine = pl.ds(me_d * slots, slots)

    def a1(k, which):
        src, dst = ((kg4, r1k), (vg4, r1v))[which]
        return remote(
            src.at[:, dnext(k)], dst.at[mine], a1_s.at[which, k], a1_r.at[which, k], (dnext(k), me)
        )

    @pl.loop(1, dp)
    def _(k):
        a1(k, 0).start()
        a1(k, 1).start()

    loads[1].wait()
    loads[2].wait()
    gather_start(1, gk_block)
    gather_start(2, gv_block)

    def stage(x, n, psend, own, l1):
        def chunk(m):
            k_part = jnp.dot(x[...], wk[:, col(m)], preferred_element_type=F32)
            v_part = jnp.dot(x[...], wv[:, col(m)], preferred_element_type=F32)
            return k_part, v_part

        for k in range(ycount):
            yk = ynext(k)
            k_part, v_part = chunk(yk * 2 + 1 - core)
            psend[yk, :, :kvd] = k_part.astype(BF16)
            psend[yk, :, kvd:] = v_part.astype(BF16)
            send(psend.at[yk], l1.at[yk], rs_s.at[n, 0, k], rs_r.at[n, 0, k], (me_d, partner))
        for k in range(ycount):
            yk = ynext(k)
            k_part, v_part = chunk(yk * 2 + core)
            own[yk, :, :kvd] = k_part
            own[yk, :, kvd:] = v_part

    def level_two(n, own, l1, s2, l2):
        for k in range(ycount - 1, 0, -1):
            yk = ynext(k)
            arrived(l1.at[yk], rs_s.at[n, 0, k], rs_r.at[n, 0, k])
            s2[k] = (own[yk] + l1[yk].astype(F32)).astype(BF16)

    def level_go(n, s2, l2):
        for k in range(ycount - 1, 0, -1):
            send(s2.at[k], l2.at[k], rs_s.at[n, 1, k], rs_r.at[n, 1, k], (me_d, ynext(k) * 2 + core))

    def level_end(n, own, l1, l2):
        arrived(l1.at[y], rs_s.at[n, 0, 0], rs_r.at[n, 0, 0])
        total = own[y] + l1[y].astype(F32)
        for k in range(1, ycount):
            arrived(l2.at[k], rs_s.at[n, 1, k], rs_r.at[n, 1, k])
            total = total + l2[k].astype(F32)
        return total

    def stats_send(n, st, sr):
        for k in range(1, mp):
            send(st, sr.at[k], st_s.at[n, k], st_r.at[n, k], (me_d, lax.rem(me + k, mp)))

    def stats_end(n, st, sr, sc, co, keep):
        total = st[...]
        for k in range(1, mp):
            arrived(sr.at[k], st_s.at[n, k], st_r.at[n, k])
            total = total + sr[k]
        sq, inner = to_columns(total)
        scale = lax.rsqrt(sq / d_model + 1e-05)
        sc[...] = jnp.broadcast_to(scale * keep, sc.shape)
        co[...] = jnp.broadcast_to(scale * scale * scale * (inner / d_model) * keep, co.shape)

    loads[3].wait()
    tf = text[...].astype(F32)
    sq_t = jnp.sum(tf * tf, axis=1, keepdims=True)
    xt[...] = (tf * gain[...]).astype(BF16)
    loads[4].wait()
    loads[5].wait()
    stage(xt, 0, t_send, t_own, t_l1)
    gather_relay(0, vis_block)
    level_two(0, t_own, t_l1, t_s2, t_l2)

    gather_finish(0, vis_block)
    loads[6].wait()
    step = 256
    dimg_rows = mp * rows


    def project(j, acc):
        cs = pl.ds(pl.multiple_of(j * step, step), step)
        e = jnp.concatenate([vis_all[m] for m in range(mp)], axis=0)
        e = jnp.dot(e, wp[:, cs], preferred_element_type=F32).astype(BF16)
        emb[:, cs] = e
        ef = e.astype(F32)
        xi[:, cs] = (ef * gain[:, cs]).astype(BF16)
        return acc + jnp.sum(ef * ef, axis=1, keepdims=True)

    half = width // step // 2
    sq_i = lax.fori_loop(0, half, project, jnp.zeros((dimg_rows, 1), F32))

    loads[7].wait()
    loads[8].wait()

    @pl.loop(1, dp)
    def _(k):
        for which, dst in ((0, r1k), (1, r1v)):
            block = dst.at[pl.ds(dprev(k) * slots, slots)]
            remote(block, block, a1_s.at[which, k], a1_r.at[which, k], (me_d, partner)).wait_recv()

    @pl.loop(0, dp)
    def _(i):
        s2k[i] = r1k[slot_ref[i]]
        s2v[i] = r1v[slot_ref[i]]

    r2k[me_d] = s2k[me_d]
    r2v[me_d] = s2v[me_d]

    def a2(k, which):
        src, dst = ((s2k, r2k), (s2v, r2v))[which]
        return remote(
            src.at[dnext(k)], dst.at[me_d], a2_s.at[which, k], a2_r.at[which, k], (dnext(k), me)
        )

    @pl.loop(1, dp)
    def _(k):
        a2(k, 0).start()
        a2(k, 1).start()

    sq_i = lax.fori_loop(half, width // step, project, sq_i)
    stage(xi, 1, i_send, i_own, i_l1)
    level_two(1, i_own, i_l1, i_s2, i_l2)
    level_go(1, i_s2, i_l2)

    @pl.loop(1, dp)
    def _(k):
        for which, dst in ((0, r2k), (1, r2v)):
            block = dst.at[dprev(k)]
            remote(block, block, a2_s.at[which, k], a2_r.at[which, k], (me_d, partner)).wait_recv()

    own_k = r2k[...].astype(F32).reshape(PATCH, kvd)
    own_v = r2v[...].astype(F32).reshape(PATCH, kvd)
    gik[:, col(me)] = own_k.astype(BF16)
    giv[:, col(me)] = own_v.astype(BF16)
    gather_start(3, gik_block)
    gather_start(4, giv_block)
    level_go(0, t_s2, t_l2)
    gather_relay(1, gk_block)
    gather_relay(2, gv_block)
    gather_finish(1, gk_block)
    gather_finish(2, gv_block)

    def text_product(j, _):
        cs = pl.ds(pl.multiple_of(j * step, step), step)
        dt[:, cs] = (nt(gk[...], wk[cs, :]) + nt(gv[...], wv[cs, :])) * gain[:, cs]
        return 0

    lax.fori_loop(0, width // step, text_product, 0)

    total = level_end(1, i_own, i_l1, i_l2)
    kvi[...] = total
    inner = jnp.sum(
        total[:, :kvd] * gik[:, col(me)].astype(F32) + total[:, kvd:] * giv[:, col(me)].astype(F32),
        axis=1, keepdims=True,
    )
    st_i[...] = to_rows(sq_i, inner)
    stats_send(1, st_i, sr_i)
    gather_relay(3, gik_block)
    gather_relay(4, giv_block)
    gather_finish(3, gik_block)
    gather_finish(4, giv_block)

    def image_back(j, _):
        cs = pl.ds(pl.multiple_of(j * step, step), step)
        dg[:, cs] = (nt(gik[...], wk[cs, :]) + nt(giv[...], wv[cs, :])) * gain[:, cs]
        return 0

    lax.fori_loop(0, width // step, image_back, 0)
    stats_end(1, st_i, sr_i, sc_i, co_i, 1.0)
    kvb[...] = (kvi[...] * sc_i[:, 0:1]).reshape(dp, rb, 2 * kvd).astype(BF16)
    r3[me_d] = kvb[me_d]

    def b1(k):
        return remote(kvb.at[dnext(k)], r3.at[me_d], b1_s.at[k], b1_r.at[k], (dnext(k), me))

    @pl.loop(1, dp)
    def _(k):
        b1(k).start()

    def image_end(j, _):
        cs = pl.ds(pl.multiple_of(j * step, step), step)
        d = sc_i[:, 0:1] * dg[:, cs] - emb[:, cs].astype(F32) * co_i[:, 0:1]
        dimg[:, cs] = d.astype(BF16)
        return 0

    lax.fori_loop(0, width // step, image_end, 0)

    pieces = d_send.shape[0]
    span = dv // pieces

    def vis_chunk(j):
        d = nt(dimg[...], wp[j * span:(j + 1) * span, :]).reshape(ycount, 2, rows, span)
        for yi in range(ycount):
            a, b = d[yi, 0], d[yi, 1]
            first = core == 0
            d_own[j, yi] = jnp.where(first, a, b)
            d_send[j, yi] = jnp.where(first, b, a).astype(BF16)
        send(d_send.at[j], d_l1.at[j], dv_s.at[0, j, 0], dv_r.at[0, j, 0], (me_d, partner))

    def vis_two(j):
        arrived(d_l1.at[j], dv_s.at[0, j, 0], dv_r.at[0, j, 0])
        for k in range(1, ycount):
            yk = ynext(k)
            d_s2[j, k] = (d_own[j, yk] + d_l1[j, yk].astype(F32)).astype(BF16)
            send(d_s2.at[j, k], d_l2.at[j, k], dv_s.at[1, j, k], dv_r.at[1, j, k], (me_d, yk * 2 + core))

    def b2(k):
        return remote(s4.at[dnext(k)], r4.at[:, me_d], b2_s.at[k], b2_r.at[k], (dnext(k), me))

    for j in range(pieces):
        vis_chunk(j)
        if j > 0:
            vis_two(j - 1)
        if j == min(2, pieces - 1):

            @pl.loop(1, dp)
            def _(k):
                block = r3.at[dprev(k)]
                remote(block, block, b1_s.at[k], b1_r.at[k], (me_d, partner)).wait_recv()

            @pl.loop(0, dp)
            def _(d):
                for s in range(slots):
                    s4[d, s] = r3[owner_of(d * slots + s)]

            for s in range(slots):
                r4[s, me_d] = s4[me_d, s]

            @pl.loop(1, dp)
            def _(k):
                b2(k).start()

    vis_two(pieces - 1)

    total = level_end(0, t_own, t_l1, t_l2)
    kvt[...] = total
    inner = jnp.sum(
        total[:, :kvd] * gk[:, col(me)].astype(F32) + total[:, kvd:] * gv[:, col(me)].astype(F32),
        axis=1, keepdims=True,
    )
    st_t[...] = to_rows(sq_t, inner)
    stats_send(0, st_t, sr_t)
    keep = jnp.concatenate([jnp.full((PATCH, 1), 1.0, F32) * (1.0 - filled(s)) for s in range(slots)], axis=0)
    stats_end(0, st_t, sr_t, sc_t, co_t, keep)

    def text_back(j, _):
        cs = pl.ds(pl.multiple_of(j * step, step), step)
        d = sc_t[:, 0:1] * dt[:, cs] - text[:, cs].astype(F32) * co_t[:, 0:1]
        tg[:, cs] = d.astype(BF16)
        return 0

    lax.fori_loop(0, width // step, text_back, 0)

    hs = []
    for j in range(pieces):
        d = d_own[j, y] + d_l1[j, y].astype(F32)
        for k in range(1, ycount):
            arrived(d_l2.at[j, k], dv_s.at[1, j, k], dv_r.at[1, j, k])
            d = d + d_l2[j, k].astype(F32)
        hs.append(d.astype(BF16).astype(F32))
    vf = vis[...].astype(F32)
    vscale = lax.rsqrt(jnp.mean(vf * vf, axis=1, keepdims=True) + 1e-06)
    h = jnp.concatenate(hs, axis=1) * gain_row(vgain)
    v_inner = jnp.mean(h * vf, axis=1, keepdims=True)
    vg_out[...] = (vscale * h - vf * vscale * vscale * vscale * v_inner).astype(BF16)

    @pl.loop(1, dp)
    def _(k):
        block = r4.at[:, dprev(k)]
        remote(block, block, b2_s.at[k], b2_r.at[k], (me_d, partner)).wait_recv()

    for s in range(slots):
        at = pl.ds(s * PATCH, PATCH)
        out = kvt[at, :] * sc_t[at, 0:1] + r4[s].astype(F32).reshape(PATCH, 2 * kvd) * filled(s)
        k_out[at, :] = out[:, :kvd].astype(BF16)
        v_out[at, :] = out[:, kvd:].astype(BF16)

    for copy in sends:
        copy.wait_send()

    @pl.loop(1, dp)
    def _(k):
        a1(k, 0).wait_send()
        a1(k, 1).wait_send()
        a2(k, 0).wait_send()
        a2(k, 1).wait_send()
        b1(k).wait_send()
        b2(k).wait_send()


def shards(vision, vision_gain, image_slot, text_embed, w_proj, llm_gain, w_key, w_value, key_grad, value_grad):
    dp = lax.axis_size("dp")
    mp = lax.axis_size("mp")
    tokens, width = text_embed.shape
    slots = tokens // PATCH
    rows, dv = vision.shape
    kvd = key_grad.shape[1]
    kv = kvd * mp
    img = rows * mp
    rb = PATCH // dp
    ys = mp // 2
    pieces = 5 if dv % 640 == 0 else 1
    span = dv // pieces
    V = pltpu.VMEM
    any_spec = pl.BlockSpec(memory_space=pl.ANY)
    vmem = pl.BlockSpec(memory_space=pltpu.VMEM)
    smem = pl.BlockSpec(memory_space=pltpu.SMEM)
    scratch = [
        V((rows, dv), BF16), V((mp, rows, dv), BF16), V((tokens, width), BF16), V((dv, width), BF16),
        V((width, kv), BF16), V((width, kv), BF16), V((tokens, width), BF16),
        V((tokens, kv), BF16), V((tokens, kv), BF16), V((img, kv), BF16), V((img, kv), BF16),
        V((img, width), BF16), V((img, width), BF16), V((img, width), BF16), V((img, width), F32),
    ]
    for n in (tokens, img):
        scratch += [
            V((ys, n, 2 * kvd), BF16), V((ys, n, 2 * kvd), F32), V((ys, n, 2 * kvd), BF16),
            V((ys, n, 2 * kvd), BF16), V((ys, n, 2 * kvd), BF16),
        ]
    scratch += [
        V((pieces, ys, rows, span), BF16), V((pieces, ys, rows, span), F32), V((pieces, ys, rows, span), BF16),
        V((pieces, ys, rows, span), BF16), V((pieces, ys, rows, span), BF16),
        V((tokens, 2 * kvd), F32), V((img, 2 * kvd), F32),
        V((8, tokens), F32), V((mp, 8, tokens), F32), V((8, img), F32), V((mp, 8, img), F32),
        V((tokens, 128), F32), V((tokens, 128), F32), V((img, 128), F32), V((img, 128), F32),
        V((dp * slots, rb, kvd), BF16), V((dp * slots, rb, kvd), BF16),
        V((dp, rb, kvd), BF16), V((dp, rb, kvd), BF16), V((dp, rb, kvd), BF16), V((dp, rb, kvd), BF16),
        V((dp, rb, 2 * kvd), BF16), V((dp, rb, 2 * kvd), BF16),
        V((dp, slots, rb, 2 * kvd), BF16), V((slots, dp, rb, 2 * kvd), BF16),
        DMA((9,)), DMA((5, 2, ys)), DMA((5, 2, ys)), DMA((2, 2, ys)), DMA((2, 2, ys)),
        DMA((2, mp)), DMA((2, mp)), DMA((2, pieces, ys)), DMA((2, pieces, ys)),
        DMA((2, dp)), DMA((2, dp)), DMA((2, dp)), DMA((2, dp)),
        DMA((dp,)), DMA((dp,)), DMA((dp,)), DMA((dp,)), V((tokens, width), F32),
    ]
    shapes = ((tokens, kvd), (tokens, kvd), (tokens, width), (rows, dv))
    room = sum(2 * a * b for a, b in shapes)
    lanes = 128 if dv % 128 == 0 else dv
    results = pl.pallas_call(
        functools.partial(kernel, dp, mp),
        out_shape=tuple(V(shape, BF16) for shape in shapes),
        in_specs=[smem, any_spec, vmem, any_spec, any_spec, vmem] + [any_spec] * 6,
        out_specs=(vmem,) * len(shapes),
        scratch_shapes=scratch,
        compiler_params=pltpu.CompilerParams(
            collective_id=0, has_side_effects=True, vmem_limit_bytes=67043328 - room
        ),
    )(
        image_slot, vision, vision_gain.reshape(-1, lanes), text_embed, w_proj, llm_gain[None, :],
        w_key, w_value, key_grad, value_grad,
        key_grad.reshape(slots, dp, rb, kvd), value_grad.reshape(slots, dp, rb, kvd),
    )
    return pl.pallas_call(
        write_out,
        out_shape=tuple(jax.ShapeDtypeStruct(shape, BF16) for shape in shapes),
        in_specs=[vmem] * len(shapes),
        out_specs=(any_spec,) * len(shapes),
        scratch_shapes=[DMA((len(shapes),))],
        compiler_params=pltpu.CompilerParams(vmem_limit_bytes=1 << 20),
    )(*results)


def solution(mesh):
    placed = (
        P(("dp", "mp"), None),
        P(),
        P(),
        P("dp", "mp"),
        P(None, "mp"),
        P("mp"),
        P("mp", None),
        P("mp", None),
        P("dp", "mp"),
        P("dp", "mp"),
    )
    return jax.shard_map(
        shards,
        mesh=mesh,
        in_specs=placed,
        out_specs=(P("dp", "mp"), P("dp", "mp"), P("dp", "mp"), P(("dp", "mp"), None)),
        check_vma=False,
    )
```

```python
import functools

import jax
import jax.numpy as jnp
from jax import lax
from jax.experimental import pallas as pl
from jax.experimental.pallas import tpu as pltpu
from jax.sharding import PartitionSpec as P

PATCH = 256
F32 = jnp.float32
BF16 = jnp.bfloat16
NT = (((1,), (1,)), ((), ()))
DMA = pltpu.SemaphoreType.DMA


def nt(a, b):
    return lax.dot_general(a, b, NT, preferred_element_type=F32)


def remote(src, dst, send_sem, recv_sem, device):
    return pltpu.make_async_remote_copy(
        src_ref=src, dst_ref=dst, send_sem=send_sem, recv_sem=recv_sem,
        device_id=device, device_id_type=pl.DeviceIdType.MESH,
    )


def to_rows(sq, inner):
    lane = lax.broadcasted_iota(jnp.int32, (sq.shape[0], 128), 1)
    wide = jnp.where(lane == 0, sq, jnp.where(lane == 1, inner, 0.0))
    return jnp.transpose(wide)[:8]


def to_columns(rows):
    wide = jnp.transpose(jnp.concatenate([rows] * 16, axis=0))
    return wide[:, 0:1], wide[:, 1:2]


def gain_row(ref):
    if ref.shape[0] == 1:
        return ref[...]
    return jnp.concatenate([ref[i:i + 1, :] for i in range(ref.shape[0])], axis=1)


def write_out(*refs):
    count = (len(refs) - 1) // 2
    copies = [pltpu.make_async_copy(refs[n], refs[count + n], refs[-1].at[n]) for n in range(count)]
    for copy in copies:
        copy.start()
    for copy in copies:
        copy.wait()


def kernel(
    dp, mp, slot_ref, vision_h, vgain, text_h, wp_h, gain, wk_h, wv_h, kg_h, vg_h, kg4, vg4,
    k_out, v_out, tg, vg_out,
    vis, vis_all, text, wp, wk, wv, xt, gk, gv, gik, giv, emb, xi, dimg, dg,
    t_send, t_own, t_l1, t_s2, t_l2, i_send, i_own, i_l1, i_s2, i_l2,
    d_send, d_own, d_l1, d_s2, d_l2,
    st_t, sr_t, st_i, sr_i, st_q, sr_q, sc_t, co_t, sc_i, co_i,
    r1k, r1v, s2k, s2v, r2k, r2v, kvb, r3, s4, r4,
    load_sem, ag_s, ag_r, rs_s, rs_r, t2_s, t2_r, st_s, st_r, dv_s, dv_r,
    a1_s, a1_r, a2_s, a2_r, b1_s, b1_r, b2_s, b2_r, dt,
):
    me_d = lax.axis_index("dp")
    me = lax.axis_index("mp")
    ycount = mp // 2
    core = lax.rem(me, 2)
    y = lax.div(me, 2)
    partner = y * 2 + (1 - core)
    tokens, width = text.shape
    slots = tokens // PATCH
    kvd = gk.shape[1] // mp
    rows = vis.shape[0]
    dv = vis.shape[1]
    d_model = width * mp
    rb = r1k.shape[1]
    img_rows = mp * rows
    t_pieces = 2 * slots
    piece_rows = tokens // t_pieces

    def ynext(k):
        return lax.rem(y + k, ycount)

    def yprev(k):
        return lax.rem(y + ycount - k, ycount)

    def dnext(k):
        return lax.rem(me_d + k, dp)

    def dprev(k):
        return lax.rem(me_d + dp - k, dp)

    def col(m):
        return pl.ds(pl.multiple_of(m * kvd, kvd), kvd)

    def owner_of(slot):
        found = jnp.int32(0)
        for i in range(dp):
            found = jnp.where(slot_ref[i] == slot, jnp.int32(i), found)
        return found

    def filled(s):
        found = jnp.int32(0)
        for i in range(dp):
            found = jnp.where(slot_ref[i] == me_d * slots + s, jnp.int32(1), found)
        return found.astype(F32)

    sends = []

    def send(*args):
        copy = remote(*args)
        copy.start()
        sends.append(copy)

    loads = [
        (vision_h, vis), (kg_h, gk.at[:, col(me)]), (vg_h, gv.at[:, col(me)]),
        (text_h, text), (wk_h, wk), (wv_h, wv), (wp_h, wp),
        (kg4.at[:, me_d], r1k.at[pl.ds(me_d * slots, slots)]),
        (vg4.at[:, me_d], r1v.at[pl.ds(me_d * slots, slots)]),
    ]
    loads = [pltpu.make_async_copy(a, b, load_sem.at[n]) for n, (a, b) in enumerate(loads)]
    for copy in loads:
        copy.start()

    barrier = pltpu.get_barrier_semaphore()

    @pl.loop(1, dp)
    def _(k):
        pl.semaphore_signal(barrier, inc=1, device_id=(dnext(k), me), device_id_type=pl.DeviceIdType.MESH)

    for k in range(1, mp):
        pl.semaphore_signal(
            barrier, inc=1, device_id=(me_d, lax.rem(me + k, mp)), device_id_type=pl.DeviceIdType.MESH
        )

    loads[0].wait()
    vf = vis[...].astype(F32)
    vscale = lax.rsqrt(jnp.mean(vf * vf, axis=1, keepdims=True) + 1e-06)
    vis_gain = gain_row(vgain)
    vis_all[me] = (vf * vscale * vis_gain).astype(BF16)
    pl.semaphore_wait(barrier, dp - 1 + mp - 1)

    def gather_start(g, block):
        for k in range(1, ycount):
            send(block(me), block(me), ag_s.at[g, 0, k], ag_r.at[g, 0, k], (me_d, ynext(k) * 2 + core))
        send(block(me), block(me), ag_s.at[g, 0, 0], ag_r.at[g, 0, 0], (me_d, partner))

    def arrived(block, send_sem, recv_sem):
        remote(block, block, send_sem, recv_sem, (me_d, partner)).wait_recv()

    def gather_relay(g, block):
        for k in range(1, ycount):
            got = block(yprev(k) * 2 + core)
            arrived(got, ag_s.at[g, 0, k], ag_r.at[g, 0, k])
            send(got, got, ag_s.at[g, 1, k], ag_r.at[g, 1, k], (me_d, partner))

    def gather_finish(g, block):
        arrived(block(partner), ag_s.at[g, 0, 0], ag_r.at[g, 0, 0])
        for k in range(1, ycount):
            arrived(block(yprev(k) * 2 + 1 - core), ag_s.at[g, 1, k], ag_r.at[g, 1, k])

    vis_block = lambda m: vis_all.at[m]
    gk_block = lambda m: gk.at[:, col(m)]
    gv_block = lambda m: gv.at[:, col(m)]
    gik_block = lambda m: gik.at[:, col(m)]
    giv_block = lambda m: giv.at[:, col(m)]

    gather_start(0, vis_block)

    mine = pl.ds(me_d * slots, slots)

    def a1(k, which):
        src, dst = ((kg4, r1k), (vg4, r1v))[which]
        return remote(
            src.at[:, dnext(k)], dst.at[mine], a1_s.at[which, k], a1_r.at[which, k], (dnext(k), me)
        )

    @pl.loop(1, dp)
    def _(k):
        a1(k, 0).start()
        a1(k, 1).start()

    loads[1].wait()
    loads[2].wait()
    gather_start(1, gk_block)
    gather_start(2, gv_block)

    def stage(x, n, psend, own, l1):
        def chunk(m):
            k_part = jnp.dot(x[...], wk[:, col(m)], preferred_element_type=F32)
            v_part = jnp.dot(x[...], wv[:, col(m)], preferred_element_type=F32)
            return k_part, v_part

        for k in range(ycount):
            yk = ynext(k)
            k_part, v_part = chunk(yk * 2 + 1 - core)
            psend[yk, :, :kvd] = k_part.astype(BF16)
            psend[yk, :, kvd:] = v_part.astype(BF16)
            send(psend.at[yk], l1.at[yk], rs_s.at[n, 0, k], rs_r.at[n, 0, k], (me_d, partner))
        for k in range(ycount):
            yk = ynext(k)
            k_part, v_part = chunk(yk * 2 + core)
            own[yk, :, :kvd] = k_part
            own[yk, :, kvd:] = v_part

    def level_two(n, own, l1, s2, l2):
        for k in range(ycount - 1, 0, -1):
            yk = ynext(k)
            arrived(l1.at[yk], rs_s.at[n, 0, k], rs_r.at[n, 0, k])
            s2[k] = (own[yk] + l1[yk].astype(F32)).astype(BF16)

    def level_go(n, s2, l2):
        for k in range(ycount - 1, 0, -1):
            send(s2.at[k], l2.at[k], rs_s.at[n, 1, k], rs_r.at[n, 1, k], (me_d, ynext(k) * 2 + core))

    def level_end(n, own, l1, l2):
        arrived(l1.at[y], rs_s.at[n, 0, 0], rs_r.at[n, 0, 0])
        total = own[y] + l1[y].astype(F32)
        for k in range(1, ycount):
            arrived(l2.at[k], rs_s.at[n, 1, k], rs_r.at[n, 1, k])
            total = total + l2[k].astype(F32)
        return total

    def text_piece(p, k):
        at = pl.ds(p * piece_rows, piece_rows)
        return remote(
            t_s2.at[k, at], t_l2.at[k, at], t2_s.at[k, p], t2_r.at[k, p], (me_d, ynext(k) * 2 + core)
        )

    def text_go(p):
        for k in range(ycount - 1, 0, -1):
            copy = text_piece(p, k)
            copy.start()
            sends.append(copy)

    def stats_send(n, st, sr):
        for k in range(1, mp):
            send(st, sr.at[k], st_s.at[n, k], st_r.at[n, k], (me_d, lax.rem(me + k, mp)))

    def stats_total(n, st, sr):
        total = st[...]
        for k in range(1, mp):
            arrived(sr.at[k], st_s.at[n, k], st_r.at[n, k])
            total = total + sr[k]
        return to_columns(total)

    def fold(p):
        total = p[:, :128]
        for n in range(1, p.shape[1] // 128):
            total = total + p[:, n * 128:(n + 1) * 128]
        return total

    loads[3].wait()
    tf = text[...].astype(F32)
    sc_t[...] = fold(tf * tf)
    xt[...] = (tf * gain[...]).astype(BF16)
    loads[4].wait()
    loads[5].wait()
    stage(xt, 0, t_send, t_own, t_l1)
    level_two(0, t_own, t_l1, t_s2, t_l2)
    gather_relay(0, vis_block)
    loads[7].wait()
    loads[8].wait()

    @pl.loop(1, dp)
    def _(k):
        for which, dst in ((0, r1k), (1, r1v)):
            block = dst.at[pl.ds(dprev(k) * slots, slots)]
            remote(block, block, a1_s.at[which, k], a1_r.at[which, k], (me_d, partner)).wait_recv()

    @pl.loop(0, dp)
    def _(i):
        s2k[i] = r1k[slot_ref[i]]
        s2v[i] = r1v[slot_ref[i]]

    r2k[me_d] = s2k[me_d]
    r2v[me_d] = s2v[me_d]

    def a2(k, which):
        src, dst = ((s2k, r2k), (s2v, r2v))[which]
        return remote(
            src.at[dnext(k)], dst.at[me_d], a2_s.at[which, k], a2_r.at[which, k], (dnext(k), me)
        )

    @pl.loop(1, dp)
    def _(k):
        a2(k, 0).start()
        a2(k, 1).start()

    gather_finish(0, vis_block)
    loads[6].wait()
    step = 256

    sc_i[...] = jnp.zeros(sc_i.shape, F32)

    def project(j, _):
        cs = pl.ds(pl.multiple_of(j * step, step), step)
        e = jnp.concatenate([vis_all[m] for m in range(mp)], axis=0)
        e = jnp.dot(e, wp[:, cs], preferred_element_type=F32).astype(BF16)
        emb[:, cs] = e
        ef = e.astype(F32)
        xi[:, cs] = (ef * gain[:, cs]).astype(BF16)
        sc_i[...] += fold(ef * ef)
        return 0

    lax.fori_loop(0, width // step, project, 0)
    zero = jnp.zeros((img_rows, 1), F32)
    st_q[...] = to_rows(jnp.sum(sc_i[...], axis=1, keepdims=True), zero)
    stats_send(2, st_q, sr_q)
    stage(xi, 1, i_send, i_own, i_l1)

    @pl.loop(1, dp)
    def _(k):
        for which, dst in ((0, r2k), (1, r2v)):
            block = dst.at[dprev(k)]
            remote(block, block, a2_s.at[which, k], a2_r.at[which, k], (me_d, partner)).wait_recv()

    own_k = r2k[...].astype(F32).reshape(PATCH, kvd)
    own_v = r2v[...].astype(F32).reshape(PATCH, kvd)
    gik[:, col(me)] = own_k.astype(BF16)
    giv[:, col(me)] = own_v.astype(BF16)
    gather_start(3, gik_block)
    gather_start(4, giv_block)
    level_two(1, i_own, i_l1, i_s2, i_l2)
    level_go(1, i_s2, i_l2)
    gather_relay(1, gk_block)
    gather_relay(2, gv_block)
    gather_finish(1, gk_block)
    gather_finish(2, gv_block)
    co_t[...] = jnp.zeros(co_t.shape, F32)

    def text_product(j, _):
        cs = pl.ds(pl.multiple_of(j * step, step), step)
        d = (nt(gk[...], wk[cs, :]) + nt(gv[...], wv[cs, :])) * gain[:, cs]
        dt[:, cs] = d
        co_t[...] += fold(d * text[:, cs].astype(F32))
        return 0

    lax.fori_loop(0, width // step, text_product, 0)
    st_t[...] = to_rows(
        jnp.sum(sc_t[...], axis=1, keepdims=True), jnp.sum(co_t[...], axis=1, keepdims=True)
    )
    stats_send(0, st_t, sr_t)
    gather_relay(3, gik_block)
    gather_relay(4, giv_block)
    gather_finish(3, gik_block)
    gather_finish(4, giv_block)
    co_i[...] = jnp.zeros(co_i.shape, F32)

    def image_back(j, _):
        cs = pl.ds(pl.multiple_of(j * step, step), step)
        d = (nt(gik[...], wk[cs, :]) + nt(giv[...], wv[cs, :])) * gain[:, cs]
        dg[:, cs] = d
        co_i[...] += fold(d * emb[:, cs].astype(F32))
        return 0

    lax.fori_loop(0, width // step, image_back, 0)
    st_i[...] = to_rows(zero, jnp.sum(co_i[...], axis=1, keepdims=True))
    stats_send(1, st_i, sr_i)
    early = t_pieces // 2
    for p in range(early):
        text_go(p)
    sq_i, _ = stats_total(2, st_q, sr_q)
    scale_i = lax.rsqrt(sq_i / d_model + 1e-05)
    sc_i[...] = jnp.broadcast_to(scale_i, sc_i.shape)
    sq_t, inner_t = stats_total(0, st_t, sr_t)
    keep = jnp.concatenate([jnp.full((PATCH, 1), 1.0, F32) * (1.0 - filled(s)) for s in range(slots)], axis=0)
    scale_t = lax.rsqrt(sq_t / d_model + 1e-05)
    sc_t[...] = jnp.broadcast_to(scale_t * keep, sc_t.shape)
    co_t[...] = jnp.broadcast_to(scale_t * scale_t * scale_t * (inner_t / d_model) * keep, co_t.shape)
    total = level_end(1, i_own, i_l1, i_l2)
    kvb[...] = (total * sc_i[:, 0:1]).reshape(dp, rb, 2 * kvd).astype(BF16)
    r3[me_d] = kvb[me_d]

    def b1(k):
        return remote(kvb.at[dnext(k)], r3.at[me_d], b1_s.at[k], b1_r.at[k], (dnext(k), me))

    @pl.loop(1, dp)
    def _(k):
        b1(k).start()


    def text_back(j, _):
        cs = pl.ds(pl.multiple_of(j * step, step), step)
        d = sc_t[:, 0:1] * dt[:, cs] - text[:, cs].astype(F32) * co_t[:, 0:1]
        tg[:, cs] = d.astype(BF16)
        return 0

    lax.fori_loop(0, width // step, text_back, 0)
    _, inner_i = stats_total(1, st_i, sr_i)
    scale_i = sc_i[:, 0:1]
    co_i[...] = jnp.broadcast_to(scale_i * scale_i * scale_i * (inner_i / d_model), co_i.shape)

    def image_end(j, _):
        cs = pl.ds(pl.multiple_of(j * step, step), step)
        d = sc_i[:, 0:1] * dg[:, cs] - emb[:, cs].astype(F32) * co_i[:, 0:1]
        dimg[:, cs] = d.astype(BF16)
        return 0

    lax.fori_loop(0, width // step, image_end, 0)
    pieces = d_send.shape[0]
    span = dv // pieces

    def vis_chunk(j):
        d = nt(dimg[...], wp[j * span:(j + 1) * span, :]).reshape(ycount, 2, rows, span)
        for yi in range(ycount):
            a, b = d[yi, 0], d[yi, 1]
            first = core == 0
            d_own[j, yi] = jnp.where(first, a, b)
            d_send[j, yi] = jnp.where(first, b, a).astype(BF16)
        send(d_send.at[j], d_l1.at[j], dv_s.at[0, j, 0], dv_r.at[0, j, 0], (me_d, partner))

    def vis_two(j):
        arrived(d_l1.at[j], dv_s.at[0, j, 0], dv_r.at[0, j, 0])
        for k in range(1, ycount):
            yk = ynext(k)
            d_s2[j, k] = (d_own[j, yk] + d_l1[j, yk].astype(F32)).astype(BF16)
            send(d_s2.at[j, k], d_l2.at[j, k], dv_s.at[1, j, k], dv_r.at[1, j, k], (me_d, yk * 2 + core))

    def b2(k):
        return remote(s4.at[dnext(k)], r4.at[:, me_d], b2_s.at[k], b2_r.at[k], (dnext(k), me))

    for j in range(pieces):
        vis_chunk(j)
        if j > 0:
            vis_two(j - 1)
        if j == min(2, pieces - 1):

            @pl.loop(1, dp)
            def _(k):
                block = r3.at[dprev(k)]
                remote(block, block, b1_s.at[k], b1_r.at[k], (me_d, partner)).wait_recv()

            @pl.loop(0, dp)
            def _(d):
                for s in range(slots):
                    s4[d, s] = r3[owner_of(d * slots + s)]

            for s in range(slots):
                r4[s, me_d] = s4[me_d, s]

            @pl.loop(1, dp)
            def _(k):
                b2(k).start()

    vis_two(pieces - 1)
    for p in range(early, t_pieces):
        text_go(p)
    vf = vis[...].astype(F32)
    vscale = lax.rsqrt(jnp.mean(vf * vf, axis=1, keepdims=True) + 1e-06)
    hs = []
    for j in range(pieces):
        d = d_own[j, y] + d_l1[j, y].astype(F32)
        for k in range(1, ycount):
            arrived(d_l2.at[j, k], dv_s.at[1, j, k], dv_r.at[1, j, k])
            d = d + d_l2[j, k].astype(F32)
        hs.append(d.astype(BF16).astype(F32))
    h = jnp.concatenate(hs, axis=1) * gain_row(vgain)
    v_inner = jnp.mean(h * vf, axis=1, keepdims=True)
    vg_out[...] = (vscale * h - vf * vscale * vscale * vscale * v_inner).astype(BF16)

    @pl.loop(1, dp)
    def _(k):
        block = r4.at[:, dprev(k)]
        remote(block, block, b2_s.at[k], b2_r.at[k], (me_d, partner)).wait_recv()

    arrived(t_l1.at[y], rs_s.at[0, 0, 0], rs_r.at[0, 0, 0])
    for p in range(t_pieces):
        at = pl.ds(p * piece_rows, piece_rows)
        total = t_own[y, at, :] + t_l1[y, at, :].astype(F32)
        for k in range(1, ycount):
            text_piece(p, k).wait_recv()
            total = total + t_l2[k, at, :].astype(F32)
        s, half = p // 2, p % 2
        group = pl.ds(half * (dp // 2), dp // 2)
        placed = r4[s, group].astype(F32).reshape(piece_rows, 2 * kvd)
        out = total * sc_t[at, 0:1] + placed * filled(s)
        k_out[at, :] = out[:, :kvd].astype(BF16)
        v_out[at, :] = out[:, kvd:].astype(BF16)
    for copy in sends:
        copy.wait_send()

    @pl.loop(1, dp)
    def _(k):
        a1(k, 0).wait_send()
        a1(k, 1).wait_send()
        a2(k, 0).wait_send()
        a2(k, 1).wait_send()
        b1(k).wait_send()
        b2(k).wait_send()


def shards(vision, vision_gain, image_slot, text_embed, w_proj, llm_gain, w_key, w_value, key_grad, value_grad):
    dp = lax.axis_size("dp")
    mp = lax.axis_size("mp")
    tokens, width = text_embed.shape
    slots = tokens // PATCH
    rows, dv = vision.shape
    kvd = key_grad.shape[1]
    kv = kvd * mp
    img = rows * mp
    rb = PATCH // dp
    ys = mp // 2
    pieces = 5 if dv % 640 == 0 else 1
    span = dv // pieces
    V = pltpu.VMEM
    any_spec = pl.BlockSpec(memory_space=pl.ANY)
    vmem = pl.BlockSpec(memory_space=pltpu.VMEM)
    smem = pl.BlockSpec(memory_space=pltpu.SMEM)
    scratch = [
        V((rows, dv), BF16), V((mp, rows, dv), BF16), V((tokens, width), BF16), V((dv, width), BF16),
        V((width, kv), BF16), V((width, kv), BF16), V((tokens, width), BF16),
        V((tokens, kv), BF16), V((tokens, kv), BF16), V((img, kv), BF16), V((img, kv), BF16),
        V((img, width), BF16), V((img, width), BF16), V((img, width), BF16), V((img, width), F32),
    ]
    for n in (tokens, img):
        scratch += [
            V((ys, n, 2 * kvd), BF16), V((ys, n, 2 * kvd), F32), V((ys, n, 2 * kvd), BF16),
            V((ys, n, 2 * kvd), BF16), V((ys, n, 2 * kvd), BF16),
        ]
    scratch += [
        V((pieces, ys, rows, span), BF16), V((pieces, ys, rows, span), F32), V((pieces, ys, rows, span), BF16),
        V((pieces, ys, rows, span), BF16), V((pieces, ys, rows, span), BF16),
        V((8, tokens), F32), V((mp, 8, tokens), F32), V((8, img), F32), V((mp, 8, img), F32),
        V((8, img), F32), V((mp, 8, img), F32),
        V((tokens, 128), F32), V((tokens, 128), F32), V((img, 128), F32), V((img, 128), F32),
        V((dp * slots, rb, kvd), BF16), V((dp * slots, rb, kvd), BF16),
        V((dp, rb, kvd), BF16), V((dp, rb, kvd), BF16), V((dp, rb, kvd), BF16), V((dp, rb, kvd), BF16),
        V((dp, rb, 2 * kvd), BF16), V((dp, rb, 2 * kvd), BF16),
        V((dp, slots, rb, 2 * kvd), BF16), V((slots, dp, rb, 2 * kvd), BF16),
        DMA((9,)), DMA((5, 2, ys)), DMA((5, 2, ys)), DMA((2, 2, ys)), DMA((2, 2, ys)),
        DMA((ys, 2 * slots)), DMA((ys, 2 * slots)), DMA((3, mp)), DMA((3, mp)), DMA((2, pieces, ys)), DMA((2, pieces, ys)),
        DMA((2, dp)), DMA((2, dp)), DMA((2, dp)), DMA((2, dp)),
        DMA((dp,)), DMA((dp,)), DMA((dp,)), DMA((dp,)), V((tokens, width), F32),
    ]
    shapes = ((tokens, kvd), (tokens, kvd), (tokens, width), (rows, dv))
    room = sum(2 * a * b for a, b in shapes)
    lanes = 128 if dv % 128 == 0 else dv
    results = pl.pallas_call(
        functools.partial(kernel, dp, mp),
        out_shape=tuple(V(shape, BF16) for shape in shapes),
        in_specs=[smem, any_spec, vmem, any_spec, any_spec, vmem] + [any_spec] * 6,
        out_specs=(vmem,) * len(shapes),
        scratch_shapes=scratch,
        compiler_params=pltpu.CompilerParams(
            collective_id=0, has_side_effects=True, vmem_limit_bytes=67043328 - room
        ),
    )(
        image_slot, vision, vision_gain.reshape(-1, lanes), text_embed, w_proj, llm_gain[None, :],
        w_key, w_value, key_grad, value_grad,
        key_grad.reshape(slots, dp, rb, kvd), value_grad.reshape(slots, dp, rb, kvd),
    )
    return pl.pallas_call(
        write_out,
        out_shape=tuple(jax.ShapeDtypeStruct(shape, BF16) for shape in shapes),
        in_specs=[vmem] * len(shapes),
        out_specs=(any_spec,) * len(shapes),
        scratch_shapes=[DMA((len(shapes),))],
        compiler_params=pltpu.CompilerParams(vmem_limit_bytes=1 << 20),
    )(*results)


def solution(mesh):
    placed = (
        P(("dp", "mp"), None),
        P(),
        P(),
        P("dp", "mp"),
        P(None, "mp"),
        P("mp"),
        P("mp", None),
        P("mp", None),
        P("dp", "mp"),
        P("dp", "mp"),
    )
    return jax.shard_map(
        shards,
        mesh=mesh,
        in_specs=placed,
        out_specs=(P("dp", "mp"), P("dp", "mp"), P("dp", "mp"), P(("dp", "mp"), None)),
        check_vma=False,
    )
```

```python
import functools

import jax
import jax.numpy as jnp
from jax import lax
from jax.experimental import pallas as pl
from jax.experimental.pallas import tpu as pltpu
from jax.sharding import PartitionSpec as P

PATCH = 256
F32 = jnp.float32
BF16 = jnp.bfloat16
NT = (((1,), (1,)), ((), ()))
DMA = pltpu.SemaphoreType.DMA


def nt(a, b):
    return lax.dot_general(a, b, NT, preferred_element_type=F32)


def remote(src, dst, send_sem, recv_sem, device):
    return pltpu.make_async_remote_copy(
        src_ref=src, dst_ref=dst, send_sem=send_sem, recv_sem=recv_sem,
        device_id=device, device_id_type=pl.DeviceIdType.MESH,
    )


def to_rows(sq, inner):
    lane = lax.broadcasted_iota(jnp.int32, (sq.shape[0], 128), 1)
    wide = jnp.where(lane == 0, sq, jnp.where(lane == 1, inner, 0.0))
    return jnp.transpose(wide)[:8]


def to_columns(rows):
    wide = jnp.transpose(jnp.concatenate([rows] * 16, axis=0))
    return wide[:, 0:1], wide[:, 1:2]


def gain_row(ref):
    if ref.shape[0] == 1:
        return ref[...]
    return jnp.concatenate([ref[i:i + 1, :] for i in range(ref.shape[0])], axis=1)


def write_out(*refs):
    count = (len(refs) - 1) // 2
    copies = [pltpu.make_async_copy(refs[n], refs[count + n], refs[-1].at[n]) for n in range(count)]
    for copy in copies:
        copy.start()
    for copy in copies:
        copy.wait()


def kernel(
    dp, mp, slot_ref, vision_h, vgain, text_h, wp_h, gain, wk_h, wv_h, kg_h, vg_h, kg4, vg4,
    k_out, v_out, tg, vg_out,
    vis, vis_all, text, wp, wk, wv, xt, gk, gv, gik, giv, emb, xi, dimg, dg,
    t_send, t_own, t_l1, t_s2, t_l2, i_send, i_own, i_l1, i_s2, i_l2,
    d_send, d_own, d_l1, d_s2, d_l2,
    st_t, sr_t, st_i, sr_i, st_q, sr_q, sc_t, co_t, sc_i, co_i,
    kgs, vgs, kb_send, kb_y, kbr, tb_send, tb_recv, tb_sel, tb_y,
    r1k, r1v, s2k, s2v, r2k, r2v, kvb, r3, s4, r4,
    load_sem, ag_s, ag_r, rs_s, rs_r, t2_s, t2_r, st_s, st_r, dv_s, dv_r,
    a1_s, a1_r, a2_s, a2_r, b1_s, b1_r, b2_s, b2_r, kby_s, kby_r, kbz_s, kbz_r, kbp_s, kbp_r,
    tbz_s, tbz_r, tby_s, tby_r, dt,
):
    me_d = lax.axis_index("dp")
    me = lax.axis_index("mp")
    ycount = mp // 2
    core = lax.rem(me, 2)
    y = lax.div(me, 2)
    partner = y * 2 + (1 - core)
    slots, _, width = text.shape
    tokens = slots * PATCH
    kvd = gk.shape[1] // mp
    rows = vis.shape[0]
    dv = vis.shape[1]
    d_model = width * mp
    rb = r1k.shape[1]
    img_rows = mp * rows
    t_pieces = 2
    piece_rows = PATCH // t_pieces

    def ynext(k):
        return lax.rem(y + k, ycount)

    def yprev(k):
        return lax.rem(y + ycount - k, ycount)

    def dnext(k):
        return lax.rem(me_d + k, dp)

    def dprev(k):
        return lax.rem(me_d + dp - k, dp)

    def col(m):
        return pl.ds(pl.multiple_of(m * kvd, kvd), kvd)

    def owner_of(slot):
        found = jnp.int32(0)
        for i in range(dp):
            found = jnp.where(slot_ref[i] == slot, jnp.int32(i), found)
        return found

    def holds(s):
        found = jnp.int32(0)
        for i in range(dp):
            found = jnp.where(slot_ref[i] == me_d * slots + s, jnp.int32(1), found)
        return found

    first_holds, second_holds = holds(0), holds(1)
    turned = first_holds * (1 - second_holds)
    slot_at = (turned, 1 - turned)
    place_of = (turned, 1 - turned)
    filled = (first_holds.astype(F32), second_holds.astype(F32))
    keeps = (1.0 - filled[0] * filled[1], (1.0 - filled[0]) * (1.0 - filled[1]))

    def bare(d, found):
        used = jnp.int32(0)
        for i in range(dp):
            used = jnp.where(lax.div(slot_ref[i], jnp.int32(slots)) == d, jnp.int32(1), used)
        return jnp.where(used == 0, d, found)

    lone = lax.fori_loop(0, dp, bare, jnp.int32(0))
    lone_slot = lone * slots + 1
    at_lone = keeps[1]

    sends = []

    def send(*args):
        copy = remote(*args)
        copy.start()
        sends.append(copy)

    loads = [
        (vision_h, vis), (kg_h, kgs), (vg_h, vgs),
        (text_h, text), (wk_h, wk), (wv_h, wv), (wp_h, wp),
        (kg4.at[:, me_d], r1k.at[pl.ds(me_d * slots, slots)]),
        (vg4.at[:, me_d], r1v.at[pl.ds(me_d * slots, slots)]),
    ]
    loads = [pltpu.make_async_copy(a, b, load_sem.at[n]) for n, (a, b) in enumerate(loads)]
    for copy in loads:
        copy.start()

    barrier = pltpu.get_barrier_semaphore()

    @pl.loop(1, dp)
    def _(k):
        pl.semaphore_signal(barrier, inc=1, device_id=(dnext(k), me), device_id_type=pl.DeviceIdType.MESH)

    for k in range(1, mp):
        pl.semaphore_signal(
            barrier, inc=1, device_id=(me_d, lax.rem(me + k, mp)), device_id_type=pl.DeviceIdType.MESH
        )

    loads[0].wait()
    vf = vis[...].astype(F32)
    vscale = lax.rsqrt(jnp.mean(vf * vf, axis=1, keepdims=True) + 1e-06)
    vis_gain = gain_row(vgain)
    vis_all[me] = (vf * vscale * vis_gain).astype(BF16)
    pl.semaphore_wait(barrier, dp - 1 + mp - 1)

    def gather_start(g, block):
        for k in range(1, ycount):
            send(block(me), block(me), ag_s.at[g, 0, k], ag_r.at[g, 0, k], (me_d, ynext(k) * 2 + core))
        send(block(me), block(me), ag_s.at[g, 0, 0], ag_r.at[g, 0, 0], (me_d, partner))

    def arrived(block, send_sem, recv_sem):
        remote(block, block, send_sem, recv_sem, (me_d, partner)).wait_recv()

    def gather_relay(g, block):
        for k in range(1, ycount):
            got = block(yprev(k) * 2 + core)
            arrived(got, ag_s.at[g, 0, k], ag_r.at[g, 0, k])
            send(got, got, ag_s.at[g, 1, k], ag_r.at[g, 1, k], (me_d, partner))

    def gather_finish(g, block):
        arrived(block(partner), ag_s.at[g, 0, 0], ag_r.at[g, 0, 0])
        for k in range(1, ycount):
            arrived(block(yprev(k) * 2 + 1 - core), ag_s.at[g, 1, k], ag_r.at[g, 1, k])

    vis_block = lambda m: vis_all.at[m]
    gk_block = lambda m: gk.at[:, col(m)]
    gv_block = lambda m: gv.at[:, col(m)]
    gik_block = lambda m: gik.at[:, col(m)]
    giv_block = lambda m: giv.at[:, col(m)]

    gather_start(0, vis_block)

    mine = pl.ds(me_d * slots, slots)

    def a1(k, which):
        src, dst = ((kg4, r1k), (vg4, r1v))[which]
        return remote(
            src.at[:, dnext(k)], dst.at[mine], a1_s.at[which, k], a1_r.at[which, k], (dnext(k), me)
        )

    @pl.loop(1, dp)
    def _(k):
        a1(k, 0).start()
        a1(k, 1).start()

    loads[1].wait()
    loads[2].wait()
    for p in range(slots):
        gk[p * PATCH:(p + 1) * PATCH, col(me)] = kgs[slot_at[p]]
        gv[p * PATCH:(p + 1) * PATCH, col(me)] = vgs[slot_at[p]]
    first_rows = pl.ds(0, PATCH)
    later_rows = pl.ds(PATCH, PATCH)
    gka_block = lambda m: gk.at[first_rows, col(m)]
    gva_block = lambda m: gv.at[first_rows, col(m)]

    def pair_start(g, block, whole):
        for k in range(1, ycount):
            send(block(me), block(me), ag_s.at[g, 0, k], ag_r.at[g, 0, k], (me_d, ynext(k) * 2 + core))
        send(whole(me), whole(me), ag_s.at[g, 0, 0], ag_r.at[g, 0, 0], (me_d, partner))

    def near_finish(g, block):
        arrived(block(partner), ag_s.at[g, 0, 0], ag_r.at[g, 0, 0])

    def far_finish(g, block):
        for k in range(1, ycount):
            arrived(block(yprev(k) * 2 + 1 - core), ag_s.at[g, 1, k], ag_r.at[g, 1, k])

    def heads(yk):
        return pl.ds(pl.multiple_of(yk * 2 * kvd, 2 * kvd), 2 * kvd)

    def products(keys, values, at, cs, yk):
        at_heads = heads(yk)
        return nt(keys[at, at_heads], wk[cs, at_heads]) + nt(values[at, at_heads], wv[cs, at_heads])

    def far_products(keys, values, at, cs):
        total = products(keys, values, at, cs, ynext(1))
        for k in range(2, ycount):
            total = total + products(keys, values, at, cs, ynext(k))
        return total

    step = 256
    every = pl.ds(0, tokens)
    image_rows = pl.ds(0, img_rows)

    pair_start(1, gka_block, gk_block)
    pair_start(2, gva_block, gv_block)

    def chunk(x, m):
        k_part = jnp.dot(x[...], wk[:, col(m)], preferred_element_type=F32)
        v_part = jnp.dot(x[...], wv[:, col(m)], preferred_element_type=F32)
        return k_part, v_part

    def stage_send(x, n, psend, l1):
        for k in range(ycount):
            yk = ynext(k)
            k_part, v_part = chunk(x, yk * 2 + 1 - core)
            shape = psend.shape[1:-1] + (kvd,)
            psend[yk, ..., :kvd] = k_part.astype(BF16).reshape(shape)
            psend[yk, ..., kvd:] = v_part.astype(BF16).reshape(shape)
            send(psend.at[yk], l1.at[yk], rs_s.at[n, 0, k], rs_r.at[n, 0, k], (me_d, partner))

    def stage_own(x, own):
        for k in range(ycount):
            yk = ynext(k)
            k_part, v_part = chunk(x, yk * 2 + core)
            shape = own.shape[1:-1] + (kvd,)
            own[yk, ..., :kvd] = k_part.reshape(shape)
            own[yk, ..., kvd:] = v_part.reshape(shape)

    def level_two(n, own, l1, s2, l2):
        for k in range(ycount - 1, 0, -1):
            yk = ynext(k)
            arrived(l1.at[yk], rs_s.at[n, 0, k], rs_r.at[n, 0, k])
            s2[k] = (own[yk] + l1[yk].astype(F32)).astype(BF16)

    def level_go(n, s2, l2):
        for k in range(ycount - 1, 0, -1):
            send(s2.at[k], l2.at[k], rs_s.at[n, 1, k], rs_r.at[n, 1, k], (me_d, ynext(k) * 2 + core))

    def level_end(n, own, l1, l2):
        arrived(l1.at[y], rs_s.at[n, 0, 0], rs_r.at[n, 0, 0])
        total = own[y] + l1[y].astype(F32)
        for k in range(1, ycount):
            arrived(l2.at[k], rs_s.at[n, 1, k], rs_r.at[n, 1, k])
            total = total + l2[k].astype(F32)
        return total

    def text_piece(p, k):
        at = pl.ds(p * piece_rows, piece_rows)
        return remote(
            t_s2.at[k, at], t_l2.at[k, at], t2_s.at[k, p], t2_r.at[k, p], (me_d, ynext(k) * 2 + core)
        )

    def text_go(p):
        for k in range(ycount - 1, 0, -1):
            copy = text_piece(p, k)
            copy.start()
            sends.append(copy)

    def stats_send(n, st, sr):
        for k in range(1, mp):
            send(st, sr.at[k], st_s.at[n, k], st_r.at[n, k], (me_d, lax.rem(me + k, mp)))

    def stats_total(n, st, sr):
        total = st[...]
        for k in range(1, mp):
            arrived(sr.at[k], st_s.at[n, k], st_r.at[n, k])
            total = total + sr[k]
        return to_columns(total)

    def fold(p):
        total = p[:, :128]
        for n in range(1, p.shape[1] // 128):
            total = total + p[:, n * 128:(n + 1) * 128]
        return total

    loads[3].wait()
    for p in range(slots):
        tf = text[slot_at[p]].astype(F32)
        sc_t[p] = fold(tf * tf)
        xt[p * PATCH:(p + 1) * PATCH, :] = (tf * gain[...]).astype(BF16)
    loads[4].wait()
    loads[5].wait()
    stage_send(xt, 0, t_send, t_l1)
    stage_own(xt, t_own)
    for k in range(ycount - 1, 0, -1):
        yk = ynext(k)
        arrived(t_l1.at[yk], rs_s.at[0, 0, k], rs_r.at[0, 0, k])
        t_s2[k] = (t_own[yk, 0] + t_l1[yk, 0].astype(F32)).astype(BF16)
        rest = t_own[yk, 1] + t_l1[yk, 1].astype(F32)
        tb_send[:, k - 1] = rest.reshape(dp, rb, 2 * kvd).astype(BF16)
    tb_recv[me_d] = tb_send[me_d]
    near_finish(1, gk_block)
    near_finish(2, gv_block)

    def text_near(j, _):
        cs = pl.ds(pl.multiple_of(j * step, step), step)
        dt[:, :, cs] = products(gk, gv, every, cs, y).reshape(slots, PATCH, step)
        return 0

    lax.fori_loop(0, width // step, text_near, 0)
    co_t[...] = jnp.zeros(co_t.shape, F32)
    gather_relay(0, vis_block)
    loads[7].wait()
    loads[8].wait()

    @pl.loop(1, dp)
    def _(k):
        for which, dst in ((0, r1k), (1, r1v)):
            block = dst.at[pl.ds(dprev(k) * slots, slots)]
            remote(block, block, a1_s.at[which, k], a1_r.at[which, k], (me_d, partner)).wait_recv()

    @pl.loop(0, dp)
    def _(i):
        s2k[i] = r1k[slot_ref[i]]
        s2v[i] = r1v[slot_ref[i]]

    r2k[me_d] = s2k[me_d]
    r2v[me_d] = s2v[me_d]

    def a2(k, which):
        src, dst = ((s2k, r2k), (s2v, r2v))[which]
        return remote(
            src.at[dnext(k)], dst.at[me_d], a2_s.at[which, k], a2_r.at[which, k], (dnext(k), me)
        )

    @pl.loop(1, dp)
    def _(k):
        a2(k, 0).start()
        a2(k, 1).start()

    kb_send[0] = r1k[lone_slot]
    kb_send[1] = r1v[lone_slot]
    for k in range(1, ycount):
        send(kb_send, kb_y.at[k - 1], kby_s.at[k], kby_r.at[k], (me_d, ynext(k) * 2 + core))
    gather_finish(0, vis_block)
    loads[6].wait()

    sc_i[...] = jnp.zeros(sc_i.shape, F32)

    def project(j, _):
        cs = pl.ds(pl.multiple_of(j * step, step), step)
        e = jnp.concatenate([vis_all[m] for m in range(mp)], axis=0)
        e = jnp.dot(e, wp[:, cs], preferred_element_type=F32).astype(BF16)
        emb[:, cs] = e
        ef = e.astype(F32)
        xi[:, cs] = (ef * gain[:, cs]).astype(BF16)
        sc_i[...] += fold(ef * ef)
        return 0

    lax.fori_loop(0, width // step, project, 0)
    for k in range(1, ycount):
        arrived(kb_y.at[k - 1], kby_s.at[k], kby_r.at[k])
    kbr[me_d] = kb_y[...]

    def kbz(k):
        return remote(kb_y, kbr.at[me_d], kbz_s.at[k], kbz_r.at[k], (dnext(k), me))

    def tbz(k):
        return remote(tb_send.at[dnext(k)], tb_recv.at[me_d], tbz_s.at[k], tbz_r.at[k], (dnext(k), me))

    @pl.loop(1, dp)
    def _(k):
        kbz(k).start()

    @pl.loop(1, dp)
    def _(k):
        tbz(k).start()

    gather_relay(1, gka_block)
    gather_relay(2, gva_block)
    zero = jnp.zeros((img_rows, 1), F32)
    st_q[...] = to_rows(jnp.sum(sc_i[...], axis=1, keepdims=True), zero)
    stats_send(2, st_q, sr_q)
    stage_send(xi, 1, i_send, i_l1)

    @pl.loop(1, dp)
    def _(k):
        for which, dst in ((0, r2k), (1, r2v)):
            block = dst.at[dprev(k)]
            remote(block, block, a2_s.at[which, k], a2_r.at[which, k], (me_d, partner)).wait_recv()

    own_k = r2k[...].astype(F32).reshape(PATCH, kvd)
    own_v = r2v[...].astype(F32).reshape(PATCH, kvd)
    gik[:, col(me)] = own_k.astype(BF16)
    giv[:, col(me)] = own_v.astype(BF16)
    gather_start(3, gik_block)
    gather_start(4, giv_block)
    stage_own(xi, i_own)
    level_two(1, i_own, i_l1, i_s2, i_l2)
    level_go(1, i_s2, i_l2)
    far_finish(1, gka_block)
    far_finish(2, gva_block)

    def text_far(p):
        rows_p = pl.ds(p * PATCH, PATCH)

        def body(j, _):
            cs = pl.ds(pl.multiple_of(j * step, step), step)
            d = (dt[p, :, cs] + far_products(gk, gv, rows_p, cs)) * gain[:, cs]
            dt[p, :, cs] = d
            co_t[p] += fold(d * text[slot_at[p], :, cs].astype(F32))
            return 0

        lax.fori_loop(0, width // step, body, 0)

    text_far(0)
    near_finish(3, gik_block)
    near_finish(4, giv_block)

    def image_near(j, _):
        cs = pl.ds(pl.multiple_of(j * step, step), step)
        dg[:, cs] = products(gik, giv, image_rows, cs, y)
        return 0

    lax.fori_loop(0, width // step, image_near, 0)
    co_i[...] = jnp.zeros(co_i.shape, F32)

    @pl.loop(1, dp)
    def _(k):
        block = kbr.at[dprev(k)]
        remote(block, block, kbz_s.at[k], kbz_r.at[k], (me_d, partner)).wait_recv()

    for k in range(1, ycount):
        m = yprev(k) * 2 + core
        for which, g in ((0, gk), (1, gv)):
            g[later_rows, col(m)] = kbr[:, k - 1, which].astype(F32).reshape(PATCH, kvd).astype(BF16)
            send(
                g.at[later_rows, col(m)], g.at[later_rows, col(m)], kbp_s.at[which, k], kbp_r.at[which, k],
                (me_d, partner),
            )
    gather_relay(3, gik_block)
    gather_relay(4, giv_block)
    for k in range(1, ycount):
        for which, g in ((0, gk), (1, gv)):
            arrived(g.at[later_rows, col(yprev(k) * 2 + 1 - core)], kbp_s.at[which, k], kbp_r.at[which, k])
    text_far(1)
    st_t[...] = to_rows(
        jnp.sum(sc_t[...].reshape(tokens, 128), axis=1, keepdims=True),
        jnp.sum(co_t[...].reshape(tokens, 128), axis=1, keepdims=True),
    )
    stats_send(0, st_t, sr_t)
    far_finish(3, gik_block)
    far_finish(4, giv_block)

    def image_far(j, _):
        cs = pl.ds(pl.multiple_of(j * step, step), step)
        d = (dg[:, cs] + far_products(gik, giv, image_rows, cs)) * gain[:, cs]
        dg[:, cs] = d
        co_i[...] += fold(d * emb[:, cs].astype(F32))
        return 0

    lax.fori_loop(0, width // step, image_far, 0)
    st_i[...] = to_rows(zero, jnp.sum(co_i[...], axis=1, keepdims=True))
    stats_send(1, st_i, sr_i)

    @pl.loop(1, dp)
    def _(k):
        block = tb_recv.at[dprev(k)]
        remote(block, block, tbz_s.at[k], tbz_r.at[k], (me_d, partner)).wait_recv()

    tb_sel[...] = tb_recv[lone]
    for k in range(1, ycount):
        send(tb_sel.at[k - 1], tb_y.at[k - 1], tby_s.at[k], tby_r.at[k], (me_d, ynext(k) * 2 + core))
    for p in range(t_pieces):
        text_go(p)
    sq_i, _ = stats_total(2, st_q, sr_q)
    scale_i = lax.rsqrt(sq_i / d_model + 1e-05)
    sc_i[...] = jnp.broadcast_to(scale_i, sc_i.shape)
    total = level_end(1, i_own, i_l1, i_l2)
    kvb[...] = (total * sc_i[:, 0:1]).reshape(dp, rb, 2 * kvd).astype(BF16)
    r3[me_d] = kvb[me_d]

    def b1(k):
        return remote(kvb.at[dnext(k)], r3.at[me_d], b1_s.at[k], b1_r.at[k], (dnext(k), me))

    @pl.loop(1, dp)
    def _(k):
        b1(k).start()

    sq_t, inner_t = stats_total(0, st_t, sr_t)
    keep = jnp.concatenate([jnp.full((PATCH, 1), 1.0, F32) * keeps[p] for p in range(slots)], axis=0)
    scale_t = lax.rsqrt(sq_t / d_model + 1e-05)
    sc_t[...] = jnp.broadcast_to(scale_t * keep, (tokens, 128)).reshape(sc_t.shape)
    co_t[...] = jnp.broadcast_to(
        scale_t * scale_t * scale_t * (inner_t / d_model) * keep, (tokens, 128)
    ).reshape(co_t.shape)

    def text_back(j, _):
        cs = pl.ds(pl.multiple_of(j * step, step), step)
        for s in range(slots):
            at = place_of[s]
            d = sc_t[at][:, 0:1] * dt[at, :, cs] - text[s, :, cs].astype(F32) * co_t[at][:, 0:1]
            tg[s * PATCH:(s + 1) * PATCH, cs] = d.astype(BF16)
        return 0

    lax.fori_loop(0, width // step, text_back, 0)
    _, inner_i = stats_total(1, st_i, sr_i)
    scale_i = sc_i[:, 0:1]
    co_i[...] = jnp.broadcast_to(scale_i * scale_i * scale_i * (inner_i / d_model), co_i.shape)

    def image_end(j, _):
        cs = pl.ds(pl.multiple_of(j * step, step), step)
        d = sc_i[:, 0:1] * dg[:, cs] - emb[:, cs].astype(F32) * co_i[:, 0:1]
        dimg[:, cs] = d.astype(BF16)
        return 0

    lax.fori_loop(0, width // step, image_end, 0)
    pieces = d_send.shape[0]
    span = dv // pieces

    def vis_chunk(j):
        d = nt(dimg[...], wp[j * span:(j + 1) * span, :]).reshape(ycount, 2, rows, span)
        for yi in range(ycount):
            a, b = d[yi, 0], d[yi, 1]
            first = core == 0
            d_own[j, yi] = jnp.where(first, a, b)
            d_send[j, yi] = jnp.where(first, b, a).astype(BF16)
        send(d_send.at[j], d_l1.at[j], dv_s.at[0, j, 0], dv_r.at[0, j, 0], (me_d, partner))

    def vis_two(j):
        arrived(d_l1.at[j], dv_s.at[0, j, 0], dv_r.at[0, j, 0])
        for k in range(1, ycount):
            yk = ynext(k)
            d_s2[j, k] = (d_own[j, yk] + d_l1[j, yk].astype(F32)).astype(BF16)
            send(d_s2.at[j, k], d_l2.at[j, k], dv_s.at[1, j, k], dv_r.at[1, j, k], (me_d, yk * 2 + core))

    def b2(k):
        return remote(s4.at[dnext(k)], r4.at[:, me_d], b2_s.at[k], b2_r.at[k], (dnext(k), me))

    for j in range(pieces):
        vis_chunk(j)
        if j > 0:
            vis_two(j - 1)
        if j == min(2, pieces - 1):

            @pl.loop(1, dp)
            def _(k):
                block = r3.at[dprev(k)]
                remote(block, block, b1_s.at[k], b1_r.at[k], (me_d, partner)).wait_recv()

            extra = jnp.zeros((rb, 2 * kvd), F32)
            for k in range(1, ycount):
                arrived(tb_y.at[k - 1], tby_s.at[k], tby_r.at[k])
                extra = extra + tb_y[k - 1].astype(F32)
            r3[dp] = extra.astype(BF16)

            @pl.loop(0, dp)
            def _(d):
                for s in range(slots):
                    slot = d * slots + s
                    s4[d, s] = r3[jnp.where(slot == lone_slot, jnp.int32(dp), owner_of(slot))]

            for s in range(slots):
                r4[s, me_d] = s4[me_d, s]

            @pl.loop(1, dp)
            def _(k):
                b2(k).start()

    vis_two(pieces - 1)
    vf = vis[...].astype(F32)
    vscale = lax.rsqrt(jnp.mean(vf * vf, axis=1, keepdims=True) + 1e-06)
    hs = []
    for j in range(pieces):
        d = d_own[j, y] + d_l1[j, y].astype(F32)
        for k in range(1, ycount):
            arrived(d_l2.at[j, k], dv_s.at[1, j, k], dv_r.at[1, j, k])
            d = d + d_l2[j, k].astype(F32)
        hs.append(d.astype(BF16).astype(F32))
    h = jnp.concatenate(hs, axis=1) * gain_row(vgain)
    v_inner = jnp.mean(h * vf, axis=1, keepdims=True)
    vg_out[...] = (vscale * h - vf * vscale * vscale * vscale * v_inner).astype(BF16)

    @pl.loop(1, dp)
    def _(k):
        block = r4.at[:, dprev(k)]
        remote(block, block, b2_s.at[k], b2_r.at[k], (me_d, partner)).wait_recv()

    arrived(t_l1.at[y], rs_s.at[0, 0, 0], rs_r.at[0, 0, 0])
    for p in range(t_pieces):
        for k in range(1, ycount):
            text_piece(p, k).wait_recv()
    direct = t_l2[1].astype(F32)
    for k in range(2, ycount):
        direct = direct + t_l2[k].astype(F32)
    for s in range(slots):
        at = place_of[s]
        is_first = 1.0 - at.astype(F32)
        placed = r4[s].astype(F32).reshape(PATCH, 2 * kvd)
        total = t_own[y, at] + t_l1[y, at].astype(F32) + direct * is_first + placed * ((1.0 - is_first) * at_lone)
        out = total * sc_t[at][:, 0:1] + placed * filled[s]
        rows_s = pl.ds(s * PATCH, PATCH)
        k_out[rows_s, :] = out[:, :kvd].astype(BF16)
        v_out[rows_s, :] = out[:, kvd:].astype(BF16)
    for copy in sends:
        copy.wait_send()

    @pl.loop(1, dp)
    def _(k):
        a1(k, 0).wait_send()
        a1(k, 1).wait_send()
        a2(k, 0).wait_send()
        a2(k, 1).wait_send()
        b1(k).wait_send()
        kbz(k).wait_send()
        tbz(k).wait_send()
        b2(k).wait_send()


def shards(vision, vision_gain, image_slot, text_embed, w_proj, llm_gain, w_key, w_value, key_grad, value_grad):
    dp = lax.axis_size("dp")
    mp = lax.axis_size("mp")
    tokens, width = text_embed.shape
    slots = tokens // PATCH
    rows, dv = vision.shape
    kvd = key_grad.shape[1]
    kv = kvd * mp
    img = rows * mp
    rb = PATCH // dp
    ys = mp // 2
    pieces = 5 if dv % 640 == 0 else 1
    span = dv // pieces
    V = pltpu.VMEM
    any_spec = pl.BlockSpec(memory_space=pl.ANY)
    vmem = pl.BlockSpec(memory_space=pltpu.VMEM)
    smem = pl.BlockSpec(memory_space=pltpu.SMEM)
    scratch = [
        V((rows, dv), BF16), V((mp, rows, dv), BF16), V((slots, PATCH, width), BF16), V((dv, width), BF16),
        V((width, kv), BF16), V((width, kv), BF16), V((tokens, width), BF16),
        V((tokens, kv), BF16), V((tokens, kv), BF16), V((img, kv), BF16), V((img, kv), BF16),
        V((img, width), BF16), V((img, width), BF16), V((img, width), BF16), V((img, width), F32),
    ]
    t_shape = (ys, slots, PATCH, 2 * kvd)
    i_shape = (ys, img, 2 * kvd)
    half = (ys, PATCH, 2 * kvd)
    scratch += [V(t_shape, BF16), V(t_shape, F32), V(t_shape, BF16), V(half, BF16), V(half, BF16)]
    scratch += [V(i_shape, BF16), V(i_shape, F32), V(i_shape, BF16), V(i_shape, BF16), V(i_shape, BF16)]
    scratch += [
        V((pieces, ys, rows, span), BF16), V((pieces, ys, rows, span), F32), V((pieces, ys, rows, span), BF16),
        V((pieces, ys, rows, span), BF16), V((pieces, ys, rows, span), BF16),
        V((8, tokens), F32), V((mp, 8, tokens), F32), V((8, img), F32), V((mp, 8, img), F32),
        V((8, img), F32), V((mp, 8, img), F32),
        V((slots, PATCH, 128), F32), V((slots, PATCH, 128), F32), V((img, 128), F32), V((img, 128), F32),
        V((slots, PATCH, kvd), BF16), V((slots, PATCH, kvd), BF16),
        V((2, rb, kvd), BF16), V((ys - 1, 2, rb, kvd), BF16), V((dp, ys - 1, 2, rb, kvd), BF16),
        V((dp, ys - 1, rb, 2 * kvd), BF16), V((dp, ys - 1, rb, 2 * kvd), BF16),
        V((ys - 1, rb, 2 * kvd), BF16), V((ys - 1, rb, 2 * kvd), BF16),
        V((dp * slots, rb, kvd), BF16), V((dp * slots, rb, kvd), BF16),
        V((dp, rb, kvd), BF16), V((dp, rb, kvd), BF16), V((dp, rb, kvd), BF16), V((dp, rb, kvd), BF16),
        V((dp, rb, 2 * kvd), BF16), V((dp + 1, rb, 2 * kvd), BF16),
        V((dp, slots, rb, 2 * kvd), BF16), V((slots, dp, rb, 2 * kvd), BF16),
        DMA((9,)), DMA((5, 2, ys)), DMA((5, 2, ys)), DMA((2, 2, ys)), DMA((2, 2, ys)),
        DMA((ys, 2)), DMA((ys, 2)), DMA((3, mp)), DMA((3, mp)), DMA((2, pieces, ys)), DMA((2, pieces, ys)),
        DMA((2, dp)), DMA((2, dp)), DMA((2, dp)), DMA((2, dp)),
        DMA((dp,)), DMA((dp,)), DMA((dp,)), DMA((dp,)),
        DMA((ys,)), DMA((ys,)), DMA((dp,)), DMA((dp,)), DMA((2, ys)), DMA((2, ys)),
        DMA((dp,)), DMA((dp,)), DMA((ys,)), DMA((ys,)), V((slots, PATCH, width), F32),
    ]
    shapes = ((tokens, kvd), (tokens, kvd), (tokens, width), (rows, dv))
    room = sum(2 * a * b for a, b in shapes)
    lanes = 128 if dv % 128 == 0 else dv
    results = pl.pallas_call(
        functools.partial(kernel, dp, mp),
        out_shape=tuple(V(shape, BF16) for shape in shapes),
        in_specs=[smem, any_spec, vmem, any_spec, any_spec, vmem] + [any_spec] * 6,
        out_specs=(vmem,) * len(shapes),
        scratch_shapes=scratch,
        compiler_params=pltpu.CompilerParams(
            collective_id=0, has_side_effects=True, vmem_limit_bytes=67043328 - room
        ),
    )(
        image_slot, vision, vision_gain.reshape(-1, lanes), text_embed.reshape(slots, PATCH, width), w_proj,
        llm_gain[None, :], w_key, w_value, key_grad.reshape(slots, PATCH, kvd), value_grad.reshape(slots, PATCH, kvd),
        key_grad.reshape(slots, dp, rb, kvd), value_grad.reshape(slots, dp, rb, kvd),
    )
    return pl.pallas_call(
        write_out,
        out_shape=tuple(jax.ShapeDtypeStruct(shape, BF16) for shape in shapes),
        in_specs=[vmem] * len(shapes),
        out_specs=(any_spec,) * len(shapes),
        scratch_shapes=[DMA((len(shapes),))],
        compiler_params=pltpu.CompilerParams(vmem_limit_bytes=1 << 20),
    )(*results)


def solution(mesh):
    placed = (
        P(("dp", "mp"), None),
        P(),
        P(),
        P("dp", "mp"),
        P(None, "mp"),
        P("mp"),
        P("mp", None),
        P("mp", None),
        P("dp", "mp"),
        P("dp", "mp"),
    )
    return jax.shard_map(
        shards,
        mesh=mesh,
        in_specs=placed,
        out_specs=(P("dp", "mp"), P("dp", "mp"), P("dp", "mp"), P(("dp", "mp"), None)),
        check_vma=False,
    )
```

```python
import functools

import jax
import jax.numpy as jnp
from jax import lax
from jax.experimental import pallas as pl
from jax.experimental.pallas import tpu as pltpu
from jax.sharding import PartitionSpec as P

PATCH = 256
F32 = jnp.float32
BF16 = jnp.bfloat16
NT = (((1,), (1,)), ((), ()))
DMA = pltpu.SemaphoreType.DMA


def nt(a, b):
    return lax.dot_general(a, b, NT, preferred_element_type=F32)


def remote(src, dst, send_sem, recv_sem, device):
    return pltpu.make_async_remote_copy(
        src_ref=src, dst_ref=dst, send_sem=send_sem, recv_sem=recv_sem,
        device_id=device, device_id_type=pl.DeviceIdType.MESH,
    )


def to_rows(sq, inner):
    lane = lax.broadcasted_iota(jnp.int32, (sq.shape[0], 128), 1)
    wide = jnp.where(lane == 0, sq, jnp.where(lane == 1, inner, 0.0))
    return jnp.transpose(wide)[:8]


def to_columns(rows):
    wide = jnp.transpose(jnp.concatenate([rows] * 16, axis=0))
    return wide[:, 0:1], wide[:, 1:2]


def gain_row(ref):
    if ref.shape[0] == 1:
        return ref[...]
    return jnp.concatenate([ref[i:i + 1, :] for i in range(ref.shape[0])], axis=1)


def vis_cuts(dv):
    if dv % 128:
        return (0, dv)
    units = dv // 128
    first = max(units // 12, 1)
    cuts = [0, first]
    while cuts[-1] < units:
        cuts.append(min(cuts[-1] + max(units // 5, 1), units))
    return tuple(128 * c for c in cuts)


def write_out(*refs):
    count = (len(refs) - 1) // 2
    copies = [pltpu.make_async_copy(refs[n], refs[count + n], refs[-1].at[n]) for n in range(count)]
    for copy in copies:
        copy.start()
    for copy in copies:
        copy.wait()


def kernel(
    dp, mp, slot_ref, vision_h, vgain, text_h, wp_h, gain, wk_h, wv_h, kg_h, vg_h, kg4, vg4,
    k_out, v_out, tg, vg_out,
    vis, vis_all, text, wp, wk, wv, xt, gk, gv, gik, giv, emb, xi, dimg, dg,
    t_send, t_own, t_l1, t_s2, t_l2, i_send, i_own, i_l1, i_s2, i_l2,
    d_send, d_own, d_l1, d_s2, d_l2,
    st_t, sr_t, st_i, sr_i, st_q, sr_q, sc_t, co_t, sc_i, co_i,
    kgs, vgs, kb_send, kb_y, kbr, tb_send, tb_recv, tb_sel, tb_y,
    r1k, r1v, s2k, s2v, r2k, r2v, kvb, r3, s4, s5, r4,
    load_sem, ag_s, ag_r, rs_s, rs_r, rs1_r, t2_r, st_s, st_r, dv_s, dv_r,
    a1_s, a1_r, a2_s, a2_r, b1_s, b1_r, b2_s, b2_r, b3_s, b3_r, kby_s, kby_r, kbz_s, kbz_r, kbp_s, kbp_r,
    tbz_s, tbz_r, tby_s, tby_r, dt,
):
    me_d = lax.axis_index("dp")
    me = lax.axis_index("mp")
    ycount = mp // 2
    core = lax.rem(me, 2)
    y = lax.div(me, 2)
    partner = y * 2 + (1 - core)
    slots, _, width = text.shape
    tokens = slots * PATCH
    kvd = gk.shape[1] // mp
    rows = vis.shape[0]
    dv = vis.shape[1]
    d_model = width * mp
    rb = r1k.shape[1]
    img_rows = mp * rows
    t_pieces = 2
    piece_rows = PATCH // t_pieces

    def ynext(k):
        return lax.rem(y + k, ycount)

    def yprev(k):
        return lax.rem(y + ycount - k, ycount)

    def dnext(k):
        return lax.rem(me_d + k, dp)

    def dprev(k):
        return lax.rem(me_d + dp - k, dp)

    def col(m):
        return pl.ds(pl.multiple_of(m * kvd, kvd), kvd)

    def is_filled(slot):
        found = jnp.int32(0)
        for i in range(dp):
            found = jnp.where(slot_ref[i] == slot, jnp.int32(1), found)
        return found

    def owner_of(slot):
        found = jnp.int32(0)
        for i in range(dp):
            found = jnp.where(slot_ref[i] == slot, jnp.int32(i), found)
        return found

    def holds(s):
        return is_filled(me_d * slots + s)

    first_holds, second_holds = holds(0), holds(1)
    turned = first_holds * (1 - second_holds)
    slot_at = (turned, 1 - turned)
    place_of = (turned, 1 - turned)
    filled = (first_holds.astype(F32), second_holds.astype(F32))
    keeps = (1.0 - filled[0] * filled[1], (1.0 - filled[0]) * (1.0 - filled[1]))

    def survey(d, found):
        count = jnp.int32(0)
        for i in range(dp):
            count = count + jnp.where(lax.div(slot_ref[i], jnp.int32(slots)) == d, jnp.int32(1), jnp.int32(0))
        return jnp.where(count == 0, d, found[0]), jnp.where(count > 1, d, found[1])

    lone, crowded = lax.fori_loop(0, dp, survey, (jnp.int32(0), jnp.int32(0)))
    lone_slot = lone * slots + 1
    at_lone = keeps[1]
    inner = 2
    outer = dp // inner
    my_inner = lax.rem(me_d, inner)
    my_outer = lax.div(me_d, inner)

    sends = []

    def send(*args):
        copy = remote(*args)
        copy.start()
        sends.append(copy)

    def start(*args):
        remote(*args).start()

    loads = [
        (vision_h, vis), (kg_h, kgs), (vg_h, vgs),
        (text_h, text), (wk_h, wk), (wv_h, wv), (wp_h, wp),
        (kg4.at[:, me_d], r1k.at[pl.ds(me_d * slots, slots)]),
        (vg4.at[:, me_d], r1v.at[pl.ds(me_d * slots, slots)]),
    ]
    loads = [pltpu.make_async_copy(a, b, load_sem.at[n]) for n, (a, b) in enumerate(loads)]
    for copy in loads:
        copy.start()

    barrier = pltpu.get_barrier_semaphore()

    @pl.loop(1, dp)
    def _(k):
        pl.semaphore_signal(barrier, inc=1, device_id=(dnext(k), me), device_id_type=pl.DeviceIdType.MESH)

    for k in range(1, mp):
        pl.semaphore_signal(
            barrier, inc=1, device_id=(me_d, lax.rem(me + k, mp)), device_id_type=pl.DeviceIdType.MESH
        )

    loads[0].wait()
    vf = vis[...].astype(F32)
    vscale = lax.rsqrt(jnp.mean(vf * vf, axis=1, keepdims=True) + 1e-06)
    vis_gain = gain_row(vgain)
    vis_all[me] = (vf * vscale * vis_gain).astype(BF16)
    pl.semaphore_wait(barrier, dp - 1 + mp - 1)
    mine = pl.ds(me_d * slots, slots)
    others = pl.ds(0, dp - 1)

    def a1(k, which):
        src, dst = ((kg4, r1k), (vg4, r1v))[which]
        return remote(
            src.at[:, dnext(k)], dst.at[mine], a1_s.at[which], a1_r.at[which], (dnext(k), me)
        )

    @pl.loop(1, dp)
    def _(k):
        a1(k, 0).start()
        a1(k, 1).start()


    def gather_start(g, block):
        for k in range(1, ycount):
            send(block(me), block(me), ag_s.at[g, k], ag_r.at[g, k], (me_d, ynext(k) * 2 + core))
        send(block(me), block(me), ag_s.at[g, 0], ag_r.at[g, 0], (me_d, partner))

    def arrived(block, send_sem, recv_sem):
        remote(block, block, send_sem, recv_sem, (me_d, partner)).wait_recv()

    def gather_relay(g, block):
        for k in range(1, ycount):
            got = block(yprev(k) * 2 + core)
            arrived(got, ag_s.at[g, k], ag_r.at[g, k])
            send(got, got, ag_s.at[g, ycount + k - 1], ag_r.at[g, ycount + k - 1], (me_d, partner))

    def gather_finish(g, block):
        arrived(block(partner), ag_s.at[g, 0], ag_r.at[g, 0])
        for k in range(1, ycount):
            arrived(block(yprev(k) * 2 + 1 - core), ag_s.at[g, ycount + k - 1], ag_r.at[g, ycount + k - 1])

    vis_block = lambda m: vis_all.at[m]
    gk_block = lambda m: gk.at[:, col(m)]
    gv_block = lambda m: gv.at[:, col(m)]
    gik_block = lambda m: gik.at[:, col(m)]
    giv_block = lambda m: giv.at[:, col(m)]

    gather_start(0, vis_block)

    loads[1].wait()
    loads[2].wait()
    for p in range(slots):
        gk[p * PATCH:(p + 1) * PATCH, col(me)] = kgs[slot_at[p]]
        gv[p * PATCH:(p + 1) * PATCH, col(me)] = vgs[slot_at[p]]
    first_rows = pl.ds(0, PATCH)
    later_rows = pl.ds(PATCH, PATCH)
    gka_block = lambda m: gk.at[first_rows, col(m)]
    gva_block = lambda m: gv.at[first_rows, col(m)]

    def pair_start(g, block, whole):
        for k in range(1, ycount):
            send(block(me), block(me), ag_s.at[g, k], ag_r.at[g, k], (me_d, ynext(k) * 2 + core))
        send(whole(me), whole(me), ag_s.at[g, 0], ag_r.at[g, 0], (me_d, partner))

    def near_finish(g, block):
        arrived(block(partner), ag_s.at[g, 0], ag_r.at[g, 0])

    def far_finish(g, block):
        for k in range(1, ycount):
            arrived(block(yprev(k) * 2 + 1 - core), ag_s.at[g, ycount + k - 1], ag_r.at[g, ycount + k - 1])

    def heads(yk):
        return pl.ds(pl.multiple_of(yk * 2 * kvd, 2 * kvd), 2 * kvd)

    def products(keys, values, at, cs, yk):
        at_heads = heads(yk)
        return nt(keys[at, at_heads], wk[cs, at_heads]) + nt(values[at, at_heads], wv[cs, at_heads])

    def far_products(keys, values, at, cs):
        total = products(keys, values, at, cs, ynext(1))
        for k in range(2, ycount):
            total = total + products(keys, values, at, cs, ynext(k))
        return total

    step = 256
    every = pl.ds(0, tokens)
    image_rows = pl.ds(0, img_rows)

    pair_start(1, gka_block, gk_block)
    pair_start(2, gva_block, gv_block)

    def chunk(x, m):
        k_part = jnp.dot(x[...], wk[:, col(m)], preferred_element_type=F32)
        v_part = jnp.dot(x[...], wv[:, col(m)], preferred_element_type=F32)
        return k_part, v_part

    def stage_send(x, n, psend, l1):
        for k in range(ycount):
            yk = ynext(k)
            k_part, v_part = chunk(x, yk * 2 + 1 - core)
            shape = psend.shape[1:-1] + (kvd,)
            psend[yk, ..., :kvd] = k_part.astype(BF16).reshape(shape)
            psend[yk, ..., kvd:] = v_part.astype(BF16).reshape(shape)
            start(psend.at[yk], l1.at[yk], rs_s.at[n, 0], rs_r.at[n, k], (me_d, partner))

    def stage_own(x, own):
        for k in range(ycount):
            yk = ynext(k)
            k_part, v_part = chunk(x, yk * 2 + core)
            shape = own.shape[1:-1] + (kvd,)
            own[yk, ..., :kvd] = k_part.reshape(shape)
            own[yk, ..., kvd:] = v_part.reshape(shape)

    def level_two(n, own, l1, s2, l2):
        for k in range(ycount - 1, 0, -1):
            yk = ynext(k)
            arrived(l1.at[yk], rs_s.at[n, 0], rs_r.at[n, k])
            s2[k] = (own[yk] + l1[yk].astype(F32)).astype(BF16)

    def level_go(n, s2, l2):
        for k in range(ycount - 1, 0, -1):
            start(s2.at[k], l2.at[k], rs_s.at[n, k], rs1_r.at[k - 1], (me_d, ynext(k) * 2 + core))

    def level_end(n, own, l1, l2):
        arrived(l1.at[y], rs_s.at[n, 0], rs_r.at[n, 0])
        total = own[y] + l1[y].astype(F32)
        for k in range(1, ycount):
            arrived(l2.at[k], rs_s.at[n, k], rs1_r.at[k - 1])
            total = total + l2[k].astype(F32)
        return total

    def text_piece(p, k):
        at = pl.ds(p * piece_rows, piece_rows)
        return remote(
            t_s2.at[k, at], t_l2.at[k, at], rs_s.at[0, k], t2_r.at[k - 1, p], (me_d, ynext(k) * 2 + core)
        )

    def text_go(p):
        for k in range(ycount - 1, 0, -1):
            text_piece(p, k).start()

    def stats_send(n, st, sr):
        for k in range(1, mp):
            start(st, sr.at[k], st_s.at[n], st_r.at[n], (me_d, lax.rem(me + k, mp)))

    def stats_total(n, st, sr):
        total = st[...]
        arrived(sr.at[pl.ds(1, mp - 1)], st_s.at[n], st_r.at[n])
        for k in range(1, mp):
            total = total + sr[k]
        return to_columns(total)

    def wide(p):
        return jnp.concatenate([p] * (step // 128), axis=1)

    def fold(p):
        total = p[:, :128]
        for n in range(1, p.shape[1] // 128):
            total = total + p[:, n * 128:(n + 1) * 128]
        return total

    loads[3].wait()
    for p in range(slots):
        tf = text[slot_at[p]].astype(F32)
        sc_t[p] = fold(tf * tf)
        xt[p * PATCH:(p + 1) * PATCH, :] = (tf * gain[...]).astype(BF16)
    loads[4].wait()
    loads[5].wait()
    stage_send(xt, 0, t_send, t_l1)
    stage_own(xt, t_own)
    for k in range(ycount - 1, 0, -1):
        yk = ynext(k)
        arrived(t_l1.at[yk], rs_s.at[0, 0], rs_r.at[0, k])
        t_s2[k] = (t_own[yk, 0] + t_l1[yk, 0].astype(F32)).astype(BF16)
        rest = t_own[yk, 1] + t_l1[yk, 1].astype(F32)
        tb_send[:, k - 1] = rest.reshape(dp, rb, 2 * kvd).astype(BF16)
    tb_recv[me_d] = tb_send[me_d]
    near_finish(1, gk_block)
    near_finish(2, gv_block)

    def text_near(j, _):
        cs = pl.ds(pl.multiple_of(j * step, step), step)
        dt[:, :, cs] = products(gk, gv, every, cs, y).reshape(slots, PATCH, step)
        return 0

    lax.fori_loop(0, width // step, text_near, 0)
    co_t[...] = jnp.zeros(co_t.shape, F32)
    gather_relay(0, vis_block)
    loads[7].wait()
    loads[8].wait()

    for which, dst in ((0, r1k), (1, r1v)):
        arrived(dst.at[pl.ds(0, (dp - 1) * slots)], a1_s.at[which], a1_r.at[which])

    @pl.loop(0, dp)
    def _(i):
        s2k[i] = r1k[slot_ref[i]]
        s2v[i] = r1v[slot_ref[i]]

    r2k[me_d] = s2k[me_d]
    r2v[me_d] = s2v[me_d]

    def a2(k, which):
        src, dst = ((s2k, r2k), (s2v, r2v))[which]
        return remote(
            src.at[dnext(k)], dst.at[me_d], a2_s.at[which], a2_r.at[which], (dnext(k), me)
        )

    @pl.loop(1, dp)
    def _(k):
        a2(k, 0).start()
        a2(k, 1).start()

    kb_send[0] = r1k[lone_slot]
    kb_send[1] = r1v[lone_slot]
    for k in range(1, ycount):
        send(kb_send, kb_y.at[k - 1], kby_s.at[k - 1], kby_r.at[k - 1], (me_d, ynext(k) * 2 + core))
    text_go(0)
    gather_finish(0, vis_block)
    loads[6].wait()

    sc_i[...] = jnp.zeros(sc_i.shape, F32)

    def project(j, _):
        cs = pl.ds(pl.multiple_of(j * step, step), step)
        e = jnp.concatenate([vis_all[m] for m in range(mp)], axis=0)
        e = jnp.dot(e, wp[:, cs], preferred_element_type=F32).astype(BF16)
        emb[:, cs] = e
        ef = e.astype(F32)
        xi[:, cs] = (ef * gain[:, cs]).astype(BF16)
        sc_i[...] += fold(ef * ef)
        return 0

    lax.fori_loop(0, width // step, project, 0)
    for k in range(1, ycount):
        arrived(kb_y.at[k - 1], kby_s.at[k - 1], kby_r.at[k - 1])
    kbr[me_d] = kb_y[...]

    def kbz(k):
        return remote(kb_y, kbr.at[me_d], kbz_s.at[0], kbz_r.at[0], (dnext(k), me))

    def tbz(k):
        return remote(tb_send.at[dnext(k)], tb_recv.at[me_d], tbz_s.at[0], tbz_r.at[0], (dnext(k), me))

    @pl.loop(1, dp)
    def _(k):
        kbz(k).start()

    @pl.loop(1, dp)
    def _(k):
        tbz(k).start()

    gather_relay(1, gka_block)
    gather_relay(2, gva_block)
    zero = jnp.zeros((img_rows, 1), F32)
    st_q[...] = to_rows(jnp.sum(sc_i[...], axis=1, keepdims=True), zero)
    stats_send(2, st_q, sr_q)

    for which, dst in ((0, r2k), (1, r2v)):
        arrived(dst.at[others], a2_s.at[which], a2_r.at[which])

    own_k = r2k[...].astype(F32).reshape(PATCH, kvd)
    own_v = r2v[...].astype(F32).reshape(PATCH, kvd)
    gik[:, col(me)] = own_k.astype(BF16)
    giv[:, col(me)] = own_v.astype(BF16)
    gather_start(3, gik_block)
    gather_start(4, giv_block)
    stage_send(xi, 1, i_send, i_l1)
    stage_own(xi, i_own)
    level_two(1, i_own, i_l1, i_s2, i_l2)
    level_go(1, i_s2, i_l2)
    far_finish(1, gka_block)
    far_finish(2, gva_block)

    def text_far(p):
        rows_p = pl.ds(p * PATCH, PATCH)

        def body(j, _):
            cs = pl.ds(pl.multiple_of(j * step, step), step)
            d = (dt[p, :, cs] + far_products(gk, gv, rows_p, cs)) * gain[:, cs]
            dt[p, :, cs] = d
            co_t[p] += fold(d * text[slot_at[p], :, cs].astype(F32))
            return 0

        lax.fori_loop(0, width // step, body, 0)

    text_far(0)
    near_finish(3, gik_block)
    near_finish(4, giv_block)

    def image_near(j, _):
        cs = pl.ds(pl.multiple_of(j * step, step), step)
        dg[:, cs] = products(gik, giv, image_rows, cs, y)
        return 0

    lax.fori_loop(0, width // step // 2, image_near, 0)
    gather_relay(3, gik_block)
    gather_relay(4, giv_block)
    lax.fori_loop(width // step // 2, width // step, image_near, 0)
    co_i[...] = jnp.zeros(co_i.shape, F32)

    arrived(kbr.at[others], kbz_s.at[0], kbz_r.at[0])

    for k in range(1, ycount):
        m = yprev(k) * 2 + core
        for which, g in ((0, gk), (1, gv)):
            g[later_rows, col(m)] = kbr[:, k - 1, which].astype(F32).reshape(PATCH, kvd).astype(BF16)
            send(
                g.at[later_rows, col(m)], g.at[later_rows, col(m)], kbp_s.at[which, k - 1], kbp_r.at[which, k - 1],
                (me_d, partner),
            )
    far_finish(3, gik_block)
    far_finish(4, giv_block)

    def image_far(j, _):
        cs = pl.ds(pl.multiple_of(j * step, step), step)
        d = (dg[:, cs] + far_products(gik, giv, image_rows, cs)) * gain[:, cs]
        dg[:, cs] = d
        co_i[...] += fold(d * emb[:, cs].astype(F32))
        return 0

    lax.fori_loop(0, width // step, image_far, 0)
    st_i[...] = to_rows(zero, jnp.sum(co_i[...], axis=1, keepdims=True))
    stats_send(1, st_i, sr_i)
    text_go(1)
    sq_i, _ = stats_total(2, st_q, sr_q)
    scale_i = lax.rsqrt(sq_i / d_model + 1e-05)
    sc_i[...] = jnp.broadcast_to(scale_i, sc_i.shape)
    total = level_end(1, i_own, i_l1, i_l2)
    kvb[...] = (total * sc_i[:, 0:1]).reshape(dp, rb, 2 * kvd).astype(BF16)
    r3[me_d] = kvb[me_d]

    def b1(k):
        return remote(kvb.at[dnext(k)], r3.at[me_d], b1_s.at[0], b1_r.at[0], (dnext(k), me))

    @pl.loop(1, dp)
    def _(k):
        b1(k).start()

    for k in range(1, ycount):
        for which, g in ((0, gk), (1, gv)):
            arrived(g.at[later_rows, col(yprev(k) * 2 + 1 - core)], kbp_s.at[which, k - 1], kbp_r.at[which, k - 1])
    text_far(1)
    st_t[...] = to_rows(
        jnp.sum(sc_t[...].reshape(tokens, 128), axis=1, keepdims=True),
        jnp.sum(co_t[...].reshape(tokens, 128), axis=1, keepdims=True),
    )
    stats_send(0, st_t, sr_t)

    arrived(tb_recv.at[others], tbz_s.at[0], tbz_r.at[0])

    tb_sel[...] = tb_recv[lone]
    for k in range(1, ycount):
        send(tb_sel.at[k - 1], tb_y.at[k - 1], tby_s.at[k - 1], tby_r.at[k - 1], (me_d, ynext(k) * 2 + core))
    _, inner_i = stats_total(1, st_i, sr_i)
    scale_i = sc_i[:, 0:1]
    co_i[...] = jnp.broadcast_to(scale_i * scale_i * scale_i * (inner_i / d_model), co_i.shape)

    def image_end(j, _):
        cs = pl.ds(pl.multiple_of(j * step, step), step)
        d = wide(sc_i[...]) * dg[:, cs] - emb[:, cs].astype(F32) * wide(co_i[...])
        dimg[:, cs] = d.astype(BF16)
        return 0

    lax.fori_loop(0, width // step, image_end, 0)
    cuts = vis_cuts(dv)
    pieces = len(cuts) - 1

    def vis_chunk(j):
        at = pl.ds(cuts[j], cuts[j + 1] - cuts[j])
        d = nt(dimg[...], wp[at, :]).reshape(ycount, 2, rows, cuts[j + 1] - cuts[j])
        for yi in range(ycount):
            a, b = d[yi, 0], d[yi, 1]
            first = core == 0
            d_own[yi, :, at] = jnp.where(first, a, b)
            d_send[yi, :, at] = jnp.where(first, b, a).astype(BF16)
        start(d_send.at[:, :, at], d_l1.at[:, :, at], dv_s.at[0], dv_r.at[j, 0], (me_d, partner))

    def vis_two(j):
        at = pl.ds(cuts[j], cuts[j + 1] - cuts[j])
        arrived(d_l1.at[:, :, at], dv_s.at[0], dv_r.at[j, 0])
        for k in range(1, ycount):
            yk = ynext(k)
            d_s2[k, :, at] = (d_own[yk, :, at] + d_l1[yk, :, at].astype(F32)).astype(BF16)
            start(d_s2.at[k, :, at], d_l2.at[k, :, at], dv_s.at[k], dv_r.at[j, k], (me_d, yk * 2 + core))

    def b2(k):
        return remote(s4.at[dnext(k)], r4.at[0, my_inner, my_outer], b2_s.at[0], b2_r.at[0], (dnext(k), me))

    def b3(k):
        target = lax.rem(my_outer + k, outer) * inner + my_inner
        return remote(s5, r4.at[1, my_inner, my_outer], b3_s.at[0], b3_r.at[0], (target, me))

    def b4():
        block = r4.at[1, my_inner]
        return remote(block, block, b3_s.at[1], b3_r.at[1], (my_outer * inner + 1 - my_inner, me))

    for j in range(pieces):
        vis_chunk(j)
        if j > 0:
            vis_two(j - 1)
        if j == min(2, pieces - 1):

            arrived(r3.at[others], b1_s.at[0], b1_r.at[0])

            extra = jnp.zeros((rb, 2 * kvd), F32)
            for k in range(1, ycount):
                arrived(tb_y.at[k - 1], tby_s.at[k - 1], tby_r.at[k - 1])
                extra = extra + tb_y[k - 1].astype(F32)
            r3[dp] = extra.astype(BF16)

            @pl.loop(0, dp)
            def _(d):
                source = owner_of(d * slots + 1)
                source = jnp.where(is_filled(d * slots) == 1, owner_of(d * slots), source)
                s4[d] = r3[jnp.where(d == lone, jnp.int32(dp), source)]

            s5[...] = r3[owner_of(crowded * slots + 1)]
            r4[0, my_inner, my_outer] = s4[me_d]
            r4[1, my_inner, my_outer] = s5[...]

            @pl.loop(1, outer)
            def _(k):
                b3(k).start()

            @pl.loop(1, dp)
            def _(k):
                b2(k).start()

    vis_two(pieces - 1)
    arrived(r4.at[1, my_inner, pl.ds(0, outer - 1)], b3_s.at[0], b3_r.at[0])
    b4().start()
    sq_t, inner_t = stats_total(0, st_t, sr_t)
    keep = jnp.concatenate([jnp.full((PATCH, 1), 1.0, F32) * keeps[p] for p in range(slots)], axis=0)
    scale_t = lax.rsqrt(sq_t / d_model + 1e-05)
    sc_t[...] = jnp.broadcast_to(scale_t * keep, (tokens, 128)).reshape(sc_t.shape)
    co_t[...] = jnp.broadcast_to(
        scale_t * scale_t * scale_t * (inner_t / d_model) * keep, (tokens, 128)
    ).reshape(co_t.shape)

    def text_back(j, _):
        cs = pl.ds(pl.multiple_of(j * step, step), step)
        for s in range(slots):
            at = place_of[s]
            d = wide(sc_t[at]) * dt[at, :, cs] - text[s, :, cs].astype(F32) * wide(co_t[at])
            tg[s * PATCH:(s + 1) * PATCH, cs] = d.astype(BF16)
        return 0

    lax.fori_loop(0, width // step, text_back, 0)
    vf = vis[...].astype(F32)
    vscale = lax.rsqrt(jnp.mean(vf * vf, axis=1, keepdims=True) + 1e-06)
    hs = []
    for j in range(pieces):
        at = pl.ds(cuts[j], cuts[j + 1] - cuts[j])
        d = d_own[y, :, at] + d_l1[y, :, at].astype(F32)
        for k in range(1, ycount):
            arrived(d_l2.at[k, :, at], dv_s.at[k], dv_r.at[j, k])
            d = d + d_l2[k, :, at].astype(F32)
        hs.append(d.astype(BF16).astype(F32))
    h = jnp.concatenate(hs, axis=1) * gain_row(vgain)
    v_inner = jnp.mean(h * vf, axis=1, keepdims=True)
    vg_out[...] = (vscale * h - vf * vscale * vscale * vscale * v_inner).astype(BF16)

    arrived(s4.at[others], b2_s.at[0], b2_r.at[0])
    arrived(r4.at[1, 1 - my_inner], b3_s.at[1], b3_r.at[1])

    arrived(t_l1.at[y], rs_s.at[0, 0], rs_r.at[0, 0])
    for p in range(t_pieces):
        for k in range(1, ycount):
            text_piece(p, k).wait_recv()
    direct = t_l2[1].astype(F32)
    for k in range(2, ycount):
        direct = direct + t_l2[k].astype(F32)
    for s in range(slots):
        at = place_of[s]
        is_first = 1.0 - at.astype(F32)
        which = s * first_holds * second_holds
        placed = jnp.concatenate([r4[which, r % inner, r // inner] for r in range(dp)], axis=0).astype(F32)
        total = t_own[y, at] + t_l1[y, at].astype(F32) + direct * is_first + placed * ((1.0 - is_first) * at_lone)
        out = total * sc_t[at][:, 0:1] + placed * filled[s]
        rows_s = pl.ds(s * PATCH, PATCH)
        k_out[rows_s, :] = out[:, :kvd].astype(BF16)
        v_out[rows_s, :] = out[:, kvd:].astype(BF16)
    for copy in sends:
        copy.wait_send()

    def sent(block, sem):
        remote(block, block, sem, ag_r.at[0, 0], (me_d, partner)).wait_send()

    for which, (first, second) in enumerate(((kg4, s2k), (vg4, s2v))):
        sent(first.at[:, others], a1_s.at[which])
        sent(second.at[others], a2_s.at[which])
    sent(kvb.at[others], b1_s.at[0])
    sent(s4.at[others], b2_s.at[0])
    sent(r4.at[1, my_inner, pl.ds(0, outer - 1)], b3_s.at[0])
    sent(r4.at[1, my_inner], b3_s.at[1])
    sent(kbr.at[others], kbz_s.at[0])
    sent(tb_send.at[others], tbz_s.at[0])
    sent(t_send, rs_s.at[0, 0])
    sent(i_send, rs_s.at[1, 0])
    sent(d_send, dv_s.at[0])
    for k in range(1, ycount):
        sent(t_s2.at[k], rs_s.at[0, k])
        sent(i_s2.at[k], rs_s.at[1, k])
        sent(d_s2.at[k], dv_s.at[k])
    for n, sr in enumerate((sr_t, sr_i, sr_q)):
        sent(sr.at[pl.ds(0, mp - 1)], st_s.at[n])


def shards(vision, vision_gain, image_slot, text_embed, w_proj, llm_gain, w_key, w_value, key_grad, value_grad):
    dp = lax.axis_size("dp")
    mp = lax.axis_size("mp")
    tokens, width = text_embed.shape
    slots = tokens // PATCH
    rows, dv = vision.shape
    kvd = key_grad.shape[1]
    kv = kvd * mp
    img = rows * mp
    rb = PATCH // dp
    ys = mp // 2
    pieces = len(vis_cuts(dv)) - 1
    V = pltpu.VMEM
    any_spec = pl.BlockSpec(memory_space=pl.ANY)
    vmem = pl.BlockSpec(memory_space=pltpu.VMEM)
    smem = pl.BlockSpec(memory_space=pltpu.SMEM)
    scratch = [
        V((rows, dv), BF16), V((mp, rows, dv), BF16), V((slots, PATCH, width), BF16), V((dv, width), BF16),
        V((width, kv), BF16), V((width, kv), BF16), V((tokens, width), BF16),
        V((tokens, kv), BF16), V((tokens, kv), BF16), V((img, kv), BF16), V((img, kv), BF16),
        V((img, width), BF16), V((img, width), BF16), V((img, width), BF16), V((img, width), F32),
    ]
    t_shape = (ys, slots, PATCH, 2 * kvd)
    i_shape = (ys, img, 2 * kvd)
    half = (ys, PATCH, 2 * kvd)
    scratch += [V(t_shape, BF16), V(t_shape, F32), V(t_shape, BF16), V(half, BF16), V(half, BF16)]
    scratch += [V(i_shape, BF16), V(i_shape, F32), V(i_shape, BF16), V(i_shape, BF16), V(i_shape, BF16)]
    scratch += [
        V((ys, rows, dv), BF16), V((ys, rows, dv), F32), V((ys, rows, dv), BF16), V((ys, rows, dv), BF16),
        V((ys, rows, dv), BF16),
        V((8, tokens), F32), V((mp, 8, tokens), F32), V((8, img), F32), V((mp, 8, img), F32),
        V((8, img), F32), V((mp, 8, img), F32),
        V((slots, PATCH, 128), F32), V((slots, PATCH, 128), F32), V((img, 128), F32), V((img, 128), F32),
        V((slots, PATCH, kvd), BF16), V((slots, PATCH, kvd), BF16),
        V((2, rb, kvd), BF16), V((ys - 1, 2, rb, kvd), BF16), V((dp, ys - 1, 2, rb, kvd), BF16),
        V((dp, ys - 1, rb, 2 * kvd), BF16), V((dp, ys - 1, rb, 2 * kvd), BF16),
        V((ys - 1, rb, 2 * kvd), BF16), V((ys - 1, rb, 2 * kvd), BF16),
        V((dp * slots, rb, kvd), BF16), V((dp * slots, rb, kvd), BF16),
        V((dp, rb, kvd), BF16), V((dp, rb, kvd), BF16), V((dp, rb, kvd), BF16), V((dp, rb, kvd), BF16),
        V((dp, rb, 2 * kvd), BF16), V((dp + 1, rb, 2 * kvd), BF16),
        V((dp, rb, 2 * kvd), BF16), V((rb, 2 * kvd), BF16), V((2, 2, dp // 2, rb, 2 * kvd), BF16),
        DMA((9,)), DMA((5, 2 * ys - 1)), DMA((5, 2 * ys - 1)), DMA((2, ys)), DMA((2, ys)), DMA((ys - 1,)),
        DMA((ys - 1, 2)), DMA((3,)), DMA((3,)), DMA((ys,)), DMA((pieces, ys)),
        DMA((2,)), DMA((2,)), DMA((2,)), DMA((2,)),
        DMA((1,)), DMA((1,)), DMA((1,)), DMA((1,)), DMA((2,)), DMA((2,)),
        DMA((ys - 1,)), DMA((ys - 1,)), DMA((1,)), DMA((1,)), DMA((2, ys - 1)), DMA((2, ys - 1)),
        DMA((1,)), DMA((1,)), DMA((ys - 1,)), DMA((ys - 1,)), V((slots, PATCH, width), F32),
    ]
    shapes = ((tokens, kvd), (tokens, kvd), (tokens, width), (rows, dv))
    room = sum(2 * a * b for a, b in shapes)
    lanes = 128 if dv % 128 == 0 else dv
    results = pl.pallas_call(
        functools.partial(kernel, dp, mp),
        out_shape=tuple(V(shape, BF16) for shape in shapes),
        in_specs=[smem, any_spec, vmem, any_spec, any_spec, vmem] + [any_spec] * 6,
        out_specs=(vmem,) * len(shapes),
        scratch_shapes=scratch,
        compiler_params=pltpu.CompilerParams(
            collective_id=0, has_side_effects=True, vmem_limit_bytes=67043328 - room
        ),
    )(
        image_slot, vision, vision_gain.reshape(-1, lanes), text_embed.reshape(slots, PATCH, width), w_proj,
        llm_gain[None, :], w_key, w_value, key_grad.reshape(slots, PATCH, kvd), value_grad.reshape(slots, PATCH, kvd),
        key_grad.reshape(slots, dp, rb, kvd), value_grad.reshape(slots, dp, rb, kvd),
    )
    return pl.pallas_call(
        write_out,
        out_shape=tuple(jax.ShapeDtypeStruct(shape, BF16) for shape in shapes),
        in_specs=[vmem] * len(shapes),
        out_specs=(any_spec,) * len(shapes),
        scratch_shapes=[DMA((len(shapes),))],
        compiler_params=pltpu.CompilerParams(vmem_limit_bytes=1 << 20),
    )(*results)


def solution(mesh):
    placed = (
        P(("dp", "mp"), None),
        P(),
        P(),
        P("dp", "mp"),
        P(None, "mp"),
        P("mp"),
        P("mp", None),
        P("mp", None),
        P("dp", "mp"),
        P("dp", "mp"),
    )
    return jax.shard_map(
        shards,
        mesh=mesh,
        in_specs=placed,
        out_specs=(P("dp", "mp"), P("dp", "mp"), P("dp", "mp"), P(("dp", "mp"), None)),
        check_vma=False,
    )
```

```python
import functools

import jax
import jax.numpy as jnp
from jax import lax
from jax.experimental import pallas as pl
from jax.experimental.pallas import tpu as pltpu
from jax.sharding import PartitionSpec as P

PATCH = 256
F32 = jnp.float32
BF16 = jnp.bfloat16
NT = (((1,), (1,)), ((), ()))
DMA = pltpu.SemaphoreType.DMA


def nt(a, b):
    return lax.dot_general(a, b, NT, preferred_element_type=F32)


def remote(src, dst, send_sem, recv_sem, device):
    return pltpu.make_async_remote_copy(
        src_ref=src, dst_ref=dst, send_sem=send_sem, recv_sem=recv_sem,
        device_id=device, device_id_type=pl.DeviceIdType.MESH,
    )


def to_rows(sq, inner):
    lane = lax.broadcasted_iota(jnp.int32, (sq.shape[0], 128), 1)
    wide = jnp.where(lane == 0, sq, jnp.where(lane == 1, inner, 0.0))
    return jnp.transpose(wide)[:8]


def to_columns(rows):
    wide = jnp.transpose(jnp.concatenate([rows] * 16, axis=0))
    return wide[:, 0:1], wide[:, 1:2]


def gain_row(ref):
    if ref.shape[0] == 1:
        return ref[...]
    return jnp.concatenate([ref[i:i + 1, :] for i in range(ref.shape[0])], axis=1)


def vis_cuts(dv):
    if dv % 128:
        return (0, dv)
    units = dv // 128
    first = max(units // 12, 1)
    cuts = [0, first, min(2 * first, units)]
    while cuts[-1] < units:
        cuts.append(min(cuts[-1] + 2 * first, units))
    if len(cuts) > 3 and cuts[-1] - cuts[-2] < first:
        del cuts[-2]
    return tuple(128 * c for c in cuts)


def write_out(*refs):
    count = (len(refs) - 1) // 2
    copies = [pltpu.make_async_copy(refs[n], refs[count + n], refs[-1].at[n]) for n in range(count)]
    for copy in copies:
        copy.start()
    for copy in copies:
        copy.wait()


def kernel(
    dp, mp, slot_ref, vision_h, vgain, text_h, wp_h, gain, wk_h, wv_h, kg_h, vg_h, kg4, vg4,
    k_out, v_out, tg, vg_out,
    vis, vis_all, text, wp, wk, wv, xt, gk, gv, gik, giv, emb, xi, dimg, dg,
    t_send, t_own, t_l1, t_s2, t_l2, i_send, i_own, i_l1, i_s2, i_l2,
    d_send, d_own, d_l1, d_s2, d_l2,
    st_t, sr_t, st_i, sr_i, st_q, sr_q, sc_t, co_t, sc_i, co_i,
    kgs, vgs, kb_send, kb_y, kbr, tb_send, tb_recv, tb_sel, tb_y,
    r1k, r1v, s2k, s2v, r2k, r2v, kvb, r3, s4, s5, r4,
    load_sem, ag_s, ag_r, rs_s, rs_r, rs1_r, t2_r, st_s, st_r, dv_s, dv_r,
    a1_s, a1_r, a2_s, a2_r, b1_s, b1_r, b2_s, b2_r, b3_s, b3_r, kby_s, kby_r, kbz_s, kbz_r, kbp_s, kbp_r,
    tbz_s, tbz_r, tby_s, tby_r, dt,
):
    me_d = lax.axis_index("dp")
    me = lax.axis_index("mp")
    ycount = mp // 2
    core = lax.rem(me, 2)
    y = lax.div(me, 2)
    partner = y * 2 + (1 - core)
    slots, _, width = text.shape
    tokens = slots * PATCH
    kvd = gk.shape[1] // mp
    rows = vis.shape[0]
    dv = vis.shape[1]
    d_model = width * mp
    rb = r1k.shape[1]
    img_rows = mp * rows
    t_pieces = 2
    piece_rows = PATCH // t_pieces

    def ynext(k):
        return lax.rem(y + k, ycount)

    def yprev(k):
        return lax.rem(y + ycount - k, ycount)

    def dnext(k):
        return lax.rem(me_d + k, dp)

    def dprev(k):
        return lax.rem(me_d + dp - k, dp)

    def col(m):
        return pl.ds(pl.multiple_of(m * kvd, kvd), kvd)

    def is_filled(slot):
        found = jnp.int32(0)
        for i in range(dp):
            found = jnp.where(slot_ref[i] == slot, jnp.int32(1), found)
        return found

    def owner_of(slot):
        found = jnp.int32(0)
        for i in range(dp):
            found = jnp.where(slot_ref[i] == slot, jnp.int32(i), found)
        return found

    def holds(s):
        return is_filled(me_d * slots + s)

    inner = 2
    outer = dp // inner
    my_inner = lax.rem(me_d, inner)
    my_outer = lax.div(me_d, inner)

    barrier = pltpu.get_barrier_semaphore()

    @pl.loop(1, dp)
    def _(k):
        pl.semaphore_signal(barrier, inc=1, device_id=(dnext(k), me), device_id_type=pl.DeviceIdType.MESH)

    for k in range(1, mp):
        pl.semaphore_signal(
            barrier, inc=1, device_id=(me_d, lax.rem(me + k, mp)), device_id_type=pl.DeviceIdType.MESH
        )

    sends = []

    def send(*args):
        copy = remote(*args)
        copy.start()
        sends.append(copy)

    def start(*args):
        remote(*args).start()

    loads = [
        (vision_h, vis), (kg_h, kgs), (vg_h, vgs),
        (text_h, text), (wk_h, wk), (wv_h, wv), (wp_h, wp),
        (kg4.at[:, me_d], r1k.at[pl.ds(me_d * slots, slots)]),
        (vg4.at[:, me_d], r1v.at[pl.ds(me_d * slots, slots)]),
    ]
    loads = [pltpu.make_async_copy(a, b, load_sem.at[n]) for n, (a, b) in enumerate(loads)]
    for copy in loads:
        copy.start()

    pl.semaphore_wait(barrier, dp - 1 + mp - 1)
    mine = pl.ds(me_d * slots, slots)
    others = pl.ds(0, dp - 1)

    def a1(k, which):
        src, dst = ((kg4, r1k), (vg4, r1v))[which]
        return remote(
            src.at[:, dnext(k)], dst.at[mine], a1_s.at[which], a1_r.at[which], (dnext(k), me)
        )

    @pl.loop(1, dp)
    def _(k):
        a1(k, 0).start()
        a1(k, 1).start()


    def gather_start(g, block):
        for k in range(1, ycount):
            send(block(me), block(me), ag_s.at[g, k], ag_r.at[g, k], (me_d, ynext(k) * 2 + core))
        send(block(me), block(me), ag_s.at[g, 0], ag_r.at[g, 0], (me_d, partner))

    def arrived(block, send_sem, recv_sem):
        remote(block, block, send_sem, recv_sem, (me_d, partner)).wait_recv()

    def gather_relay(g, block):
        for k in range(1, ycount):
            got = block(yprev(k) * 2 + core)
            arrived(got, ag_s.at[g, k], ag_r.at[g, k])
            send(got, got, ag_s.at[g, ycount + k - 1], ag_r.at[g, ycount + k - 1], (me_d, partner))

    def gather_finish(g, block):
        arrived(block(partner), ag_s.at[g, 0], ag_r.at[g, 0])
        for k in range(1, ycount):
            arrived(block(yprev(k) * 2 + 1 - core), ag_s.at[g, ycount + k - 1], ag_r.at[g, ycount + k - 1])

    vis_block = lambda m: vis_all.at[m]
    gk_block = lambda m: gk.at[:, col(m)]
    gv_block = lambda m: gv.at[:, col(m)]
    gik_block = lambda m: gik.at[:, col(m)]
    giv_block = lambda m: giv.at[:, col(m)]

    loads[0].wait()
    vf = vis[...].astype(F32)
    vscale = lax.rsqrt(jnp.mean(vf * vf, axis=1, keepdims=True) + 1e-06)
    vis_gain = gain_row(vgain)
    vis_all[me] = (vf * vscale * vis_gain).astype(BF16)
    gather_start(0, vis_block)

    first_holds, second_holds = holds(0), holds(1)
    turned = first_holds * (1 - second_holds)
    slot_at = (turned, 1 - turned)
    place_of = (turned, 1 - turned)
    filled = (first_holds.astype(F32), second_holds.astype(F32))
    keeps = (1.0 - filled[0] * filled[1], (1.0 - filled[0]) * (1.0 - filled[1]))

    loads[1].wait()
    loads[2].wait()
    for p in range(slots):
        gk[p * PATCH:(p + 1) * PATCH, col(me)] = kgs[slot_at[p]]
        gv[p * PATCH:(p + 1) * PATCH, col(me)] = vgs[slot_at[p]]
    first_rows = pl.ds(0, PATCH)
    later_rows = pl.ds(PATCH, PATCH)
    gka_block = lambda m: gk.at[first_rows, col(m)]
    gva_block = lambda m: gv.at[first_rows, col(m)]

    def far_start(g, block):
        for k in range(1, ycount):
            send(block(me), block(me), ag_s.at[g, k], ag_r.at[g, k], (me_d, ynext(k) * 2 + core))

    def near_start(g, block):
        send(block(me), block(me), ag_s.at[g, 0], ag_r.at[g, 0], (me_d, partner))

    def near_finish(g, block):
        arrived(block(partner), ag_s.at[g, 0], ag_r.at[g, 0])

    def far_finish(g, block):
        for k in range(1, ycount):
            arrived(block(yprev(k) * 2 + 1 - core), ag_s.at[g, ycount + k - 1], ag_r.at[g, ycount + k - 1])

    def heads(yk):
        return pl.ds(pl.multiple_of(yk * 2 * kvd, 2 * kvd), 2 * kvd)

    def products(keys, values, at, cs, yk):
        at_heads = heads(yk)
        return nt(keys[at, at_heads], wk[cs, at_heads]) + nt(values[at, at_heads], wv[cs, at_heads])

    def turned_products(keys, values, at, cs, yk):
        at_heads = heads(yk)
        return nt(wk[cs, at_heads], keys[at, at_heads]) + nt(wv[cs, at_heads], values[at, at_heads])

    def far_products(keys, values, at, cs):
        total = turned_products(keys, values, at, cs, ynext(1))
        for k in range(2, ycount):
            total = total + turned_products(keys, values, at, cs, ynext(k))
        return jnp.transpose(total)

    step = 256
    big = min(1024, width)
    every = pl.ds(0, tokens)
    image_rows = pl.ds(0, img_rows)

    far_start(1, gka_block)
    far_start(2, gva_block)
    near_start(1, gk_block)
    near_start(2, gv_block)

    def chunk(x, m):
        k_part = jnp.dot(x[...], wk[:, col(m)], preferred_element_type=F32)
        v_part = jnp.dot(x[...], wv[:, col(m)], preferred_element_type=F32)
        return k_part, v_part

    def stage_send(x, n, psend, l1):
        for k in range(ycount):
            yk = ynext(k)
            k_part, v_part = chunk(x, yk * 2 + 1 - core)
            shape = psend.shape[1:-1] + (kvd,)
            psend[yk, ..., :kvd] = k_part.astype(BF16).reshape(shape)
            psend[yk, ..., kvd:] = v_part.astype(BF16).reshape(shape)
            start(psend.at[yk], l1.at[yk], rs_s.at[n, 0], rs_r.at[n, k], (me_d, partner))

    def stage_own(x, own):
        for k in range(ycount):
            yk = ynext(k)
            k_part, v_part = chunk(x, yk * 2 + core)
            shape = own.shape[1:-1] + (kvd,)
            own[yk, ..., :kvd] = k_part.reshape(shape)
            own[yk, ..., kvd:] = v_part.reshape(shape)

    def level_two(n, own, l1, s2, l2):
        for k in range(ycount - 1, 0, -1):
            yk = ynext(k)
            arrived(l1.at[yk], rs_s.at[n, 0], rs_r.at[n, k])
            s2[k] = (own[yk] + l1[yk].astype(F32)).astype(BF16)

    def level_go(n, s2, l2):
        for k in range(ycount - 1, 0, -1):
            for h in range(2):
                at = pl.ds(h * kvd, kvd)
                start(
                    s2.at[k, :, at], l2.at[k, :, at], rs_s.at[n, k], rs1_r.at[k - 1, h],
                    (me_d, ynext(k) * 2 + core),
                )

    def text_piece(p, k):
        at = pl.ds(p * piece_rows, piece_rows)
        return remote(
            t_s2.at[k, at], t_l2.at[k, at], rs_s.at[0, k], t2_r.at[k - 1, p], (me_d, ynext(k) * 2 + core)
        )

    def text_go(p):
        for k in range(ycount - 1, 0, -1):
            text_piece(p, k).start()

    def stats_send(n, st, sr):
        for k in range(1, mp):
            start(st, sr.at[k], st_s.at[n], st_r.at[n], (me_d, lax.rem(me + k, mp)))

    def stats_total(n, st, sr):
        total = st[...]
        arrived(sr.at[pl.ds(1, mp - 1)], st_s.at[n], st_r.at[n])
        for k in range(1, mp):
            total = total + sr[k]
        return to_columns(total)

    def wide(p):
        return jnp.concatenate([p] * (step // 128), axis=1)

    def fold(p):
        total = p[:, :128]
        for n in range(1, p.shape[1] // 128):
            total = total + p[:, n * 128:(n + 1) * 128]
        return total

    loads[3].wait()
    for p in range(slots):
        tf = text[slot_at[p]].astype(F32)
        sc_t[p] = fold(tf * tf)
        xt[p * PATCH:(p + 1) * PATCH, :] = (tf * gain[...]).astype(BF16)
    loads[4].wait()
    loads[5].wait()
    stage_send(xt, 0, t_send, t_l1)
    stage_own(xt, t_own)
    for k in range(ycount - 1, 0, -1):
        yk = ynext(k)
        arrived(t_l1.at[yk], rs_s.at[0, 0], rs_r.at[0, k])
        t_s2[k] = (t_own[yk, 0] + t_l1[yk, 0].astype(F32)).astype(BF16)
        rest = t_own[yk, 1] + t_l1[yk, 1].astype(F32)
        tb_send[:, k - 1] = rest.reshape(dp, rb, 2 * kvd).astype(BF16)
    tb_recv[me_d] = tb_send[me_d]
    near_finish(1, gk_block)
    near_finish(2, gv_block)

    def text_near(j, _):
        cs = pl.ds(pl.multiple_of(j * step, step), step)
        dt[:, :, cs] = products(gk, gv, every, cs, y).reshape(slots, PATCH, step)
        return 0

    lax.fori_loop(0, width // step // 2, text_near, 0)
    lax.fori_loop(width // step // 2, width // step, text_near, 0)
    co_t[...] = jnp.zeros(co_t.shape, F32)
    gather_relay(0, vis_block)
    def survey(d, found):
        count = jnp.int32(0)
        for i in range(dp):
            count = count + jnp.where(lax.div(slot_ref[i], jnp.int32(slots)) == d, jnp.int32(1), jnp.int32(0))
        return jnp.where(count == 0, d, found[0]), jnp.where(count > 1, d, found[1])

    lone, crowded = lax.fori_loop(0, dp, survey, (jnp.int32(0), jnp.int32(0)))
    lone_slot = lone * slots + 1
    at_lone = keeps[1]
    loads[7].wait()
    loads[8].wait()

    for which, dst in ((0, r1k), (1, r1v)):
        arrived(dst.at[pl.ds(0, (dp - 1) * slots)], a1_s.at[which], a1_r.at[which])

    @pl.loop(0, dp)
    def _(i):
        s2k[i] = r1k[slot_ref[i]]
        s2v[i] = r1v[slot_ref[i]]

    r2k[me_d] = s2k[me_d]
    r2v[me_d] = s2v[me_d]

    def a2(k, which):
        src, dst = ((s2k, r2k), (s2v, r2v))[which]
        return remote(
            src.at[dnext(k)], dst.at[me_d], a2_s.at[which], a2_r.at[which], (dnext(k), me)
        )

    @pl.loop(1, dp)
    def _(k):
        a2(k, 0).start()
        a2(k, 1).start()

    kb_send[0] = r1k[lone_slot]
    kb_send[1] = r1v[lone_slot]
    for k in range(1, ycount):
        send(kb_send, kb_y.at[k - 1], kby_s.at[k - 1], kby_r.at[k - 1], (me_d, ynext(k) * 2 + core))
    text_go(0)
    gather_finish(0, vis_block)
    loads[6].wait()

    sc_i[...] = jnp.zeros(sc_i.shape, F32)

    def project(j, _):
        cs = pl.ds(pl.multiple_of(j * step, step), step)
        e = jnp.concatenate([vis_all[m] for m in range(mp)], axis=0)
        e = jnp.dot(e, wp[:, cs], preferred_element_type=F32).astype(BF16)
        emb[:, cs] = e
        ef = e.astype(F32)
        xi[:, cs] = (ef * gain[:, cs]).astype(BF16)
        sc_i[...] += fold(ef * ef)
        return 0

    lax.fori_loop(0, width // step, project, 0)
    for k in range(1, ycount):
        arrived(kb_y.at[k - 1], kby_s.at[k - 1], kby_r.at[k - 1])
    kbr[me_d] = kb_y[...]

    def kbz(k):
        return remote(kb_y, kbr.at[me_d], kbz_s.at[0], kbz_r.at[0], (dnext(k), me))

    def tbz(k):
        return remote(tb_send.at[dnext(k)], tb_recv.at[me_d], tbz_s.at[0], tbz_r.at[0], (dnext(k), me))

    @pl.loop(1, dp)
    def _(k):
        kbz(k).start()

    @pl.loop(1, dp)
    def _(k):
        tbz(k).start()

    gather_relay(1, gka_block)
    gather_relay(2, gva_block)
    zero = jnp.zeros((img_rows, 1), F32)
    st_q[...] = to_rows(jnp.sum(sc_i[...], axis=1, keepdims=True), zero)
    stats_send(2, st_q, sr_q)

    for which, dst in ((0, r2k), (1, r2v)):
        arrived(dst.at[others], a2_s.at[which], a2_r.at[which])

    own_k = r2k[...].astype(F32).reshape(PATCH, kvd)
    own_v = r2v[...].astype(F32).reshape(PATCH, kvd)
    gik[:, col(me)] = own_k.astype(BF16)
    giv[:, col(me)] = own_v.astype(BF16)
    gather_start(3, gik_block)
    gather_start(4, giv_block)
    stage_send(xi, 1, i_send, i_l1)
    stage_own(xi, i_own)
    level_two(1, i_own, i_l1, i_s2, i_l2)
    level_go(1, i_s2, i_l2)
    far_finish(1, gka_block)
    far_finish(2, gva_block)

    def text_far(p):
        rows_p = pl.ds(p * PATCH, PATCH)

        def body(j, _):
            cs = pl.ds(pl.multiple_of(j * big, big), big)
            d = (dt[p, :, cs] + far_products(gk, gv, rows_p, cs)) * gain[:, cs]
            dt[p, :, cs] = d
            co_t[p] += fold(d * text[slot_at[p], :, cs].astype(F32))
            return 0

        lax.fori_loop(0, width // big, body, 0)

    text_far(0)
    near_finish(3, gik_block)
    near_finish(4, giv_block)

    def image_near(j, _):
        cs = pl.ds(pl.multiple_of(j * big, big), big)
        dg[:, cs] = jnp.transpose(turned_products(gik, giv, image_rows, cs, y))
        return 0

    lax.fori_loop(0, width // big, image_near, 0)
    gather_relay(3, gik_block)
    gather_relay(4, giv_block)
    co_i[...] = jnp.zeros(co_i.shape, F32)

    arrived(kbr.at[others], kbz_s.at[0], kbz_r.at[0])

    for k in range(1, ycount):
        m = yprev(k) * 2 + core
        for which, g in ((0, gk), (1, gv)):
            g[later_rows, col(m)] = kbr[:, k - 1, which].astype(F32).reshape(PATCH, kvd).astype(BF16)
            send(
                g.at[later_rows, col(m)], g.at[later_rows, col(m)], kbp_s.at[which, k - 1], kbp_r.at[which, k - 1],
                (me_d, partner),
            )
    far_finish(3, gik_block)
    far_finish(4, giv_block)

    def image_far(j, _):
        cs = pl.ds(pl.multiple_of(j * big, big), big)
        d = (dg[:, cs] + far_products(gik, giv, image_rows, cs)) * gain[:, cs]
        dg[:, cs] = d
        co_i[...] += fold(d * emb[:, cs].astype(F32))
        return 0

    lax.fori_loop(0, width // big, image_far, 0)
    st_i[...] = to_rows(zero, jnp.sum(co_i[...], axis=1, keepdims=True))
    stats_send(1, st_i, sr_i)
    text_go(1)
    sq_i, _ = stats_total(2, st_q, sr_q)
    scale_i = lax.rsqrt(sq_i / d_model + 1e-05)
    sc_i[...] = jnp.broadcast_to(scale_i, sc_i.shape)

    def b1(k, h):
        return remote(kvb.at[h, dnext(k)], r3.at[me_d, h], b1_s.at[h], b1_r.at[h], (dnext(k), me))

    def image_sums(h):
        at = pl.ds(h * kvd, kvd)
        total = i_own[y, :, at] + i_l1[y, :, at].astype(F32)
        for k in range(1, ycount):
            arrived(i_l2.at[k, :, at], rs_s.at[1, k], rs1_r.at[k - 1, h])
            total = total + i_l2[k, :, at].astype(F32)
        kvb[h] = (total * sc_i[:, 0:1]).reshape(dp, rb, kvd).astype(BF16)
        r3[me_d, h] = kvb[h, me_d]

        @pl.loop(1, dp)
        def _(k):
            b1(k, h).start()

    arrived(i_l1.at[y], rs_s.at[1, 0], rs_r.at[1, 0])
    image_sums(0)
    for k in range(1, ycount):
        for which, g in ((0, gk), (1, gv)):
            arrived(g.at[later_rows, col(yprev(k) * 2 + 1 - core)], kbp_s.at[which, k - 1], kbp_r.at[which, k - 1])
    text_far(1)
    image_sums(1)
    st_t[...] = to_rows(
        jnp.sum(sc_t[...].reshape(tokens, 128), axis=1, keepdims=True),
        jnp.sum(co_t[...].reshape(tokens, 128), axis=1, keepdims=True),
    )
    stats_send(0, st_t, sr_t)

    arrived(tb_recv.at[others], tbz_s.at[0], tbz_r.at[0])

    tb_sel[...] = tb_recv[lone]
    for k in range(1, ycount):
        send(tb_sel.at[k - 1], tb_y.at[k - 1], tby_s.at[k - 1], tby_r.at[k - 1], (me_d, ynext(k) * 2 + core))
    _, inner_i = stats_total(1, st_i, sr_i)
    scale_i = sc_i[:, 0:1]
    co_i[...] = jnp.broadcast_to(scale_i * scale_i * scale_i * (inner_i / d_model), co_i.shape)

    def image_end(j, _):
        cs = pl.ds(pl.multiple_of(j * step, step), step)
        d = wide(sc_i[...]) * dg[:, cs] - emb[:, cs].astype(F32) * wide(co_i[...])
        dimg[:, cs] = d.astype(BF16)
        return 0

    lax.fori_loop(0, width // step, image_end, 0)
    cuts = vis_cuts(dv)
    pieces = len(cuts) - 1

    def vis_chunk(j):
        at = pl.ds(cuts[j], cuts[j + 1] - cuts[j])
        d = nt(dimg[...], wp[at, :]).reshape(ycount, 2, rows, cuts[j + 1] - cuts[j])
        for yi in range(ycount):
            a, b = d[yi, 0], d[yi, 1]
            first = core == 0
            d_own[yi, :, at] = jnp.where(first, a, b)
            d_send[yi, :, at] = jnp.where(first, b, a).astype(BF16)
        start(d_send.at[:, :, at], d_l1.at[:, :, at], dv_s.at[0], dv_r.at[j, 0], (me_d, partner))

    def vis_two(j):
        at = pl.ds(cuts[j], cuts[j + 1] - cuts[j])
        arrived(d_l1.at[:, :, at], dv_s.at[0], dv_r.at[j, 0])
        for k in range(1, ycount):
            yk = ynext(k)
            d_s2[k, :, at] = (d_own[yk, :, at] + d_l1[yk, :, at].astype(F32)).astype(BF16)
            start(d_s2.at[k, :, at], d_l2.at[k, :, at], dv_s.at[k], dv_r.at[j, k], (me_d, yk * 2 + core))

    def b2(k):
        return remote(s4.at[dnext(k)], r4.at[0, my_inner, my_outer], b2_s.at[0], b2_r.at[0], (dnext(k), me))

    def b3(k):
        target = lax.rem(my_outer + k, outer) * inner + my_inner
        return remote(s5, r4.at[1, my_inner, my_outer], b3_s.at[0], b3_r.at[0], (target, me))

    def b4():
        block = r4.at[1, my_inner]
        return remote(block, block, b3_s.at[1], b3_r.at[1], (my_outer * inner + 1 - my_inner, me))

    for j in range(pieces):
        vis_chunk(j)
        if j > 0:
            vis_two(j - 1)
        if j == min(3, pieces - 1):

            for h in range(2):
                arrived(r3.at[others, h], b1_s.at[h], b1_r.at[h])

            extra = jnp.zeros((rb, 2 * kvd), F32)
            for k in range(1, ycount):
                arrived(tb_y.at[k - 1], tby_s.at[k - 1], tby_r.at[k - 1])
                extra = extra + tb_y[k - 1].astype(F32)
            r3[dp, 0] = extra[:, :kvd].astype(BF16)
            r3[dp, 1] = extra[:, kvd:].astype(BF16)

            @pl.loop(0, dp)
            def _(d):
                source = owner_of(d * slots + 1)
                source = jnp.where(is_filled(d * slots) == 1, owner_of(d * slots), source)
                source = jnp.where(d == lone, jnp.int32(dp), source)
                s4[d, :, :kvd] = r3[source, 0]
                s4[d, :, kvd:] = r3[source, 1]

            source = owner_of(crowded * slots + 1)
            s5[:, :kvd] = r3[source, 0]
            s5[:, kvd:] = r3[source, 1]
            r4[0, my_inner, my_outer] = s4[me_d]
            r4[1, my_inner, my_outer] = s5[...]

            @pl.loop(1, outer)
            def _(k):
                b3(k).start()

            @pl.loop(1, dp)
            def _(k):
                b2(k).start()

    vis_two(pieces - 1)
    arrived(r4.at[1, my_inner, pl.ds(0, outer - 1)], b3_s.at[0], b3_r.at[0])
    b4().start()
    sq_t, inner_t = stats_total(0, st_t, sr_t)
    keep = jnp.concatenate([jnp.full((PATCH, 1), 1.0, F32) * keeps[p] for p in range(slots)], axis=0)
    scale_t = lax.rsqrt(sq_t / d_model + 1e-05)
    sc_t[...] = jnp.broadcast_to(scale_t * keep, (tokens, 128)).reshape(sc_t.shape)
    co_t[...] = jnp.broadcast_to(
        scale_t * scale_t * scale_t * (inner_t / d_model) * keep, (tokens, 128)
    ).reshape(co_t.shape)

    def text_back(j, _):
        cs = pl.ds(pl.multiple_of(j * step, step), step)
        for s in range(slots):
            at = place_of[s]
            d = wide(sc_t[at]) * dt[at, :, cs] - text[s, :, cs].astype(F32) * wide(co_t[at])
            tg[s * PATCH:(s + 1) * PATCH, cs] = d.astype(BF16)
        return 0

    lax.fori_loop(0, width // step, text_back, 0)
    vf = vis[...].astype(F32)
    vscale = lax.rsqrt(jnp.mean(vf * vf, axis=1, keepdims=True) + 1e-06)
    row_gain = gain_row(vgain)
    lanes = jnp.zeros((rows, 128), F32)
    for j in range(pieces):
        at = pl.ds(cuts[j], cuts[j + 1] - cuts[j])
        d = d_own[y, :, at] + d_l1[y, :, at].astype(F32)
        for k in range(1, ycount):
            arrived(d_l2.at[k, :, at], dv_s.at[k], dv_r.at[j, k])
            d = d + d_l2[k, :, at].astype(F32)
        h = d.astype(BF16).astype(F32) * row_gain[:, cuts[j]:cuts[j + 1]]
        d_own[y, :, at] = h
        lanes = lanes + fold(h * vis[:, at].astype(F32))
    v_inner = jnp.sum(lanes, axis=1, keepdims=True) / dv
    vg_out[...] = (vscale * d_own[y] - vf * (vscale * vscale * vscale * v_inner)).astype(BF16)

    arrived(s4.at[others], b2_s.at[0], b2_r.at[0])
    arrived(r4.at[1, 1 - my_inner], b3_s.at[1], b3_r.at[1])

    arrived(t_l1.at[y], rs_s.at[0, 0], rs_r.at[0, 0])
    for p in range(t_pieces):
        for k in range(1, ycount):
            text_piece(p, k).wait_recv()
    direct = t_l2[1].astype(F32)
    for k in range(2, ycount):
        direct = direct + t_l2[k].astype(F32)
    for s in range(slots):
        at = place_of[s]
        is_first = 1.0 - at.astype(F32)
        which = s * first_holds * second_holds
        placed = jnp.concatenate([r4[which, r % inner, r // inner] for r in range(dp)], axis=0).astype(F32)
        total = t_own[y, at] + t_l1[y, at].astype(F32) + direct * is_first + placed * ((1.0 - is_first) * at_lone)
        out = total * sc_t[at][:, 0:1] + placed * filled[s]
        rows_s = pl.ds(s * PATCH, PATCH)
        k_out[rows_s, :] = out[:, :kvd].astype(BF16)
        v_out[rows_s, :] = out[:, kvd:].astype(BF16)
    for copy in sends:
        copy.wait_send()

    def sent(block, sem):
        remote(block, block, sem, ag_r.at[0, 0], (me_d, partner)).wait_send()

    for which, (first, second) in enumerate(((kg4, s2k), (vg4, s2v))):
        sent(first.at[:, others], a1_s.at[which])
        sent(second.at[others], a2_s.at[which])
    for h in range(2):
        sent(kvb.at[h, others], b1_s.at[h])
    sent(s4.at[others], b2_s.at[0])
    sent(r4.at[1, my_inner, pl.ds(0, outer - 1)], b3_s.at[0])
    sent(r4.at[1, my_inner], b3_s.at[1])
    sent(kbr.at[others], kbz_s.at[0])
    sent(tb_send.at[others], tbz_s.at[0])
    sent(t_send, rs_s.at[0, 0])
    sent(i_send, rs_s.at[1, 0])
    sent(d_send, dv_s.at[0])
    for k in range(1, ycount):
        sent(t_s2.at[k], rs_s.at[0, k])
        sent(i_s2.at[k], rs_s.at[1, k])
        sent(d_s2.at[k], dv_s.at[k])
    for n, sr in enumerate((sr_t, sr_i, sr_q)):
        sent(sr.at[pl.ds(0, mp - 1)], st_s.at[n])


def shards(vision, vision_gain, image_slot, text_embed, w_proj, llm_gain, w_key, w_value, key_grad, value_grad):
    dp = lax.axis_size("dp")
    mp = lax.axis_size("mp")
    tokens, width = text_embed.shape
    slots = tokens // PATCH
    rows, dv = vision.shape
    kvd = key_grad.shape[1]
    kv = kvd * mp
    img = rows * mp
    rb = PATCH // dp
    ys = mp // 2
    pieces = len(vis_cuts(dv)) - 1
    V = pltpu.VMEM
    any_spec = pl.BlockSpec(memory_space=pl.ANY)
    vmem = pl.BlockSpec(memory_space=pltpu.VMEM)
    smem = pl.BlockSpec(memory_space=pltpu.SMEM)
    scratch = [
        V((rows, dv), BF16), V((mp, rows, dv), BF16), V((slots, PATCH, width), BF16), V((dv, width), BF16),
        V((width, kv), BF16), V((width, kv), BF16), V((tokens, width), BF16),
        V((tokens, kv), BF16), V((tokens, kv), BF16), V((img, kv), BF16), V((img, kv), BF16),
        V((img, width), BF16), V((img, width), BF16), V((img, width), BF16), V((img, width), F32),
    ]
    t_shape = (ys, slots, PATCH, 2 * kvd)
    i_shape = (ys, img, 2 * kvd)
    half = (ys, PATCH, 2 * kvd)
    scratch += [V(t_shape, BF16), V(t_shape, F32), V(t_shape, BF16), V(half, BF16), V(half, BF16)]
    scratch += [V(i_shape, BF16), V(i_shape, F32), V(i_shape, BF16), V(i_shape, BF16), V(i_shape, BF16)]
    scratch += [
        V((ys, rows, dv), BF16), V((ys, rows, dv), F32), V((ys, rows, dv), BF16), V((ys, rows, dv), BF16),
        V((ys, rows, dv), BF16),
        V((8, tokens), F32), V((mp, 8, tokens), F32), V((8, img), F32), V((mp, 8, img), F32),
        V((8, img), F32), V((mp, 8, img), F32),
        V((slots, PATCH, 128), F32), V((slots, PATCH, 128), F32), V((img, 128), F32), V((img, 128), F32),
        V((slots, PATCH, kvd), BF16), V((slots, PATCH, kvd), BF16),
        V((2, rb, kvd), BF16), V((ys - 1, 2, rb, kvd), BF16), V((dp, ys - 1, 2, rb, kvd), BF16),
        V((dp, ys - 1, rb, 2 * kvd), BF16), V((dp, ys - 1, rb, 2 * kvd), BF16),
        V((ys - 1, rb, 2 * kvd), BF16), V((ys - 1, rb, 2 * kvd), BF16),
        V((dp * slots, rb, kvd), BF16), V((dp * slots, rb, kvd), BF16),
        V((dp, rb, kvd), BF16), V((dp, rb, kvd), BF16), V((dp, rb, kvd), BF16), V((dp, rb, kvd), BF16),
        V((2, dp, rb, kvd), BF16), V((dp + 1, 2, rb, kvd), BF16),
        V((dp, rb, 2 * kvd), BF16), V((rb, 2 * kvd), BF16), V((2, 2, dp // 2, rb, 2 * kvd), BF16),
        DMA((9,)), DMA((5, 2 * ys - 1)), DMA((5, 2 * ys - 1)), DMA((2, ys)), DMA((2, ys)), DMA((ys - 1, 2)),
        DMA((ys - 1, 2)), DMA((3,)), DMA((3,)), DMA((ys,)), DMA((pieces, ys)),
        DMA((2,)), DMA((2,)), DMA((2,)), DMA((2,)),
        DMA((2,)), DMA((2,)), DMA((1,)), DMA((1,)), DMA((2,)), DMA((2,)),
        DMA((ys - 1,)), DMA((ys - 1,)), DMA((1,)), DMA((1,)), DMA((2, ys - 1)), DMA((2, ys - 1)),
        DMA((1,)), DMA((1,)), DMA((ys - 1,)), DMA((ys - 1,)), V((slots, PATCH, width), F32),
    ]
    shapes = ((tokens, kvd), (tokens, kvd), (tokens, width), (rows, dv))
    room = sum(2 * a * b for a, b in shapes)
    lanes = 128 if dv % 128 == 0 else dv
    results = pl.pallas_call(
        functools.partial(kernel, dp, mp),
        out_shape=tuple(V(shape, BF16) for shape in shapes),
        in_specs=[smem, any_spec, vmem, any_spec, any_spec, vmem] + [any_spec] * 6,
        out_specs=(vmem,) * len(shapes),
        scratch_shapes=scratch,
        compiler_params=pltpu.CompilerParams(
            collective_id=0, has_side_effects=True, vmem_limit_bytes=67043328 - room
        ),
    )(
        image_slot, vision, vision_gain.reshape(-1, lanes), text_embed.reshape(slots, PATCH, width), w_proj,
        llm_gain[None, :], w_key, w_value, key_grad.reshape(slots, PATCH, kvd), value_grad.reshape(slots, PATCH, kvd),
        key_grad.reshape(slots, dp, rb, kvd), value_grad.reshape(slots, dp, rb, kvd),
    )
    return pl.pallas_call(
        write_out,
        out_shape=tuple(jax.ShapeDtypeStruct(shape, BF16) for shape in shapes),
        in_specs=[vmem] * len(shapes),
        out_specs=(any_spec,) * len(shapes),
        scratch_shapes=[DMA((len(shapes),))],
        compiler_params=pltpu.CompilerParams(vmem_limit_bytes=1 << 20),
    )(*results)


def solution(mesh):
    placed = (
        P(("dp", "mp"), None),
        P(),
        P(),
        P("dp", "mp"),
        P(None, "mp"),
        P("mp"),
        P("mp", None),
        P("mp", None),
        P("dp", "mp"),
        P("dp", "mp"),
    )
    return jax.shard_map(
        shards,
        mesh=mesh,
        in_specs=placed,
        out_specs=(P("dp", "mp"), P("dp", "mp"), P("dp", "mp"), P(("dp", "mp"), None)),
        check_vma=False,
    )
```

```python
import functools

import jax
import jax.numpy as jnp
from jax import lax
from jax.experimental import pallas as pl
from jax.experimental.pallas import tpu as pltpu
from jax.sharding import PartitionSpec as P

PATCH = 256
F32 = jnp.float32
BF16 = jnp.bfloat16
NT = (((1,), (1,)), ((), ()))
DMA = pltpu.SemaphoreType.DMA


def nt(a, b):
    return lax.dot_general(a, b, NT, preferred_element_type=F32)


def remote(src, dst, send_sem, recv_sem, device):
    return pltpu.make_async_remote_copy(
        src_ref=src, dst_ref=dst, send_sem=send_sem, recv_sem=recv_sem,
        device_id=device, device_id_type=pl.DeviceIdType.MESH,
    )


def to_rows(sq, inner):
    lane = lax.broadcasted_iota(jnp.int32, (sq.shape[0], 128), 1)
    wide = jnp.where(lane == 0, sq, jnp.where(lane == 1, inner, 0.0))
    return jnp.transpose(wide)[:8]


def to_columns(rows):
    wide = jnp.transpose(jnp.concatenate([rows] * 16, axis=0))
    return wide[:, 0:1], wide[:, 1:2]


def gain_row(ref):
    if ref.shape[0] == 1:
        return ref[...]
    return jnp.concatenate([ref[i:i + 1, :] for i in range(ref.shape[0])], axis=1)


def vis_cuts(dv):
    if dv % 128:
        return (0, dv)
    units = dv // 128
    first = max(units // 12, 1)
    cuts = [0, first, min(2 * first, units)]
    while cuts[-1] < units:
        cuts.append(min(cuts[-1] + 2 * first, units))
    if len(cuts) > 3 and cuts[-1] - cuts[-2] < first:
        del cuts[-2]
    return tuple(128 * c for c in cuts)


def write_out(*refs):
    count = (len(refs) - 1) // 2
    copies = [pltpu.make_async_copy(refs[n], refs[count + n], refs[-1].at[n]) for n in range(count)]
    for copy in copies:
        copy.start()
    for copy in copies:
        copy.wait()


def kernel(
    dp, mp, slot_ref, vision_h, vgain, text_h, wp_h, gain, wk_h, wv_h, kg_h, vg_h, kg4, vg4,
    k_out, v_out, tg, vg_out,
    vis, vis_all, text, wp, wk, wv, xt, gk, gv, gik, giv, emb, xi, dimg, dg,
    t_send, t_own, t_l1, t_s2, t_l2, i_send, i_own, i_l1, i_s2, i_l2,
    d_send, d_own, d_l1, d_s2, d_l2,
    st_t, sr_t, st_i, sr_i, st_q, sr_q, sc_t, co_t, sc_i, co_i,
    kgs, vgs, kb_send, kb_y, kbr, tb_send, tb_recv, tb_sel, tb_y,
    r1k, r1v, s2k, s2v, r2k, r2v, kvb, r3, s4, s5, r4,
    load_sem, ag_s, ag_r, rs_s, rs_r, rs1_r, t2_r, st_s, st_r, dv_s, dv_r,
    a1_s, a1_r, a2_s, a2_r, b1_s, b1_r, b2_s, b2_r, b3_s, b3_r, kby_s, kby_r, kbz_s, kbz_r, kbp_s, kbp_r,
    tbz_s, tbz_r, tby_s, tby_r, dt,
):
    me_d = lax.axis_index("dp")
    me = lax.axis_index("mp")
    ycount = mp // 2
    core = lax.rem(me, 2)
    y = lax.div(me, 2)
    partner = y * 2 + (1 - core)
    slots, _, width = text.shape
    tokens = slots * PATCH
    kvd = gk.shape[1] // mp
    rows = vis.shape[0]
    dv = vis.shape[1]
    d_model = width * mp
    rb = r1k.shape[1]
    img_rows = mp * rows
    t_pieces = 2
    piece_rows = PATCH // t_pieces

    def ynext(k):
        return lax.rem(y + k, ycount)

    def yprev(k):
        return lax.rem(y + ycount - k, ycount)

    def dnext(k):
        return lax.rem(me_d + k, dp)

    def dprev(k):
        return lax.rem(me_d + dp - k, dp)

    def col(m):
        return pl.ds(pl.multiple_of(m * kvd, kvd), kvd)

    def is_filled(slot):
        found = jnp.int32(0)
        for i in range(dp):
            found = jnp.where(slot_ref[i] == slot, jnp.int32(1), found)
        return found

    def owner_of(slot):
        found = jnp.int32(0)
        for i in range(dp):
            found = jnp.where(slot_ref[i] == slot, jnp.int32(i), found)
        return found

    def holds(s):
        return is_filled(me_d * slots + s)

    inner = 2
    outer = dp // inner
    my_inner = lax.rem(me_d, inner)
    my_outer = lax.div(me_d, inner)

    barrier = pltpu.get_barrier_semaphore()

    @pl.loop(1, dp)
    def _(k):
        pl.semaphore_signal(barrier, inc=1, device_id=(dnext(k), me), device_id_type=pl.DeviceIdType.MESH)

    for k in range(1, mp):
        pl.semaphore_signal(
            barrier, inc=1, device_id=(me_d, lax.rem(me + k, mp)), device_id_type=pl.DeviceIdType.MESH
        )

    sends = []

    def send(*args):
        copy = remote(*args)
        copy.start()
        sends.append(copy)

    def start(*args):
        remote(*args).start()

    loads = [
        (vision_h, vis), (kg_h, kgs), (vg_h, vgs),
        (text_h, text), (wk_h, wk), (wv_h, wv), (wp_h, wp),
        (kg4.at[:, me_d], r1k.at[pl.ds(me_d * slots, slots)]),
        (vg4.at[:, me_d], r1v.at[pl.ds(me_d * slots, slots)]),
    ]
    loads = [pltpu.make_async_copy(a, b, load_sem.at[n]) for n, (a, b) in enumerate(loads)]
    for copy in loads:
        copy.start()

    pl.semaphore_wait(barrier, dp - 1 + mp - 1)
    mine = pl.ds(me_d * slots, slots)
    others = pl.ds(0, dp - 1)

    def a1(k, which):
        src, dst = ((kg4, r1k), (vg4, r1v))[which]
        return remote(
            src.at[:, dnext(k)], dst.at[mine], a1_s.at[which], a1_r.at[which], (dnext(k), me)
        )

    @pl.loop(1, dp)
    def _(k):
        a1(k, 0).start()
        a1(k, 1).start()


    def gather_start(g, block):
        for k in range(1, ycount):
            send(block(me), block(me), ag_s.at[g, k], ag_r.at[g, k], (me_d, ynext(k) * 2 + core))
        send(block(me), block(me), ag_s.at[g, 0], ag_r.at[g, 0], (me_d, partner))

    def arrived(block, send_sem, recv_sem):
        remote(block, block, send_sem, recv_sem, (me_d, partner)).wait_recv()

    def gather_relay(g, block):
        for k in range(1, ycount):
            got = block(yprev(k) * 2 + core)
            arrived(got, ag_s.at[g, k], ag_r.at[g, k])
            send(got, got, ag_s.at[g, ycount + k - 1], ag_r.at[g, ycount + k - 1], (me_d, partner))

    def gather_finish(g, block):
        arrived(block(partner), ag_s.at[g, 0], ag_r.at[g, 0])
        for k in range(1, ycount):
            arrived(block(yprev(k) * 2 + 1 - core), ag_s.at[g, ycount + k - 1], ag_r.at[g, ycount + k - 1])

    vis_block = lambda m: vis_all.at[m]
    gk_block = lambda m: gk.at[:, col(m)]
    gv_block = lambda m: gv.at[:, col(m)]
    gik_block = lambda m: gik.at[:, col(m)]
    giv_block = lambda m: giv.at[:, col(m)]

    loads[0].wait()
    vf = vis[...].astype(F32)
    vscale = lax.rsqrt(jnp.mean(vf * vf, axis=1, keepdims=True) + 1e-06)
    vis_gain = gain_row(vgain)
    vis_all[me] = (vf * vscale * vis_gain).astype(BF16)
    gather_start(0, vis_block)

    first_holds, second_holds = holds(0), holds(1)
    turned = first_holds * (1 - second_holds)
    slot_at = (turned, 1 - turned)
    place_of = (turned, 1 - turned)
    filled = (first_holds.astype(F32), second_holds.astype(F32))
    keeps = (1.0 - filled[0] * filled[1], (1.0 - filled[0]) * (1.0 - filled[1]))

    loads[1].wait()
    loads[2].wait()
    for p in range(slots):
        gk[p * PATCH:(p + 1) * PATCH, col(me)] = kgs[slot_at[p]]
        gv[p * PATCH:(p + 1) * PATCH, col(me)] = vgs[slot_at[p]]
    first_rows = pl.ds(0, PATCH)
    later_rows = pl.ds(PATCH, PATCH)
    gka_block = lambda m: gk.at[first_rows, col(m)]
    gva_block = lambda m: gv.at[first_rows, col(m)]

    def far_start(g, block):
        for k in range(1, ycount):
            send(block(me), block(me), ag_s.at[g, k], ag_r.at[g, k], (me_d, ynext(k) * 2 + core))

    def near_start(g, block):
        send(block(me), block(me), ag_s.at[g, 0], ag_r.at[g, 0], (me_d, partner))

    def near_finish(g, block):
        arrived(block(partner), ag_s.at[g, 0], ag_r.at[g, 0])

    def far_finish(g, block):
        for k in range(1, ycount):
            arrived(block(yprev(k) * 2 + 1 - core), ag_s.at[g, ycount + k - 1], ag_r.at[g, ycount + k - 1])

    def heads(yk):
        return pl.ds(pl.multiple_of(yk * 2 * kvd, 2 * kvd), 2 * kvd)

    def products(keys, values, at, cs, yk):
        at_heads = heads(yk)
        return nt(keys[at, at_heads], wk[cs, at_heads]) + nt(values[at, at_heads], wv[cs, at_heads])

    def turned_products(keys, values, at, cs, yk):
        at_heads = heads(yk)
        return nt(wk[cs, at_heads], keys[at, at_heads]) + nt(wv[cs, at_heads], values[at, at_heads])

    def far_products(keys, values, at, cs):
        total = turned_products(keys, values, at, cs, ynext(1))
        for k in range(2, ycount):
            total = total + turned_products(keys, values, at, cs, ynext(k))
        return jnp.transpose(total)

    step = 256
    big = min(1024, width)
    every = pl.ds(0, tokens)
    image_rows = pl.ds(0, img_rows)

    far_start(1, gka_block)
    far_start(2, gva_block)
    near_start(1, gk_block)
    near_start(2, gv_block)

    def chunk(x, m):
        k_part = jnp.dot(x[...], wk[:, col(m)], preferred_element_type=F32)
        v_part = jnp.dot(x[...], wv[:, col(m)], preferred_element_type=F32)
        return k_part, v_part

    def stage_send(x, n, psend, l1):
        for k in range(ycount):
            yk = ynext(k)
            k_part, v_part = chunk(x, yk * 2 + 1 - core)
            shape = psend.shape[1:-1] + (kvd,)
            psend[yk, ..., :kvd] = k_part.astype(BF16).reshape(shape)
            psend[yk, ..., kvd:] = v_part.astype(BF16).reshape(shape)
            start(psend.at[yk], l1.at[yk], rs_s.at[n, 0], rs_r.at[n, k], (me_d, partner))

    def stage_own(x, own):
        for k in range(ycount):
            yk = ynext(k)
            k_part, v_part = chunk(x, yk * 2 + core)
            shape = own.shape[1:-1] + (kvd,)
            own[yk, ..., :kvd] = k_part.reshape(shape)
            own[yk, ..., kvd:] = v_part.reshape(shape)

    def level_two(n, own, l1, s2, l2):
        for k in range(ycount - 1, 0, -1):
            yk = ynext(k)
            arrived(l1.at[yk], rs_s.at[n, 0], rs_r.at[n, k])
            s2[k] = (own[yk] + l1[yk].astype(F32)).astype(BF16)

    def level_go(n, s2, l2):
        for k in range(ycount - 1, 0, -1):
            for h in range(2):
                at = pl.ds(h * kvd, kvd)
                start(
                    s2.at[k, :, at], l2.at[k, :, at], rs_s.at[n, k], rs1_r.at[k - 1, h],
                    (me_d, ynext(k) * 2 + core),
                )

    def text_piece(p, k):
        at = pl.ds(p * piece_rows, piece_rows)
        return remote(
            t_s2.at[k, at], t_l2.at[k, at], rs_s.at[0, k], t2_r.at[k - 1, p], (me_d, ynext(k) * 2 + core)
        )

    def text_go(p):
        for k in range(ycount - 1, 0, -1):
            text_piece(p, k).start()

    def stats_send(n, st, sr):
        for k in range(1, mp):
            start(st, sr.at[k], st_s.at[n], st_r.at[n], (me_d, lax.rem(me + k, mp)))

    def stats_total(n, st, sr):
        total = st[...]
        arrived(sr.at[pl.ds(1, mp - 1)], st_s.at[n], st_r.at[n])
        for k in range(1, mp):
            total = total + sr[k]
        return to_columns(total)

    def wide(p):
        return jnp.concatenate([p] * (step // 128), axis=1)

    def fold(p):
        total = p[:, :128]
        for n in range(1, p.shape[1] // 128):
            total = total + p[:, n * 128:(n + 1) * 128]
        return total

    loads[3].wait()
    for p in range(slots):
        tf = text[slot_at[p]].astype(F32)
        sc_t[p] = fold(tf * tf)
        xt[p * PATCH:(p + 1) * PATCH, :] = (tf * gain[...]).astype(BF16)
    loads[4].wait()
    loads[5].wait()
    stage_send(xt, 0, t_send, t_l1)
    stage_own(xt, t_own)
    for k in range(ycount - 1, 0, -1):
        yk = ynext(k)
        arrived(t_l1.at[yk], rs_s.at[0, 0], rs_r.at[0, k])
        t_s2[k] = (t_own[yk, 0] + t_l1[yk, 0].astype(F32)).astype(BF16)
        rest = t_own[yk, 1] + t_l1[yk, 1].astype(F32)
        tb_send[:, k - 1] = rest.reshape(dp, rb, 2 * kvd).astype(BF16)
    tb_recv[me_d] = tb_send[me_d]
    near_finish(1, gk_block)
    near_finish(2, gv_block)

    def text_near(j, _):
        cs = pl.ds(pl.multiple_of(j * step, step), step)
        dt[:, :, cs] = products(gk, gv, every, cs, y).reshape(slots, PATCH, step)
        return 0

    lax.fori_loop(0, width // step // 2, text_near, 0)
    lax.fori_loop(width // step // 2, width // step, text_near, 0)
    co_t[...] = jnp.zeros(co_t.shape, F32)
    gather_relay(0, vis_block)
    def survey(d, found):
        count = jnp.int32(0)
        for i in range(dp):
            count = count + jnp.where(lax.div(slot_ref[i], jnp.int32(slots)) == d, jnp.int32(1), jnp.int32(0))
        return jnp.where(count == 0, d, found[0]), jnp.where(count > 1, d, found[1])

    lone, crowded = lax.fori_loop(0, dp, survey, (jnp.int32(0), jnp.int32(0)))
    lone_slot = lone * slots + 1
    at_lone = keeps[1]
    loads[7].wait()
    loads[8].wait()

    for which, dst in ((0, r1k), (1, r1v)):
        arrived(dst.at[pl.ds(0, (dp - 1) * slots)], a1_s.at[which], a1_r.at[which])

    @pl.loop(0, dp)
    def _(i):
        s2k[i] = r1k[slot_ref[i]]
        s2v[i] = r1v[slot_ref[i]]

    r2k[me_d] = s2k[me_d]
    r2v[me_d] = s2v[me_d]

    def a2(k, which):
        src, dst = ((s2k, r2k), (s2v, r2v))[which]
        return remote(
            src.at[dnext(k)], dst.at[me_d], a2_s.at[which], a2_r.at[which], (dnext(k), me)
        )

    @pl.loop(1, dp)
    def _(k):
        a2(k, 0).start()
        a2(k, 1).start()

    kb_send[0] = r1k[lone_slot]
    kb_send[1] = r1v[lone_slot]
    for k in range(1, ycount):
        send(kb_send, kb_y.at[k - 1], kby_s.at[k - 1], kby_r.at[k - 1], (me_d, ynext(k) * 2 + core))
    text_go(0)
    gather_finish(0, vis_block)
    loads[6].wait()

    sc_i[...] = jnp.zeros(sc_i.shape, F32)

    def project(j, _):
        cs = pl.ds(pl.multiple_of(j * step, step), step)
        e = jnp.concatenate([vis_all[m] for m in range(mp)], axis=0)
        e = jnp.dot(e, wp[:, cs], preferred_element_type=F32).astype(BF16)
        emb[:, cs] = e
        ef = e.astype(F32)
        xi[:, cs] = (ef * gain[:, cs]).astype(BF16)
        sc_i[...] += fold(ef * ef)
        return 0

    lax.fori_loop(0, width // step, project, 0)
    for k in range(1, ycount):
        arrived(kb_y.at[k - 1], kby_s.at[k - 1], kby_r.at[k - 1])
    kbr[me_d] = kb_y[...]

    def kbz(k):
        return remote(kb_y, kbr.at[me_d], kbz_s.at[0], kbz_r.at[0], (dnext(k), me))

    def tbz(k):
        return remote(tb_send.at[dnext(k)], tb_recv.at[me_d], tbz_s.at[0], tbz_r.at[0], (dnext(k), me))

    @pl.loop(1, dp)
    def _(k):
        kbz(k).start()

    @pl.loop(1, dp)
    def _(k):
        tbz(k).start()

    gather_relay(1, gka_block)
    gather_relay(2, gva_block)
    zero = jnp.zeros((img_rows, 1), F32)
    st_q[...] = to_rows(jnp.sum(sc_i[...], axis=1, keepdims=True), zero)
    stats_send(2, st_q, sr_q)

    for which, dst in ((0, r2k), (1, r2v)):
        arrived(dst.at[others], a2_s.at[which], a2_r.at[which])

    own_k = r2k[...].astype(F32).reshape(PATCH, kvd)
    own_v = r2v[...].astype(F32).reshape(PATCH, kvd)
    gik[:, col(me)] = own_k.astype(BF16)
    giv[:, col(me)] = own_v.astype(BF16)
    gather_start(3, gik_block)
    gather_start(4, giv_block)
    stage_send(xi, 1, i_send, i_l1)
    stage_own(xi, i_own)
    level_two(1, i_own, i_l1, i_s2, i_l2)
    level_go(1, i_s2, i_l2)
    far_finish(1, gka_block)
    far_finish(2, gva_block)

    def text_far(p):
        rows_p = pl.ds(p * PATCH, PATCH)

        def body(j, _):
            cs = pl.ds(pl.multiple_of(j * big, big), big)
            d = (dt[p, :, cs] + far_products(gk, gv, rows_p, cs)) * gain[:, cs]
            dt[p, :, cs] = d
            co_t[p] += fold(d * text[slot_at[p], :, cs].astype(F32))
            return 0

        lax.fori_loop(0, width // big, body, 0)

    text_far(0)
    near_finish(3, gik_block)
    near_finish(4, giv_block)

    def image_near(j, _):
        cs = pl.ds(pl.multiple_of(j * big, big), big)
        dg[:, cs] = jnp.transpose(turned_products(gik, giv, image_rows, cs, y))
        return 0

    lax.fori_loop(0, width // big, image_near, 0)
    gather_relay(3, gik_block)
    gather_relay(4, giv_block)
    co_i[...] = jnp.zeros(co_i.shape, F32)

    arrived(kbr.at[others], kbz_s.at[0], kbz_r.at[0])

    for k in range(1, ycount):
        m = yprev(k) * 2 + core
        for which, g in ((0, gk), (1, gv)):
            g[later_rows, col(m)] = kbr[:, k - 1, which].astype(F32).reshape(PATCH, kvd).astype(BF16)
            send(
                g.at[later_rows, col(m)], g.at[later_rows, col(m)], kbp_s.at[which, k - 1], kbp_r.at[which, k - 1],
                (me_d, partner),
            )
    far_finish(3, gik_block)
    far_finish(4, giv_block)

    def image_far(j, _):
        cs = pl.ds(pl.multiple_of(j * big, big), big)
        d = (dg[:, cs] + far_products(gik, giv, image_rows, cs)) * gain[:, cs]
        dg[:, cs] = d
        co_i[...] += fold(d * emb[:, cs].astype(F32))
        return 0

    lax.fori_loop(0, width // big, image_far, 0)
    st_i[...] = to_rows(zero, jnp.sum(co_i[...], axis=1, keepdims=True))
    stats_send(1, st_i, sr_i)
    text_go(1)
    sq_i, _ = stats_total(2, st_q, sr_q)
    scale_i = lax.rsqrt(sq_i / d_model + 1e-05)
    sc_i[...] = jnp.broadcast_to(scale_i, sc_i.shape)

    def b1(k, h):
        return remote(kvb.at[h, dnext(k)], r3.at[me_d, h], b1_s.at[h], b1_r.at[h], (dnext(k), me))

    def image_sums(h):
        at = pl.ds(h * kvd, kvd)
        total = i_own[y, :, at] + i_l1[y, :, at].astype(F32)
        for k in range(1, ycount):
            arrived(i_l2.at[k, :, at], rs_s.at[1, k], rs1_r.at[k - 1, h])
            total = total + i_l2[k, :, at].astype(F32)
        kvb[h] = (total * sc_i[:, 0:1]).reshape(dp, rb, kvd).astype(BF16)
        r3[me_d, h] = kvb[h, me_d]

        @pl.loop(1, dp)
        def _(k):
            b1(k, h).start()

    arrived(i_l1.at[y], rs_s.at[1, 0], rs_r.at[1, 0])
    image_sums(0)
    for k in range(1, ycount):
        for which, g in ((0, gk), (1, gv)):
            arrived(g.at[later_rows, col(yprev(k) * 2 + 1 - core)], kbp_s.at[which, k - 1], kbp_r.at[which, k - 1])
    text_far(1)
    image_sums(1)
    st_t[...] = to_rows(
        jnp.sum(sc_t[...].reshape(tokens, 128), axis=1, keepdims=True),
        jnp.sum(co_t[...].reshape(tokens, 128), axis=1, keepdims=True),
    )
    stats_send(0, st_t, sr_t)

    arrived(tb_recv.at[others], tbz_s.at[0], tbz_r.at[0])

    tb_sel[...] = tb_recv[lone]
    for k in range(1, ycount):
        send(tb_sel.at[k - 1], tb_y.at[k - 1], tby_s.at[k - 1], tby_r.at[k - 1], (me_d, ynext(k) * 2 + core))
    _, inner_i = stats_total(1, st_i, sr_i)
    scale_i = sc_i[:, 0:1]
    co_i[...] = jnp.broadcast_to(scale_i * scale_i * scale_i * (inner_i / d_model), co_i.shape)

    def image_end(j, _):
        cs = pl.ds(pl.multiple_of(j * step, step), step)
        d = wide(sc_i[...]) * dg[:, cs] - emb[:, cs].astype(F32) * wide(co_i[...])
        dimg[:, cs] = d.astype(BF16)
        return 0

    lax.fori_loop(0, width // step, image_end, 0)
    cuts = vis_cuts(dv)
    pieces = len(cuts) - 1

    def vis_chunk(j):
        at = pl.ds(cuts[j], cuts[j + 1] - cuts[j])
        d = nt(dimg[...], wp[at, :]).reshape(ycount, 2, rows, cuts[j + 1] - cuts[j])
        for yi in range(ycount):
            a, b = d[yi, 0], d[yi, 1]
            first = core == 0
            d_own[yi, :, at] = jnp.where(first, a, b)
            d_send[yi, :, at] = jnp.where(first, b, a).astype(BF16)
        start(d_send.at[:, :, at], d_l1.at[:, :, at], dv_s.at[0], dv_r.at[j, 0], (me_d, partner))

    def vis_two(j):
        at = pl.ds(cuts[j], cuts[j + 1] - cuts[j])
        arrived(d_l1.at[:, :, at], dv_s.at[0], dv_r.at[j, 0])
        for k in range(1, ycount):
            yk = ynext(k)
            d_s2[k, :, at] = (d_own[yk, :, at] + d_l1[yk, :, at].astype(F32)).astype(BF16)
            start(d_s2.at[k, :, at], d_l2.at[k, :, at], dv_s.at[k], dv_r.at[j, k], (me_d, yk * 2 + core))

    def b2(k):
        return remote(s4.at[dnext(k)], r4.at[0, my_inner, my_outer], b2_s.at[0], b2_r.at[0], (dnext(k), me))

    def b3(k):
        target = lax.rem(my_outer + k, outer) * inner + my_inner
        return remote(s5, r4.at[1, my_inner, my_outer], b3_s.at[0], b3_r.at[k], (target, me))

    def b4(k):
        block = r4.at[1, my_inner, lax.rem(my_outer + outer - k, outer)]
        return remote(block, block, b3_s.at[1], b3_r.at[0], (my_outer * inner + 1 - my_inner, me))

    for j in range(pieces):
        vis_chunk(j)
        if j > 0:
            vis_two(j - 1)
        if j == min(4, pieces - 1):

            for h in range(2):
                arrived(r3.at[others, h], b1_s.at[h], b1_r.at[h])

            extra = jnp.zeros((rb, 2 * kvd), F32)
            for k in range(1, ycount):
                arrived(tb_y.at[k - 1], tby_s.at[k - 1], tby_r.at[k - 1])
                extra = extra + tb_y[k - 1].astype(F32)
            r3[dp, 0] = extra[:, :kvd].astype(BF16)
            r3[dp, 1] = extra[:, kvd:].astype(BF16)

            @pl.loop(0, dp)
            def _(d):
                source = owner_of(d * slots + 1)
                source = jnp.where(is_filled(d * slots) == 1, owner_of(d * slots), source)
                source = jnp.where(d == lone, jnp.int32(dp), source)
                s4[d, :, :kvd] = r3[source, 0]
                s4[d, :, kvd:] = r3[source, 1]

            source = owner_of(crowded * slots + 1)
            s5[:, :kvd] = r3[source, 0]
            s5[:, kvd:] = r3[source, 1]
            r4[0, my_inner, my_outer] = s4[me_d]
            r4[1, my_inner, my_outer] = s5[...]

            for k in range(1, outer):
                b3(k).start()

            @pl.loop(1, dp)
            def _(k):
                b2(k).start()

            start(s5, r4.at[1, my_inner, my_outer], b3_s.at[1], b3_r.at[0], (my_outer * inner + 1 - my_inner, me))

    vis_two(pieces - 1)
    for k in range(1, outer):
        arrived(r4.at[1, my_inner, lax.rem(my_outer + outer - k, outer)], b3_s.at[0], b3_r.at[k])
        b4(k).start()
    sq_t, inner_t = stats_total(0, st_t, sr_t)
    keep = jnp.concatenate([jnp.full((PATCH, 1), 1.0, F32) * keeps[p] for p in range(slots)], axis=0)
    scale_t = lax.rsqrt(sq_t / d_model + 1e-05)
    sc_t[...] = jnp.broadcast_to(scale_t * keep, (tokens, 128)).reshape(sc_t.shape)
    co_t[...] = jnp.broadcast_to(
        scale_t * scale_t * scale_t * (inner_t / d_model) * keep, (tokens, 128)
    ).reshape(co_t.shape)

    def text_back(j, _):
        cs = pl.ds(pl.multiple_of(j * step, step), step)
        for s in range(slots):
            at = place_of[s]
            d = wide(sc_t[at]) * dt[at, :, cs] - text[s, :, cs].astype(F32) * wide(co_t[at])
            tg[s * PATCH:(s + 1) * PATCH, cs] = d.astype(BF16)
        return 0

    lax.fori_loop(0, width // step, text_back, 0)
    arrived(t_l1.at[y], rs_s.at[0, 0], rs_r.at[0, 0])
    for p in range(t_pieces):
        for k in range(1, ycount):
            text_piece(p, k).wait_recv()
    direct = t_l2[1].astype(F32)
    for k in range(2, ycount):
        direct = direct + t_l2[k].astype(F32)
    for s in range(slots):
        at = place_of[s]
        total = t_own[y, at] + t_l1[y, at].astype(F32) + direct * (1.0 - at.astype(F32))
        dt[s, :, :2 * kvd] = total * sc_t[at][:, 0:1]
    vf = vis[...].astype(F32)
    vscale = lax.rsqrt(jnp.mean(vf * vf, axis=1, keepdims=True) + 1e-06)
    row_gain = gain_row(vgain)
    lanes = jnp.zeros((rows, 128), F32)
    for j in range(pieces):
        at = pl.ds(cuts[j], cuts[j + 1] - cuts[j])
        d = d_own[y, :, at] + d_l1[y, :, at].astype(F32)
        for k in range(1, ycount):
            arrived(d_l2.at[k, :, at], dv_s.at[k], dv_r.at[j, k])
            d = d + d_l2[k, :, at].astype(F32)
        h = d.astype(BF16).astype(F32) * row_gain[:, cuts[j]:cuts[j + 1]]
        d_own[y, :, at] = h
        lanes = lanes + fold(h * vis[:, at].astype(F32))
    v_inner = jnp.sum(lanes, axis=1, keepdims=True) / dv
    vg_out[...] = (vscale * d_own[y] - vf * (vscale * vscale * vscale * v_inner)).astype(BF16)

    arrived(s4.at[others], b2_s.at[0], b2_r.at[0])
    arrived(r4.at[1, 1 - my_inner], b3_s.at[1], b3_r.at[0])

    for s in range(slots):
        which = s * first_holds * second_holds
        placed = jnp.concatenate([r4[which, r % inner, r // inner] for r in range(dp)], axis=0).astype(F32)
        share = sc_t[place_of[s]][:, 0:1] * (place_of[s].astype(F32) * at_lone) + filled[s]
        out = dt[s, :, :2 * kvd] + placed * share
        rows_s = pl.ds(s * PATCH, PATCH)
        k_out[rows_s, :] = out[:, :kvd].astype(BF16)
        v_out[rows_s, :] = out[:, kvd:].astype(BF16)
    for copy in sends:
        copy.wait_send()

    def sent(block, sem):
        remote(block, block, sem, ag_r.at[0, 0], (me_d, partner)).wait_send()

    for which, (first, second) in enumerate(((kg4, s2k), (vg4, s2v))):
        sent(first.at[:, others], a1_s.at[which])
        sent(second.at[others], a2_s.at[which])
    for h in range(2):
        sent(kvb.at[h, others], b1_s.at[h])
    sent(s4.at[others], b2_s.at[0])
    sent(r4.at[1, my_inner, pl.ds(0, outer - 1)], b3_s.at[0])
    sent(r4.at[1, my_inner], b3_s.at[1])
    sent(kbr.at[others], kbz_s.at[0])
    sent(tb_send.at[others], tbz_s.at[0])
    sent(t_send, rs_s.at[0, 0])
    sent(i_send, rs_s.at[1, 0])
    sent(d_send, dv_s.at[0])
    for k in range(1, ycount):
        sent(t_s2.at[k], rs_s.at[0, k])
        sent(i_s2.at[k], rs_s.at[1, k])
        sent(d_s2.at[k], dv_s.at[k])
    for n, sr in enumerate((sr_t, sr_i, sr_q)):
        sent(sr.at[pl.ds(0, mp - 1)], st_s.at[n])


def shards(vision, vision_gain, image_slot, text_embed, w_proj, llm_gain, w_key, w_value, key_grad, value_grad):
    dp = lax.axis_size("dp")
    mp = lax.axis_size("mp")
    tokens, width = text_embed.shape
    slots = tokens // PATCH
    rows, dv = vision.shape
    kvd = key_grad.shape[1]
    kv = kvd * mp
    img = rows * mp
    rb = PATCH // dp
    ys = mp // 2
    pieces = len(vis_cuts(dv)) - 1
    V = pltpu.VMEM
    any_spec = pl.BlockSpec(memory_space=pl.ANY)
    vmem = pl.BlockSpec(memory_space=pltpu.VMEM)
    smem = pl.BlockSpec(memory_space=pltpu.SMEM)
    scratch = [
        V((rows, dv), BF16), V((mp, rows, dv), BF16), V((slots, PATCH, width), BF16), V((dv, width), BF16),
        V((width, kv), BF16), V((width, kv), BF16), V((tokens, width), BF16),
        V((tokens, kv), BF16), V((tokens, kv), BF16), V((img, kv), BF16), V((img, kv), BF16),
        V((img, width), BF16), V((img, width), BF16), V((img, width), BF16), V((img, width), F32),
    ]
    t_shape = (ys, slots, PATCH, 2 * kvd)
    i_shape = (ys, img, 2 * kvd)
    half = (ys, PATCH, 2 * kvd)
    scratch += [V(t_shape, BF16), V(t_shape, F32), V(t_shape, BF16), V(half, BF16), V(half, BF16)]
    scratch += [V(i_shape, BF16), V(i_shape, F32), V(i_shape, BF16), V(i_shape, BF16), V(i_shape, BF16)]
    scratch += [
        V((ys, rows, dv), BF16), V((ys, rows, dv), F32), V((ys, rows, dv), BF16), V((ys, rows, dv), BF16),
        V((ys, rows, dv), BF16),
        V((8, tokens), F32), V((mp, 8, tokens), F32), V((8, img), F32), V((mp, 8, img), F32),
        V((8, img), F32), V((mp, 8, img), F32),
        V((slots, PATCH, 128), F32), V((slots, PATCH, 128), F32), V((img, 128), F32), V((img, 128), F32),
        V((slots, PATCH, kvd), BF16), V((slots, PATCH, kvd), BF16),
        V((2, rb, kvd), BF16), V((ys - 1, 2, rb, kvd), BF16), V((dp, ys - 1, 2, rb, kvd), BF16),
        V((dp, ys - 1, rb, 2 * kvd), BF16), V((dp, ys - 1, rb, 2 * kvd), BF16),
        V((ys - 1, rb, 2 * kvd), BF16), V((ys - 1, rb, 2 * kvd), BF16),
        V((dp * slots, rb, kvd), BF16), V((dp * slots, rb, kvd), BF16),
        V((dp, rb, kvd), BF16), V((dp, rb, kvd), BF16), V((dp, rb, kvd), BF16), V((dp, rb, kvd), BF16),
        V((2, dp, rb, kvd), BF16), V((dp + 1, 2, rb, kvd), BF16),
        V((dp, rb, 2 * kvd), BF16), V((rb, 2 * kvd), BF16), V((2, 2, dp // 2, rb, 2 * kvd), BF16),
        DMA((9,)), DMA((5, 2 * ys - 1)), DMA((5, 2 * ys - 1)), DMA((2, ys)), DMA((2, ys)), DMA((ys - 1, 2)),
        DMA((ys - 1, 2)), DMA((3,)), DMA((3,)), DMA((ys,)), DMA((pieces, ys)),
        DMA((2,)), DMA((2,)), DMA((2,)), DMA((2,)),
        DMA((2,)), DMA((2,)), DMA((1,)), DMA((1,)), DMA((2,)), DMA((dp // 2,)),
        DMA((ys - 1,)), DMA((ys - 1,)), DMA((1,)), DMA((1,)), DMA((2, ys - 1)), DMA((2, ys - 1)),
        DMA((1,)), DMA((1,)), DMA((ys - 1,)), DMA((ys - 1,)), V((slots, PATCH, width), F32),
    ]
    shapes = ((tokens, kvd), (tokens, kvd), (tokens, width), (rows, dv))
    room = sum(2 * a * b for a, b in shapes)
    lanes = 128 if dv % 128 == 0 else dv
    results = pl.pallas_call(
        functools.partial(kernel, dp, mp),
        out_shape=tuple(V(shape, BF16) for shape in shapes),
        in_specs=[smem, any_spec, vmem, any_spec, any_spec, vmem] + [any_spec] * 6,
        out_specs=(vmem,) * len(shapes),
        scratch_shapes=scratch,
        compiler_params=pltpu.CompilerParams(
            collective_id=0, has_side_effects=True, vmem_limit_bytes=67043328 - room
        ),
    )(
        image_slot, vision, vision_gain.reshape(-1, lanes), text_embed.reshape(slots, PATCH, width), w_proj,
        llm_gain[None, :], w_key, w_value, key_grad.reshape(slots, PATCH, kvd), value_grad.reshape(slots, PATCH, kvd),
        key_grad.reshape(slots, dp, rb, kvd), value_grad.reshape(slots, dp, rb, kvd),
    )
    return pl.pallas_call(
        write_out,
        out_shape=tuple(jax.ShapeDtypeStruct(shape, BF16) for shape in shapes),
        in_specs=[vmem] * len(shapes),
        out_specs=(any_spec,) * len(shapes),
        scratch_shapes=[DMA((len(shapes),))],
        compiler_params=pltpu.CompilerParams(vmem_limit_bytes=1 << 20),
    )(*results)


def solution(mesh):
    placed = (
        P(("dp", "mp"), None),
        P(),
        P(),
        P("dp", "mp"),
        P(None, "mp"),
        P("mp"),
        P("mp", None),
        P("mp", None),
        P("dp", "mp"),
        P("dp", "mp"),
    )
    return jax.shard_map(
        shards,
        mesh=mesh,
        in_specs=placed,
        out_specs=(P("dp", "mp"), P("dp", "mp"), P("dp", "mp"), P(("dp", "mp"), None)),
        check_vma=False,
    )
```

```python
import functools

import jax
import jax.numpy as jnp
from jax import lax
from jax.experimental import pallas as pl
from jax.experimental.pallas import tpu as pltpu
from jax.sharding import PartitionSpec as P

PATCH = 256
F32 = jnp.float32
BF16 = jnp.bfloat16
NT = (((1,), (1,)), ((), ()))
DMA = pltpu.SemaphoreType.DMA


def nt(a, b):
    return lax.dot_general(a, b, NT, preferred_element_type=F32)


def remote(src, dst, send_sem, recv_sem, device):
    return pltpu.make_async_remote_copy(
        src_ref=src, dst_ref=dst, send_sem=send_sem, recv_sem=recv_sem,
        device_id=device, device_id_type=pl.DeviceIdType.MESH,
    )


def to_rows(sq, inner):
    lane = lax.broadcasted_iota(jnp.int32, (sq.shape[0], 128), 1)
    wide = jnp.where(lane == 0, sq, jnp.where(lane == 1, inner, 0.0))
    return jnp.transpose(wide)[:8]


def to_columns(rows):
    wide = jnp.transpose(jnp.concatenate([rows] * 16, axis=0))
    return wide[:, 0:1], wide[:, 1:2]


def gain_row(ref):
    if ref.shape[0] == 1:
        return ref[...]
    return jnp.concatenate([ref[i:i + 1, :] for i in range(ref.shape[0])], axis=1)


def vis_cuts(dv):
    if dv % 128:
        return (0, dv)
    units = dv // 128
    first = max(units // 12, 1)
    cuts = [0, first, min(2 * first, units)]
    while cuts[-1] < units:
        cuts.append(min(cuts[-1] + 2 * first, units))
    if len(cuts) > 3 and cuts[-1] - cuts[-2] < first:
        del cuts[-2]
    return tuple(128 * c for c in cuts)


def write_out(*refs):
    count = (len(refs) - 1) // 2
    copies = [pltpu.make_async_copy(refs[n], refs[count + n], refs[-1].at[n]) for n in range(count)]
    for copy in copies:
        copy.start()
    for copy in copies:
        copy.wait()


def kernel(
    dp, mp, slot_ref, vision_h, vgain, text_h, wp_h, gain, wk_h, wv_h, kg_h, vg_h, kg4, vg4,
    k_out, v_out, tg, vg_out,
    vis, vis_all, text, wp, wk, wv, xt, gk, gv, gik, giv, emb, xi, dimg, dg,
    t_send, t_own, t_l1, t_s2, t_l2, i_send, i_own, i_l1, i_s2, i_l2,
    d_send, d_own, d_l1, d_s2, d_l2,
    st_t, sr_t, st_i, sr_i, st_q, sr_q, sc_t, co_t, sc_i, co_i,
    kgs, vgs, kb_send, kb_y, kbr, tb_send, tb_recv, tb_sel, tb_y,
    r1k, r1v, s2k, s2v, r2k, r2v, kvb, r3, s4, s5, r4, sources,
    load_sem, ag_s, ag_r, rs_s, rs_r, rs1_r, t2_r, st_s, st_r, dv_s, dv_r,
    a1_s, a1_r, a2_s, a2_r, b1_s, b1_r, b2_s, b2_r, b3_s, b3_r, kby_s, kby_r, kbz_s, kbz_r, kbp_s, kbp_r,
    tbz_s, tbz_r, tby_s, tby_r, dt,
):
    me_d = lax.axis_index("dp")
    me = lax.axis_index("mp")
    ycount = mp // 2
    core = lax.rem(me, 2)
    y = lax.div(me, 2)
    partner = y * 2 + (1 - core)
    slots, _, width = text.shape
    tokens = slots * PATCH
    kvd = gk.shape[1] // mp
    rows = vis.shape[0]
    dv = vis.shape[1]
    d_model = width * mp
    rb = r1k.shape[1]
    img_rows = mp * rows
    t_pieces = 2
    piece_rows = PATCH // t_pieces

    def ynext(k):
        return lax.rem(y + k, ycount)

    def yprev(k):
        return lax.rem(y + ycount - k, ycount)

    def dnext(k):
        return lax.rem(me_d + k, dp)

    def dprev(k):
        return lax.rem(me_d + dp - k, dp)

    def col(m):
        return pl.ds(pl.multiple_of(m * kvd, kvd), kvd)

    def is_filled(slot):
        found = jnp.int32(0)
        for i in range(dp):
            found = jnp.where(slot_ref[i] == slot, jnp.int32(1), found)
        return found

    def owner_of(slot):
        found = jnp.int32(0)
        for i in range(dp):
            found = jnp.where(slot_ref[i] == slot, jnp.int32(i), found)
        return found

    def holds(s):
        return is_filled(me_d * slots + s)

    inner = 2
    outer = dp // inner
    my_inner = lax.rem(me_d, inner)
    my_outer = lax.div(me_d, inner)

    barrier = pltpu.get_barrier_semaphore()

    @pl.loop(1, dp)
    def _(k):
        pl.semaphore_signal(barrier, inc=1, device_id=(dnext(k), me), device_id_type=pl.DeviceIdType.MESH)

    for k in range(1, mp):
        pl.semaphore_signal(
            barrier, inc=1, device_id=(me_d, lax.rem(me + k, mp)), device_id_type=pl.DeviceIdType.MESH
        )

    sends = []

    def send(*args):
        copy = remote(*args)
        copy.start()
        sends.append(copy)

    def start(*args):
        remote(*args).start()

    loads = [
        (vision_h, vis), (kg_h, kgs), (vg_h, vgs),
        (text_h, text), (wk_h, wk), (wv_h, wv), (wp_h, wp),
        (kg4.at[:, me_d], r1k.at[pl.ds(me_d * slots, slots)]),
        (vg4.at[:, me_d], r1v.at[pl.ds(me_d * slots, slots)]),
    ]
    loads = [pltpu.make_async_copy(a, b, load_sem.at[n]) for n, (a, b) in enumerate(loads)]
    for copy in loads:
        copy.start()

    pl.semaphore_wait(barrier, dp - 1 + mp - 1)
    mine = pl.ds(me_d * slots, slots)
    others = pl.ds(0, dp - 1)

    def a1(k, which):
        src, dst = ((kg4, r1k), (vg4, r1v))[which]
        return remote(
            src.at[:, dnext(k)], dst.at[mine], a1_s.at[which], a1_r.at[which], (dnext(k), me)
        )

    @pl.loop(1, dp)
    def _(k):
        a1(k, 0).start()
        a1(k, 1).start()


    def gather_start(g, block):
        for k in range(1, ycount):
            send(block(me), block(me), ag_s.at[g, k], ag_r.at[g, k], (me_d, ynext(k) * 2 + core))
        send(block(me), block(me), ag_s.at[g, 0], ag_r.at[g, 0], (me_d, partner))

    def arrived(block, send_sem, recv_sem):
        remote(block, block, send_sem, recv_sem, (me_d, partner)).wait_recv()

    def gather_relay(g, block):
        for k in range(1, ycount):
            got = block(yprev(k) * 2 + core)
            arrived(got, ag_s.at[g, k], ag_r.at[g, k])
            send(got, got, ag_s.at[g, ycount + k - 1], ag_r.at[g, ycount + k - 1], (me_d, partner))

    def gather_finish(g, block):
        arrived(block(partner), ag_s.at[g, 0], ag_r.at[g, 0])
        for k in range(1, ycount):
            arrived(block(yprev(k) * 2 + 1 - core), ag_s.at[g, ycount + k - 1], ag_r.at[g, ycount + k - 1])

    vis_block = lambda m: vis_all.at[m]
    gk_block = lambda m: gk.at[:, col(m)]
    gv_block = lambda m: gv.at[:, col(m)]
    gik_block = lambda m: gik.at[:, col(m)]
    giv_block = lambda m: giv.at[:, col(m)]

    loads[0].wait()
    vf = vis[...].astype(F32)
    vscale = lax.rsqrt(jnp.mean(vf * vf, axis=1, keepdims=True) + 1e-06)
    vis_gain = gain_row(vgain)
    vis_all[me] = (vf * vscale * vis_gain).astype(BF16)
    gather_start(0, vis_block)

    first_holds, second_holds = holds(0), holds(1)
    turned = first_holds * (1 - second_holds)
    slot_at = (turned, 1 - turned)
    place_of = (turned, 1 - turned)
    filled = (first_holds.astype(F32), second_holds.astype(F32))
    keeps = (1.0 - filled[0] * filled[1], (1.0 - filled[0]) * (1.0 - filled[1]))

    loads[1].wait()
    loads[2].wait()
    for p in range(slots):
        gk[p * PATCH:(p + 1) * PATCH, col(me)] = kgs[slot_at[p]]
        gv[p * PATCH:(p + 1) * PATCH, col(me)] = vgs[slot_at[p]]
    first_rows = pl.ds(0, PATCH)
    later_rows = pl.ds(PATCH, PATCH)
    gka_block = lambda m: gk.at[first_rows, col(m)]
    gva_block = lambda m: gv.at[first_rows, col(m)]

    def far_start(g, block):
        for k in range(1, ycount):
            send(block(me), block(me), ag_s.at[g, k], ag_r.at[g, k], (me_d, ynext(k) * 2 + core))

    def near_start(g, block):
        send(block(me), block(me), ag_s.at[g, 0], ag_r.at[g, 0], (me_d, partner))

    def near_finish(g, block):
        arrived(block(partner), ag_s.at[g, 0], ag_r.at[g, 0])

    def far_finish(g, block):
        for k in range(1, ycount):
            arrived(block(yprev(k) * 2 + 1 - core), ag_s.at[g, ycount + k - 1], ag_r.at[g, ycount + k - 1])

    def heads(yk):
        return pl.ds(pl.multiple_of(yk * 2 * kvd, 2 * kvd), 2 * kvd)

    def products(keys, values, at, cs, yk):
        at_heads = heads(yk)
        return nt(keys[at, at_heads], wk[cs, at_heads]) + nt(values[at, at_heads], wv[cs, at_heads])

    def turned_products(keys, values, at, cs, yk):
        at_heads = heads(yk)
        return nt(wk[cs, at_heads], keys[at, at_heads]) + nt(wv[cs, at_heads], values[at, at_heads])

    def far_products(keys, values, at, cs):
        total = turned_products(keys, values, at, cs, ynext(1))
        for k in range(2, ycount):
            total = total + turned_products(keys, values, at, cs, ynext(k))
        return jnp.transpose(total)

    step = 256
    big = min(1024, width)
    every = pl.ds(0, tokens)
    image_rows = pl.ds(0, img_rows)

    far_start(1, gka_block)
    far_start(2, gva_block)
    near_start(1, gk_block)
    near_start(2, gv_block)

    def chunk(x, m):
        k_part = jnp.dot(x[...], wk[:, col(m)], preferred_element_type=F32)
        v_part = jnp.dot(x[...], wv[:, col(m)], preferred_element_type=F32)
        return k_part, v_part

    def stage_send(x, n, psend, l1):
        for k in range(ycount):
            yk = ynext(k)
            k_part, v_part = chunk(x, yk * 2 + 1 - core)
            shape = psend.shape[1:-1] + (kvd,)
            psend[yk, ..., :kvd] = k_part.astype(BF16).reshape(shape)
            psend[yk, ..., kvd:] = v_part.astype(BF16).reshape(shape)
            start(psend.at[yk], l1.at[yk], rs_s.at[n, 0], rs_r.at[n, k], (me_d, partner))

    def stage_own(x, own):
        for k in range(ycount):
            yk = ynext(k)
            k_part, v_part = chunk(x, yk * 2 + core)
            shape = own.shape[1:-1] + (kvd,)
            own[yk, ..., :kvd] = k_part.reshape(shape)
            own[yk, ..., kvd:] = v_part.reshape(shape)

    def level_two(n, own, l1, s2, l2):
        for k in range(ycount - 1, 0, -1):
            yk = ynext(k)
            arrived(l1.at[yk], rs_s.at[n, 0], rs_r.at[n, k])
            s2[k] = (own[yk] + l1[yk].astype(F32)).astype(BF16)

    def level_go(n, s2, l2):
        for k in range(ycount - 1, 0, -1):
            for h in range(2):
                at = pl.ds(h * kvd, kvd)
                start(
                    s2.at[k, :, at], l2.at[k, :, at], rs_s.at[n, k], rs1_r.at[k - 1, h],
                    (me_d, ynext(k) * 2 + core),
                )

    def text_piece(p, k):
        at = pl.ds(p * piece_rows, piece_rows)
        return remote(
            t_s2.at[k, at], t_l2.at[k, at], rs_s.at[0, k], t2_r.at[k - 1, p], (me_d, ynext(k) * 2 + core)
        )

    def text_go(p):
        for k in range(ycount - 1, 0, -1):
            text_piece(p, k).start()

    def stats_send(n, st, sr):
        for k in range(1, mp):
            start(st, sr.at[k], st_s.at[n], st_r.at[n], (me_d, lax.rem(me + k, mp)))

    def stats_total(n, st, sr):
        total = st[...]
        arrived(sr.at[pl.ds(1, mp - 1)], st_s.at[n], st_r.at[n])
        for k in range(1, mp):
            total = total + sr[k]
        return to_columns(total)

    def wide(p):
        return jnp.concatenate([p] * (step // 128), axis=1)

    def fold(p):
        total = p[:, :128]
        for n in range(1, p.shape[1] // 128):
            total = total + p[:, n * 128:(n + 1) * 128]
        return total

    loads[3].wait()
    for p in range(slots):
        tf = text[slot_at[p]].astype(F32)
        sc_t[p] = fold(tf * tf)
        xt[p * PATCH:(p + 1) * PATCH, :] = (tf * gain[...]).astype(BF16)
    loads[4].wait()
    loads[5].wait()
    stage_send(xt, 0, t_send, t_l1)
    stage_own(xt, t_own)
    for k in range(ycount - 1, 0, -1):
        yk = ynext(k)
        arrived(t_l1.at[yk], rs_s.at[0, 0], rs_r.at[0, k])
        t_s2[k] = (t_own[yk, 0] + t_l1[yk, 0].astype(F32)).astype(BF16)
        rest = t_own[yk, 1] + t_l1[yk, 1].astype(F32)
        tb_send[:, k - 1] = rest.reshape(dp, rb, 2 * kvd).astype(BF16)
    tb_recv[me_d] = tb_send[me_d]
    near_finish(1, gk_block)
    near_finish(2, gv_block)

    def text_near(j, _):
        cs = pl.ds(pl.multiple_of(j * step, step), step)
        dt[:, :, cs] = products(gk, gv, every, cs, y).reshape(slots, PATCH, step)
        return 0

    lax.fori_loop(0, width // step // 2, text_near, 0)
    lax.fori_loop(width // step // 2, width // step, text_near, 0)
    co_t[...] = jnp.zeros(co_t.shape, F32)
    def survey(d, found):
        count = jnp.int32(0)
        for i in range(dp):
            count = count + jnp.where(lax.div(slot_ref[i], jnp.int32(slots)) == d, jnp.int32(1), jnp.int32(0))
        return jnp.where(count == 0, d, found[0]), jnp.where(count > 1, d, found[1])

    lone, crowded = lax.fori_loop(0, dp, survey, (jnp.int32(0), jnp.int32(0)))
    lone_slot = lone * slots + 1
    at_lone = keeps[1]

    @pl.loop(0, dp)
    def _(d):
        source = owner_of(d * slots + 1)
        source = jnp.where(is_filled(d * slots) == 1, owner_of(d * slots), source)
        sources[d] = jnp.where(d == lone, jnp.int32(dp), source)

    gather_relay(0, vis_block)
    loads[7].wait()
    loads[8].wait()

    for which, dst in ((0, r1k), (1, r1v)):
        arrived(dst.at[pl.ds(0, (dp - 1) * slots)], a1_s.at[which], a1_r.at[which])

    @pl.loop(0, dp)
    def _(i):
        s2k[i] = r1k[slot_ref[i]]
        s2v[i] = r1v[slot_ref[i]]

    r2k[me_d] = s2k[me_d]
    r2v[me_d] = s2v[me_d]

    def a2(k, which):
        src, dst = ((s2k, r2k), (s2v, r2v))[which]
        return remote(
            src.at[dnext(k)], dst.at[me_d], a2_s.at[which], a2_r.at[which], (dnext(k), me)
        )

    @pl.loop(1, dp)
    def _(k):
        a2(k, 0).start()
        a2(k, 1).start()

    kb_send[0] = r1k[lone_slot]
    kb_send[1] = r1v[lone_slot]
    for k in range(1, ycount):
        send(kb_send, kb_y.at[k - 1], kby_s.at[k - 1], kby_r.at[k - 1], (me_d, ynext(k) * 2 + core))
    text_go(0)
    gather_finish(0, vis_block)
    loads[6].wait()

    sc_i[...] = jnp.zeros(sc_i.shape, F32)

    def project(j, _):
        cs = pl.ds(pl.multiple_of(j * step, step), step)
        e = jnp.concatenate([vis_all[m] for m in range(mp)], axis=0)
        e = jnp.dot(e, wp[:, cs], preferred_element_type=F32).astype(BF16)
        emb[:, cs] = e
        ef = e.astype(F32)
        xi[:, cs] = (ef * gain[:, cs]).astype(BF16)
        sc_i[...] += fold(ef * ef)
        return 0

    lax.fori_loop(0, width // step, project, 0)
    for k in range(1, ycount):
        arrived(kb_y.at[k - 1], kby_s.at[k - 1], kby_r.at[k - 1])
    kbr[me_d] = kb_y[...]

    def kbz(k):
        return remote(kb_y, kbr.at[me_d], kbz_s.at[0], kbz_r.at[0], (dnext(k), me))

    def tbz(k):
        return remote(tb_send.at[dnext(k)], tb_recv.at[me_d], tbz_s.at[0], tbz_r.at[0], (dnext(k), me))

    @pl.loop(1, dp)
    def _(k):
        kbz(k).start()

    @pl.loop(1, dp)
    def _(k):
        tbz(k).start()

    gather_relay(1, gka_block)
    gather_relay(2, gva_block)
    zero = jnp.zeros((img_rows, 1), F32)
    st_q[...] = to_rows(jnp.sum(sc_i[...], axis=1, keepdims=True), zero)
    stats_send(2, st_q, sr_q)

    for which, dst in ((0, r2k), (1, r2v)):
        arrived(dst.at[others], a2_s.at[which], a2_r.at[which])

    own_k = r2k[...].astype(F32).reshape(PATCH, kvd)
    own_v = r2v[...].astype(F32).reshape(PATCH, kvd)
    gik[:, col(me)] = own_k.astype(BF16)
    giv[:, col(me)] = own_v.astype(BF16)
    gather_start(3, gik_block)
    gather_start(4, giv_block)
    stage_send(xi, 1, i_send, i_l1)
    stage_own(xi, i_own)
    level_two(1, i_own, i_l1, i_s2, i_l2)
    level_go(1, i_s2, i_l2)
    far_finish(1, gka_block)
    far_finish(2, gva_block)

    def text_far(p):
        rows_p = pl.ds(p * PATCH, PATCH)

        def body(j, _):
            cs = pl.ds(pl.multiple_of(j * big, big), big)
            d = (dt[p, :, cs] + far_products(gk, gv, rows_p, cs)) * gain[:, cs]
            dt[p, :, cs] = d
            co_t[p] += fold(d * text[slot_at[p], :, cs].astype(F32))
            return 0

        lax.fori_loop(0, width // big, body, 0)

    text_far(0)
    near_finish(3, gik_block)
    near_finish(4, giv_block)

    def image_near(j, _):
        cs = pl.ds(pl.multiple_of(j * big, big), big)
        dg[:, cs] = jnp.transpose(turned_products(gik, giv, image_rows, cs, y))
        return 0

    lax.fori_loop(0, width // big, image_near, 0)
    gather_relay(3, gik_block)
    gather_relay(4, giv_block)
    co_i[...] = jnp.zeros(co_i.shape, F32)

    arrived(kbr.at[others], kbz_s.at[0], kbz_r.at[0])

    for k in range(1, ycount):
        m = yprev(k) * 2 + core
        for which, g in ((0, gk), (1, gv)):
            g[later_rows, col(m)] = kbr[:, k - 1, which].astype(F32).reshape(PATCH, kvd).astype(BF16)
            send(
                g.at[later_rows, col(m)], g.at[later_rows, col(m)], kbp_s.at[which, k - 1], kbp_r.at[which, k - 1],
                (me_d, partner),
            )
    far_finish(3, gik_block)
    far_finish(4, giv_block)

    def image_far(j, _):
        cs = pl.ds(pl.multiple_of(j * big, big), big)
        d = (dg[:, cs] + far_products(gik, giv, image_rows, cs)) * gain[:, cs]
        dg[:, cs] = d
        co_i[...] += fold(d * emb[:, cs].astype(F32))
        return 0

    lax.fori_loop(0, width // big, image_far, 0)
    st_i[...] = to_rows(zero, jnp.sum(co_i[...], axis=1, keepdims=True))
    stats_send(1, st_i, sr_i)
    text_go(1)
    sq_i, _ = stats_total(2, st_q, sr_q)
    scale_i = lax.rsqrt(sq_i / d_model + 1e-05)
    sc_i[...] = jnp.broadcast_to(scale_i, sc_i.shape)

    def b1(k, h):
        return remote(kvb.at[h, dnext(k)], r3.at[me_d, h], b1_s.at[h], b1_r.at[h], (dnext(k), me))

    def image_sums(h):
        at = pl.ds(h * kvd, kvd)
        total = i_own[y, :, at] + i_l1[y, :, at].astype(F32)
        for k in range(1, ycount):
            arrived(i_l2.at[k, :, at], rs_s.at[1, k], rs1_r.at[k - 1, h])
            total = total + i_l2[k, :, at].astype(F32)
        kvb[h] = (total * sc_i[:, 0:1]).reshape(dp, rb, kvd).astype(BF16)
        r3[me_d, h] = kvb[h, me_d]

        @pl.loop(1, dp)
        def _(k):
            b1(k, h).start()

    arrived(i_l1.at[y], rs_s.at[1, 0], rs_r.at[1, 0])
    image_sums(0)
    for k in range(1, ycount):
        for which, g in ((0, gk), (1, gv)):
            arrived(g.at[later_rows, col(yprev(k) * 2 + 1 - core)], kbp_s.at[which, k - 1], kbp_r.at[which, k - 1])
    text_far(1)
    image_sums(1)
    st_t[...] = to_rows(
        jnp.sum(sc_t[...].reshape(tokens, 128), axis=1, keepdims=True),
        jnp.sum(co_t[...].reshape(tokens, 128), axis=1, keepdims=True),
    )
    stats_send(0, st_t, sr_t)

    arrived(tb_recv.at[others], tbz_s.at[0], tbz_r.at[0])

    tb_sel[...] = tb_recv[lone]
    for k in range(1, ycount):
        send(tb_sel.at[k - 1], tb_y.at[k - 1], tby_s.at[k - 1], tby_r.at[k - 1], (me_d, ynext(k) * 2 + core))
    _, inner_i = stats_total(1, st_i, sr_i)
    scale_i = sc_i[:, 0:1]
    co_i[...] = jnp.broadcast_to(scale_i * scale_i * scale_i * (inner_i / d_model), co_i.shape)

    def image_end(j, _):
        cs = pl.ds(pl.multiple_of(j * step, step), step)
        d = wide(sc_i[...]) * dg[:, cs] - emb[:, cs].astype(F32) * wide(co_i[...])
        dimg[:, cs] = d.astype(BF16)
        return 0

    lax.fori_loop(0, width // step, image_end, 0)
    cuts = vis_cuts(dv)
    pieces = len(cuts) - 1

    def vis_chunk(j):
        at = pl.ds(cuts[j], cuts[j + 1] - cuts[j])
        d = nt(dimg[...], wp[at, :]).reshape(ycount, 2, rows, cuts[j + 1] - cuts[j])
        for yi in range(ycount):
            a, b = d[yi, 0], d[yi, 1]
            first = core == 0
            d_own[yi, :, at] = jnp.where(first, a, b)
            d_send[yi, :, at] = jnp.where(first, b, a).astype(BF16)
        start(d_send.at[:, :, at], d_l1.at[:, :, at], dv_s.at[0], dv_r.at[j, 0], (me_d, partner))

    def vis_two(j):
        at = pl.ds(cuts[j], cuts[j + 1] - cuts[j])
        arrived(d_l1.at[:, :, at], dv_s.at[0], dv_r.at[j, 0])
        for k in range(1, ycount):
            yk = ynext(k)
            d_s2[k, :, at] = (d_own[yk, :, at] + d_l1[yk, :, at].astype(F32)).astype(BF16)
            start(d_s2.at[k, :, at], d_l2.at[k, :, at], dv_s.at[k], dv_r.at[j, k], (me_d, yk * 2 + core))

    def b2(k):
        return remote(s4.at[dnext(k)], r4.at[0, my_inner, my_outer], b2_s.at[0], b2_r.at[0], (dnext(k), me))

    def b3(k):
        target = lax.rem(my_outer + k, outer) * inner + my_inner
        return remote(s5, r4.at[1, my_inner, my_outer], b3_s.at[0], b3_r.at[k], (target, me))

    def b4(k):
        block = r4.at[1, my_inner, lax.rem(my_outer + outer - k, outer)]
        return remote(block, block, b3_s.at[1], b3_r.at[0], (my_outer * inner + 1 - my_inner, me))

    for j in range(pieces):
        vis_chunk(j)
        if j > 0:
            vis_two(j - 1)
        if j == min(4, pieces - 1):

            for h in range(2):
                arrived(r3.at[others, h], b1_s.at[h], b1_r.at[h])

            extra = jnp.zeros((rb, 2 * kvd), F32)
            for k in range(1, ycount):
                arrived(tb_y.at[k - 1], tby_s.at[k - 1], tby_r.at[k - 1])
                extra = extra + tb_y[k - 1].astype(F32)
            r3[dp, 0] = extra[:, :kvd].astype(BF16)
            r3[dp, 1] = extra[:, kvd:].astype(BF16)

            @pl.loop(0, dp)
            def _(d):
                source = sources[d]
                s4[d, :, :kvd] = r3[source, 0]
                s4[d, :, kvd:] = r3[source, 1]

            source = owner_of(crowded * slots + 1)
            s5[:, :kvd] = r3[source, 0]
            s5[:, kvd:] = r3[source, 1]
            r4[0, my_inner, my_outer] = s4[me_d]
            r4[1, my_inner, my_outer] = s5[...]

            for k in range(1, outer):
                b3(k).start()

            @pl.loop(1, dp)
            def _(k):
                b2(k).start()

            start(s5, r4.at[1, my_inner, my_outer], b3_s.at[1], b3_r.at[0], (my_outer * inner + 1 - my_inner, me))

    vis_two(pieces - 1)
    for k in range(1, outer):
        arrived(r4.at[1, my_inner, lax.rem(my_outer + outer - k, outer)], b3_s.at[0], b3_r.at[k])
        b4(k).start()
    sq_t, inner_t = stats_total(0, st_t, sr_t)
    keep = jnp.concatenate([jnp.full((PATCH, 1), 1.0, F32) * keeps[p] for p in range(slots)], axis=0)
    scale_t = lax.rsqrt(sq_t / d_model + 1e-05)
    sc_t[...] = jnp.broadcast_to(scale_t * keep, (tokens, 128)).reshape(sc_t.shape)
    co_t[...] = jnp.broadcast_to(
        scale_t * scale_t * scale_t * (inner_t / d_model) * keep, (tokens, 128)
    ).reshape(co_t.shape)

    def text_back(j, _):
        cs = pl.ds(pl.multiple_of(j * step, step), step)
        for s in range(slots):
            at = place_of[s]
            d = wide(sc_t[at]) * dt[at, :, cs] - text[s, :, cs].astype(F32) * wide(co_t[at])
            tg[s * PATCH:(s + 1) * PATCH, cs] = d.astype(BF16)
        return 0

    lax.fori_loop(0, width // step, text_back, 0)
    arrived(t_l1.at[y], rs_s.at[0, 0], rs_r.at[0, 0])
    for p in range(t_pieces):
        for k in range(1, ycount):
            text_piece(p, k).wait_recv()
    direct = t_l2[1].astype(F32)
    for k in range(2, ycount):
        direct = direct + t_l2[k].astype(F32)
    for s in range(slots):
        at = place_of[s]
        total = t_own[y, at] + t_l1[y, at].astype(F32) + direct * (1.0 - at.astype(F32))
        dt[s, :, :2 * kvd] = total * sc_t[at][:, 0:1]
    vf = vis[...].astype(F32)
    vscale = lax.rsqrt(jnp.mean(vf * vf, axis=1, keepdims=True) + 1e-06)
    row_gain = gain_row(vgain)
    lanes = jnp.zeros((rows, 128), F32)
    for j in range(pieces):
        at = pl.ds(cuts[j], cuts[j + 1] - cuts[j])
        d = d_own[y, :, at] + d_l1[y, :, at].astype(F32)
        for k in range(1, ycount):
            arrived(d_l2.at[k, :, at], dv_s.at[k], dv_r.at[j, k])
            d = d + d_l2[k, :, at].astype(F32)
        h = d.astype(BF16).astype(F32) * row_gain[:, cuts[j]:cuts[j + 1]]
        d_own[y, :, at] = h
        lanes = lanes + fold(h * vis[:, at].astype(F32))
    v_inner = jnp.sum(lanes, axis=1, keepdims=True) / dv
    vg_out[...] = (vscale * d_own[y] - vf * (vscale * vscale * vscale * v_inner)).astype(BF16)

    arrived(s4.at[others], b2_s.at[0], b2_r.at[0])
    arrived(r4.at[1, 1 - my_inner], b3_s.at[1], b3_r.at[0])

    for s in range(slots):
        which = s * first_holds * second_holds
        placed = jnp.concatenate([r4[which, r % inner, r // inner] for r in range(dp)], axis=0).astype(F32)
        share = sc_t[place_of[s]][:, 0:1] * (place_of[s].astype(F32) * at_lone) + filled[s]
        out = dt[s, :, :2 * kvd] + placed * share
        rows_s = pl.ds(s * PATCH, PATCH)
        k_out[rows_s, :] = out[:, :kvd].astype(BF16)
        v_out[rows_s, :] = out[:, kvd:].astype(BF16)
    for copy in sends:
        copy.wait_send()

    def sent(block, sem):
        remote(block, block, sem, ag_r.at[0, 0], (me_d, partner)).wait_send()

    for which, (first, second) in enumerate(((kg4, s2k), (vg4, s2v))):
        sent(first.at[:, others], a1_s.at[which])
        sent(second.at[others], a2_s.at[which])
    for h in range(2):
        sent(kvb.at[h, others], b1_s.at[h])
    sent(s4.at[others], b2_s.at[0])
    sent(r4.at[1, my_inner, pl.ds(0, outer - 1)], b3_s.at[0])
    sent(r4.at[1, my_inner], b3_s.at[1])
    sent(kbr.at[others], kbz_s.at[0])
    sent(tb_send.at[others], tbz_s.at[0])
    sent(t_send, rs_s.at[0, 0])
    sent(i_send, rs_s.at[1, 0])
    sent(d_send, dv_s.at[0])
    for k in range(1, ycount):
        sent(t_s2.at[k], rs_s.at[0, k])
        sent(i_s2.at[k], rs_s.at[1, k])
        sent(d_s2.at[k], dv_s.at[k])
    for n, sr in enumerate((sr_t, sr_i, sr_q)):
        sent(sr.at[pl.ds(0, mp - 1)], st_s.at[n])


def shards(vision, vision_gain, image_slot, text_embed, w_proj, llm_gain, w_key, w_value, key_grad, value_grad):
    dp = lax.axis_size("dp")
    mp = lax.axis_size("mp")
    tokens, width = text_embed.shape
    slots = tokens // PATCH
    rows, dv = vision.shape
    kvd = key_grad.shape[1]
    kv = kvd * mp
    img = rows * mp
    rb = PATCH // dp
    ys = mp // 2
    pieces = len(vis_cuts(dv)) - 1
    V = pltpu.VMEM
    any_spec = pl.BlockSpec(memory_space=pl.ANY)
    vmem = pl.BlockSpec(memory_space=pltpu.VMEM)
    smem = pl.BlockSpec(memory_space=pltpu.SMEM)
    scratch = [
        V((rows, dv), BF16), V((mp, rows, dv), BF16), V((slots, PATCH, width), BF16), V((dv, width), BF16),
        V((width, kv), BF16), V((width, kv), BF16), V((tokens, width), BF16),
        V((tokens, kv), BF16), V((tokens, kv), BF16), V((img, kv), BF16), V((img, kv), BF16),
        V((img, width), BF16), V((img, width), BF16), V((img, width), BF16), V((img, width), F32),
    ]
    t_shape = (ys, slots, PATCH, 2 * kvd)
    i_shape = (ys, img, 2 * kvd)
    half = (ys, PATCH, 2 * kvd)
    scratch += [V(t_shape, BF16), V(t_shape, F32), V(t_shape, BF16), V(half, BF16), V(half, BF16)]
    scratch += [V(i_shape, BF16), V(i_shape, F32), V(i_shape, BF16), V(i_shape, BF16), V(i_shape, BF16)]
    scratch += [
        V((ys, rows, dv), BF16), V((ys, rows, dv), F32), V((ys, rows, dv), BF16), V((ys, rows, dv), BF16),
        V((ys, rows, dv), BF16),
        V((8, tokens), F32), V((mp, 8, tokens), F32), V((8, img), F32), V((mp, 8, img), F32),
        V((8, img), F32), V((mp, 8, img), F32),
        V((slots, PATCH, 128), F32), V((slots, PATCH, 128), F32), V((img, 128), F32), V((img, 128), F32),
        V((slots, PATCH, kvd), BF16), V((slots, PATCH, kvd), BF16),
        V((2, rb, kvd), BF16), V((ys - 1, 2, rb, kvd), BF16), V((dp, ys - 1, 2, rb, kvd), BF16),
        V((dp, ys - 1, rb, 2 * kvd), BF16), V((dp, ys - 1, rb, 2 * kvd), BF16),
        V((ys - 1, rb, 2 * kvd), BF16), V((ys - 1, rb, 2 * kvd), BF16),
        V((dp * slots, rb, kvd), BF16), V((dp * slots, rb, kvd), BF16),
        V((dp, rb, kvd), BF16), V((dp, rb, kvd), BF16), V((dp, rb, kvd), BF16), V((dp, rb, kvd), BF16),
        V((2, dp, rb, kvd), BF16), V((dp + 1, 2, rb, kvd), BF16),
        V((dp, rb, 2 * kvd), BF16), V((rb, 2 * kvd), BF16), V((2, 2, dp // 2, rb, 2 * kvd), BF16), pltpu.SMEM((dp,), jnp.int32),
        DMA((9,)), DMA((5, 2 * ys - 1)), DMA((5, 2 * ys - 1)), DMA((2, ys)), DMA((2, ys)), DMA((ys - 1, 2)),
        DMA((ys - 1, 2)), DMA((3,)), DMA((3,)), DMA((ys,)), DMA((pieces, ys)),
        DMA((2,)), DMA((2,)), DMA((2,)), DMA((2,)),
        DMA((2,)), DMA((2,)), DMA((1,)), DMA((1,)), DMA((2,)), DMA((dp // 2,)),
        DMA((ys - 1,)), DMA((ys - 1,)), DMA((1,)), DMA((1,)), DMA((2, ys - 1)), DMA((2, ys - 1)),
        DMA((1,)), DMA((1,)), DMA((ys - 1,)), DMA((ys - 1,)), V((slots, PATCH, width), F32),
    ]
    shapes = ((tokens, kvd), (tokens, kvd), (tokens, width), (rows, dv))
    room = sum(2 * a * b for a, b in shapes)
    lanes = 128 if dv % 128 == 0 else dv
    results = pl.pallas_call(
        functools.partial(kernel, dp, mp),
        out_shape=tuple(V(shape, BF16) for shape in shapes),
        in_specs=[smem, any_spec, vmem, any_spec, any_spec, vmem] + [any_spec] * 6,
        out_specs=(vmem,) * len(shapes),
        scratch_shapes=scratch,
        compiler_params=pltpu.CompilerParams(
            collective_id=0, has_side_effects=True, vmem_limit_bytes=67043328 - room
        ),
    )(
        image_slot, vision, vision_gain.reshape(-1, lanes), text_embed.reshape(slots, PATCH, width), w_proj,
        llm_gain[None, :], w_key, w_value, key_grad.reshape(slots, PATCH, kvd), value_grad.reshape(slots, PATCH, kvd),
        key_grad.reshape(slots, dp, rb, kvd), value_grad.reshape(slots, dp, rb, kvd),
    )
    return pl.pallas_call(
        write_out,
        out_shape=tuple(jax.ShapeDtypeStruct(shape, BF16) for shape in shapes),
        in_specs=[vmem] * len(shapes),
        out_specs=(any_spec,) * len(shapes),
        scratch_shapes=[DMA((len(shapes),))],
        compiler_params=pltpu.CompilerParams(vmem_limit_bytes=1 << 20),
    )(*results)


def solution(mesh):
    placed = (
        P(("dp", "mp"), None),
        P(),
        P(),
        P("dp", "mp"),
        P(None, "mp"),
        P("mp"),
        P("mp", None),
        P("mp", None),
        P("dp", "mp"),
        P("dp", "mp"),
    )
    return jax.shard_map(
        shards,
        mesh=mesh,
        in_specs=placed,
        out_specs=(P("dp", "mp"), P("dp", "mp"), P("dp", "mp"), P(("dp", "mp"), None)),
        check_vma=False,
    )
```
